128 devices in a mesh: row: 8 (over y, core), col: 16 (over x, z).
Axes of the slice: x: 4, y: 4, z: 4, core: 2. Of those that a mesh axis runs over, the one named last changes fastest.
Arguments:
- points: float32 [3, 4, 16384], P(None, None, ('row', 'col')), may hold values from 0 to 1
- weights: float32 [4, 16384], P(None, ('row', 'col')), may hold values from 0.05 to 0.2
- shift: float32 [16384], P(('row', 'col')), may hold values from 0.5 to 4
- cluster_rank: int32 [32], replicated, may hold values from 0 to 31, each once
Outputs:
- factor: float32 [4, 8, 512, 2, 16, 512], P(None, 'row', None, None, 'col')
The draws below stay inside these ranges and needn't reach their ends.
Inputs may be any that keep to these rules, and one draw needn't show every extreme that they name: `cluster_rank`: every cluster has a distinct elimination position.
All inputs are finite; a program needn't handle non-finite values.
Results may differ from the reference program's by a relative error of at most 0.0003.
Values sent between devices are 32-bit elements; how exact they have to be, the bound alone decides.
No kernel may reach another device: no remote copies, remote signals or barrier semaphores. Data moves between devices by JAX's collectives and lax.ppermute only.
A program may use at most 128 MiB of HBM per device.

```python
import math
import jax
import jax.numpy as jnp
from jax import lax

TILE = 512
QUAD = 4
RB = 4
GRID_ROWS = 8
GRID_COLS = 16
NT = 32
CB = 2
W = 16384


def level_of(rng, extent, pieces, smallest, top_value):
    gain, own = 1.0, jax.random.fold_in(rng, 6)
    for dim, blocks in pieces:
        heights = jnp.exp(jax.random.uniform(jax.random.fold_in(own, dim), (blocks,), jnp.float32, smallest / len(pieces), top_value / len(pieces)))
        gain = gain * jnp.repeat(heights, extent[dim] // blocks).reshape([-1 if axis == dim else 1 for axis in range(len(extent))])
    return gain


def setup_inputs(seed: int = 0) -> dict:
    splits = jax.random.split(jax.random.key(seed), 5)
    return {
        "points": jnp.clip(1.0 * jax.random.uniform(splits[0], (3, QUAD, W), jnp.float32) ** level_of(splits[0], (3, QUAD, W), ((2, 128),), -0.2, 0.2), 0.0, 1.0),
        "weights": jnp.clip(jnp.exp(math.log(0.2) - 1.3862944 * jax.random.uniform(splits[1], (QUAD, W), jnp.float32) ** level_of(splits[1], (QUAD, W), ((1, 128),), -0.2, 0.2)), 0.05, 0.2),
        "shift": jnp.clip(jnp.exp(math.log(4.0) - 2.0794415 * jax.random.uniform(splits[2], (W,), jnp.float32) ** level_of(splits[2], (W,), ((0, 128),), -0.2, 0.2)), 0.5, 4.0),
        "cluster_rank": jax.random.permutation(splits[3], NT).astype(jnp.int32),
    }


SOFTENING_SQUARED = 0.0004

def kernel_block(row_geometry, col_geometry):
    values = jnp.zeros((row_geometry.shape[2], col_geometry.shape[2]), jnp.float32)
    for first in range(row_geometry.shape[1]):
        for second in range(col_geometry.shape[1]):
            squared = SOFTENING_SQUARED
            for coordinate in range(3):
                offset = row_geometry[coordinate, first][:, None] - col_geometry[coordinate, second][None, :]
                squared = squared + offset * offset
            product = row_geometry[3, first][:, None] * col_geometry[3, second][None, :]
            values = values + product * lax.rsqrt(squared)
    return values

def reorder(points, weights, shift, cluster_rank):
    clusters = cluster_rank.shape[0]
    positions = jnp.arange(clusters, dtype=jnp.int32)
    order = lax.optimization_barrier(jnp.sum(jnp.where(cluster_rank[None, :] == positions[:, None], positions[None, :], 0), axis=1)).astype(jnp.int32)
    geometry = jnp.concatenate([points, weights[None]], axis=0)
    quadrature = geometry.shape[1]
    geometry = geometry.reshape(4, quadrature, clusters, -1)
    geometry = jnp.take(geometry, order, axis=2).reshape(4, quadrature, -1)
    shifted = jnp.take(shift.reshape(clusters, -1), order, axis=0).reshape(-1)
    return (geometry, shifted)

def reference(points, weights, shift, cluster_rank):
    geometry, shifted = reorder(points, weights, shift, cluster_rank)

    def row_block(start):
        rows = lax.dynamic_slice_in_dim(geometry, start, TILE, 2)
        return kernel_block(rows, geometry)
    starts = (jnp.arange(NT, dtype=jnp.int32) * TILE).astype(jnp.int32)
    matrix = lax.map(row_block, starts).reshape(W, W)
    diagonal_index = jnp.arange(W, dtype=jnp.int32)
    matrix = matrix.at[diagonal_index, diagonal_index].add(shifted)
    for step in range(2):
        begin = step * TILE
        end = begin + TILE
        diagonal_factor = jnp.linalg.cholesky(matrix[begin:end, begin:end])
        panel = lax.linalg.triangular_solve(diagonal_factor, matrix[end:, begin:end], left_side=False, lower=True, transpose_a=True)
        update = jnp.dot(panel, panel.T, precision=lax.Precision.HIGHEST)
        matrix = matrix.at[end:, end:].add(-update)
        matrix = matrix.at[begin:end, begin:end].set(diagonal_factor)
        matrix = matrix.at[end:, begin:end].set(panel)
    tiles = matrix.reshape(NT, TILE, NT, TILE)
    tile_index = jnp.arange(NT, dtype=jnp.int32)
    keep = tile_index[:, None] >= tile_index[None, :]
    tiles = jnp.where(keep[:, None, :, None], tiles, 0.0)
    return tiles.reshape(RB, GRID_ROWS, TILE, CB, GRID_COLS, TILE)
```

```python
import functools

import jax
import jax.numpy as jnp
from jax import lax
from jax.experimental import pallas as pl
from jax.experimental.pallas import tpu as pltpu
from jax.sharding import PartitionSpec as P

SOFTENING_SQUARED = 0.0004
F32 = jnp.float32
BF16 = jnp.bfloat16
QUAD = 4
TILE = 512
FEAT = 48
LEAD = 1024
BASE = 128
STEP = 16
WINDOW = LEAD + BASE
HIGHEST = lax.Precision.HIGHEST


def split(value):
    high = value.astype(BF16)
    return high, (value - high.astype(F32)).astype(BF16)


def dot3(a_high, a_low, b_high, b_low):
    dot = functools.partial(jnp.dot, preferred_element_type=F32)
    return dot(a_high, b_high) + (dot(a_high, b_low) + dot(a_low, b_high))


def gather_shards(shard):
    rows, cols = lax.axis_size("row"), lax.axis_size("col")
    ys, xs = rows // 2, 4
    zs = cols // xs

    def send(value, move):
        pairs = []
        for source in range(rows * cols):
            row, col = divmod(source, cols)
            y, core, x, z = move(row // 2, row % 2, col // zs, col % zs)
            pairs.append((source, ((y % ys) * 2 + core % 2) * cols + (x % xs) * zs + z % zs))
        return lax.ppermute(value, ("row", "col"), pairs)

    held = shard[None]
    moves = [lambda y, c, x, z, k=k: (y, c, x, z + k) for k in range(1, zs)]
    held = jnp.concatenate([held] + [send(held, move) for move in moves], 0)
    moves = [lambda y, c, x, z, k=k: (y, c, x + k, z) for k in range(1, xs)]
    held = jnp.concatenate([held] + [send(held, move) for move in moves], 0)
    held = jnp.concatenate([held, send(held, lambda y, c, x, z: (y, c + 1, x, z))], 0)
    moves = [lambda y, c, x, z, k=k: (y + k, c, x, z) for k in range(1, ys)]
    return jnp.concatenate([held] + [send(held, move) for move in moves], 0)


def prep_kernel(where_ref, g0, g1, g2, g3, u_ref, v_ref, wr_ref, wc_ref, pad):
    geometry = jnp.concatenate([g0[...], g1[...], g2[...], g3[...]], axis=1)
    centred = geometry[0:12] - 0.5
    coarse = jnp.floor(centred * 256.0 + 0.5) * (1.0 / 256.0)
    fine = centred - coarse
    fine_high = fine.astype(BF16).astype(F32)
    fine_low = fine - fine_high
    per = lambda value: [value[4 * c : 4 * c + 4] for c in range(3)]
    coarse, fine, fine_high, fine_low = per(coarse), per(fine), per(fine_high), per(fine_low)
    norm = sum(c * c for c in coarse)
    norm_high = jnp.floor(norm * 256.0) * (1.0 / 256.0)
    norm_low = norm - norm_high
    mixed = sum(2.0 * c * f + f * f for c, f in zip(coarse, fine))

    def pieces(value):
        first = value.astype(BF16).astype(F32)
        second = (value - first).astype(BF16).astype(F32)
        return [first, second, value - first - second]

    one = jnp.ones_like(norm)
    twice = lambda values: [-2.0 * value for value in values]
    left = twice(coarse) + [norm_high, norm_low, one, one]
    left += twice(coarse) + twice(coarse) + twice(fine_high) + twice(fine_low)
    left += twice(fine_high) + twice(fine_high) + twice(fine_low)
    left += pieces(mixed) + [one] * 3
    right = coarse + [one, one, norm_high, norm_low]
    right += fine_high + fine_low + coarse + coarse
    right += fine_high + fine_low + fine_high
    right += [one] * 3 + pieces(mixed + SOFTENING_SQUARED)
    pad[...] = jnp.zeros_like(pad)
    for quad in range(QUAD):
        for k, value in enumerate(left):
            pad[k : k + 1, :] = value[quad : quad + 1, :]
        u_ref[quad] = jnp.transpose(pad[...])[:, :FEAT].astype(BF16)
        for k, value in enumerate(right):
            pad[k : k + 1, :] = value[quad : quad + 1, :]
        v_ref[quad] = pad[0:FEAT, :].astype(BF16)
    pad[0:8, :] = geometry[12:20]
    wr_ref[...] = jnp.transpose(pad[...])
    wc_ref[...] = geometry[12:20]


def assemble(u_ref, v_ref, wr_ref, wc_ref, left, right, start, count):
    rows = pl.ds(start, count)
    total = None
    for first in range(QUAD):
        part = None
        for second in range(QUAD):
            squared = jnp.dot(u_ref[left, first, rows, :], v_ref[right, second], preferred_element_type=F32)
            term = lax.rsqrt(squared) * wc_ref[right, second : second + 1, :]
            part = term if part is None else part + term
        part = part * wr_ref[left, rows, first : first + 1]
        total = part if total is None else total + part
    return total


def with_shift(values, wr_ref, tile, start, count):
    row = start + lax.broadcasted_iota(jnp.int32, (count, TILE), 0)
    col = lax.broadcasted_iota(jnp.int32, (count, TILE), 1)
    return values + jnp.where(row == col, wr_ref[tile, pl.ds(start, count), 4:5], 0.0)


def eliminate_base(work):
    for step in range(BASE // STEP):
        low = step * STEP
        block = work[low : low + STEP, :]
        left, right = block[:, :BASE], block[:, BASE:]
        spread = [jnp.broadcast_to(left[:, low + j : low + j + 1], (STEP, BASE)) for j in range(STEP)]
        full = lambda value, i: jnp.broadcast_to(value[i : i + 1, :], (8, BASE))
        m = [[full(spread[j], i) for j in range(i + 1)] for i in range(STEP)]
        a = [full(left, i) for i in range(STEP)]
        g = [full(right, i) for i in range(STEP)]
        for j in range(STEP):
            scale = lax.rsqrt(m[j][j])
            a[j] = a[j] * scale
            g[j] = g[j] * scale
            for i in range(j + 1, STEP):
                m[i][j] = m[i][j] * scale
            for i in range(j + 1, STEP):
                for k in range(j + 1, i + 1):
                    m[i][k] = m[i][k] - m[i][j] * m[k][j]
                a[i] = a[i] - m[i][j] * a[j]
                g[i] = g[i] - m[i][j] * g[j]
        for i in range(STEP):
            work[low + i : low + i + 1, :BASE] = a[i][0:1]
            work[low + i : low + i + 1, BASE:] = g[i][0:1]
        if low + STEP < BASE:
            done = work[low : low + STEP, :]
            rest = done[:, low + STEP : BASE]
            work[low + STEP :, :] = work[low + STEP :, :] - lax.dot_general(
                rest, done, (((0,), (0,)), ((), ())), precision=HIGHEST, preferred_element_type=F32
            )


def chain_kernel(u_ref, v_ref, wr_ref, wc_ref, ft_ref, hh_ref, hl_ref, th_ref, tl_ref, state, work):
    state[:, LEAD:] = jnp.zeros((LEAD, LEAD), F32)
    eye = (
        lax.broadcasted_iota(jnp.int32, (BASE, BASE), 0) == lax.broadcasted_iota(jnp.int32, (BASE, BASE), 1)
    ).astype(F32)
    for left, right in ((0, 0), (0, 1), (1, 1)):
        @pl.loop(0, TILE // 256)
        def _(chunk):
            start = pl.multiple_of(chunk * 256, 256)
            values = assemble(u_ref, v_ref, wr_ref, wc_ref, left, right, start, 256)
            if left == right:
                values = with_shift(values, wr_ref, left, start, 256)
            state[pl.ds(left * TILE + start, 256), right * TILE : (right + 1) * TILE] = values

    blocks = LEAD // BASE

    @pl.loop(0, blocks)
    def _(k):
        here = pl.multiple_of(k * BASE, BASE)
        rows = pl.ds(here, BASE)
        state[rows, pl.ds(pl.multiple_of(LEAD + here, BASE), BASE)] = eye
        work[:, :BASE] = state[rows, pl.ds(here, BASE)]
        work[:, BASE:] = eye
        eliminate_base(work)
        inverse = work[:, BASE:]
        window = pl.ds(here, WINDOW)
        state[rows, window] = jnp.dot(inverse, state[rows, window], precision=HIGHEST, preferred_element_type=F32)

        @pl.loop(k + 1, blocks)
        def _(i):
            below = pl.multiple_of(i * BASE, BASE)
            state[pl.ds(below, BASE), window] = state[pl.ds(below, BASE), window] - lax.dot_general(
                state[rows, pl.ds(below, BASE)],
                state[rows, window],
                (((0,), (0,)), ((), ())),
                precision=HIGHEST,
                preferred_element_type=F32,
            )

    ft_ref[...] = state[:, :LEAD]

    @pl.loop(0, blocks)
    def _(k):
        rows = pl.ds(pl.multiple_of(k * BASE, BASE), BASE)
        slab = state[rows, LEAD:]
        hh_ref[rows, :], hl_ref[rows, :] = split(slab)
        th_ref[:, rows], tl_ref[:, rows] = split(jnp.transpose(slab))


def weights_kernel(info, u_ref, v_ref, wr_ref, wc_ref, hh, hl, th, tl, yh_ref, yl_ref, ah, al, zh, zl):
    slot = pl.program_id(0)
    column = info[slot]
    panel = column < 2
    top, low = pl.ds(0, TILE), pl.ds(TILE, TILE)

    @pl.when(jnp.logical_not(panel))
    def _():
        for half in range(2):
            @pl.loop(0, TILE // 256)
            def _(chunk):
                start = pl.multiple_of(chunk * 256, 256)
                values = assemble(u_ref, v_ref, wr_ref, wc_ref, half, 6 + slot, start, 256)
                rows = pl.ds(half * TILE + start, 256)
                ah[rows, :], al[rows, :] = split(values)
        zh[top, :], zl[top, :] = split(dot3(hh[top, top], hl[top, top], ah[top, :], al[top, :]))
        zh[low, :], zl[low, :] = split(dot3(hh[low, :], hl[low, :], ah[...], al[...]))

    @pl.when(panel)
    def _():
        row = lax.broadcasted_iota(jnp.int32, (LEAD, TILE), 0)
        col = lax.broadcasted_iota(jnp.int32, (LEAD, TILE), 1)
        zh[...] = jnp.where(row == col + column * TILE, -1.0, 0.0).astype(BF16)
        zl[...] = jnp.zeros((LEAD, TILE), BF16)

    yh_ref[top, :], yl_ref[top, :] = split(dot3(th[top, :], tl[top, :], zh[...], zl[...]))
    yh_ref[low, :], yl_ref[low, :] = split(dot3(th[low, low], tl[low, low], zh[low, :], zl[low, :]))


CHUNK = 256
ZERO, UPDATE, DIAGONAL, PANEL, FACTOR = range(5)


def final_kernel(info, u_ref, v_ref, wr_ref, wc_ref, yh, yl, ft_ref, out_ref, ah, al):
    slot, chunk = pl.program_id(0), pl.program_id(1)
    start = pl.multiple_of(chunk * CHUNK, CHUNK)
    kinds = [info[2 + slot * 2], info[3 + slot * 2]]

    def store(j, values):
        for q in range(TILE // 128):
            out_ref[pl.ds(j * 4 + q, CHUNK, stride=8), :] = values[:, q * 128 : (q + 1) * 128]

    needed = lambda kind: (kind != ZERO) & (kind != FACTOR)

    @pl.when(needed(kinds[0]) | needed(kinds[1]))
    def _():
        for half in range(2):
            values = assemble(u_ref, v_ref, wr_ref, wc_ref, 2 + slot, half, start, CHUNK)
            cols = pl.ds(half * TILE, TILE)
            ah[:, cols], al[:, cols] = split(values)

    for j in range(2):
        kind = kinds[j]

        @pl.when(kind == ZERO)
        def _():
            store(j, jnp.zeros((CHUNK, TILE), F32))

        @pl.when(kind == PANEL)
        def _():
            store(j, -dot3(ah[...], al[...], yh[j], yl[j]))

        @pl.when((kind == UPDATE) | (kind == DIAGONAL))
        def _():
            values = assemble(u_ref, v_ref, wr_ref, wc_ref, 2 + slot, 6 + j, start, CHUNK)
            row = start + lax.broadcasted_iota(jnp.int32, (CHUNK, TILE), 0)
            col = lax.broadcasted_iota(jnp.int32, (CHUNK, TILE), 1)
            shift = wr_ref[2 + slot, pl.ds(start, CHUNK), 4:5]
            values = values + jnp.where((row == col) & (kind == DIAGONAL), shift, 0.0)
            store(j, values - dot3(ah[...], al[...], yh[j], yl[j]))

        if j == 0:
            @pl.when(kind == FACTOR)
            def _():
                which = info[10]
                lanes = pl.ds(pl.multiple_of(which // 2 * TILE + start, CHUNK), CHUNK)
                rows = pl.ds(pl.multiple_of(which % 2 * TILE, TILE), TILE)
                values = jnp.transpose(ft_ref[rows, lanes])
                row = start + lax.broadcasted_iota(jnp.int32, (CHUNK, TILE), 0)
                col = lax.broadcasted_iota(jnp.int32, (CHUNK, TILE), 1)
                keep = (row >= col) | (which // 2 != which % 2)
                store(j, jnp.where(keep, values, 0.0))


def whole(count):
    return [pl.BlockSpec(memory_space=pltpu.VMEM)] * count


def shards(points, weights, shift, cluster_rank):
    rows, cols = lax.axis_size("row"), lax.axis_size("col")
    row, col = lax.axis_index("row"), lax.axis_index("col")
    width = shift.shape[0]
    fill = jnp.zeros((7, width), F32)
    shard = jnp.concatenate([points.reshape(12, width), weights, shift[None], fill], 0)
    gathered = gather_shards(shard)

    slots = jnp.arange(4, dtype=jnp.int32)
    tile_rows = row + rows * slots
    tile_cols = col + cols * slots[:2]
    wanted = jnp.concatenate([slots[:2], tile_rows, tile_cols])
    clusters = jnp.arange(cluster_rank.shape[0], dtype=jnp.int32)
    found = jnp.sum(jnp.where(cluster_rank[None, :] == wanted[:, None], clusters[None, :], 0), axis=1)
    from_row, from_x = found // 4, found % 4
    dy = (row // 2 - from_row // 2) % 4
    dc = (row % 2 - from_row % 2) % 2
    dx = (col // 4 - from_x) % 4
    dz = (col % 4 - slots) % 4
    where = ((((dy * 2 + dc) * 4 + dx) * 4)[:, None] + dz[None, :]).reshape(-1).astype(jnp.int32)

    part = lambda z: pl.BlockSpec((None, 24, width), lambda t, at: (at[4 * t + z], 0, 0))
    u, v, wr, wc = pl.pallas_call(
        prep_kernel,
        grid_spec=pltpu.PrefetchScalarGridSpec(
            num_scalar_prefetch=1,
            grid=(8,),
            in_specs=[part(z) for z in range(4)],
            out_specs=[
                pl.BlockSpec((None, QUAD, TILE, FEAT), lambda t, at: (t, 0, 0, 0)),
                pl.BlockSpec((None, QUAD, FEAT, TILE), lambda t, at: (t, 0, 0, 0)),
                pl.BlockSpec((None, TILE, 128), lambda t, at: (t, 0, 0)),
                pl.BlockSpec((None, 8, TILE), lambda t, at: (t, 0, 0)),
            ],
            scratch_shapes=[pltpu.VMEM((128, TILE), F32)],
        ),
        out_shape=[
            jax.ShapeDtypeStruct((8, QUAD, TILE, FEAT), BF16),
            jax.ShapeDtypeStruct((8, QUAD, FEAT, TILE), BF16),
            jax.ShapeDtypeStruct((8, TILE, 128), F32),
            jax.ShapeDtypeStruct((8, 8, TILE), F32),
        ],
        name="prep",
    )(where, *[gathered] * 4)

    square = jax.ShapeDtypeStruct((LEAD, LEAD), BF16)
    ft, hh, hl, th, tl = pl.pallas_call(
        chain_kernel,
        in_specs=whole(4),
        out_specs=whole(5),
        out_shape=[jax.ShapeDtypeStruct((LEAD, LEAD), F32)] + [square] * 4,
        scratch_shapes=[pltpu.VMEM((LEAD, 2 * LEAD), F32), pltpu.VMEM((BASE, 2 * BASE), F32)],
        name="chain",
    )(u, v, wr, wc)

    block_rows, block_cols = tile_rows[:, None], tile_cols[None, :]
    kinds = jnp.where(
        block_rows < block_cols,
        ZERO,
        jnp.where(
            block_cols >= 2,
            jnp.where(block_rows == block_cols, DIAGONAL, UPDATE),
            jnp.where(block_rows < 2, FACTOR, PANEL),
        ),
    )
    info = jnp.concatenate([tile_cols, kinds.reshape(-1), (row * 2 + col)[None]]).astype(jnp.int32)

    half = jax.ShapeDtypeStruct((2, LEAD, TILE), BF16)
    yh, yl = pl.pallas_call(
        weights_kernel,
        grid_spec=pltpu.PrefetchScalarGridSpec(
            num_scalar_prefetch=1,
            grid=(2,),
            in_specs=whole(8),
            out_specs=[pl.BlockSpec((None, LEAD, TILE), lambda j, info: (j, 0, 0))] * 2,
            scratch_shapes=[pltpu.VMEM((LEAD, TILE), BF16)] * 4,
        ),
        out_shape=[half, half],
        name="weights",
    )(info, u, v, wr, wc, hh, hl, th, tl)

    lines = CHUNK * 8
    out = pl.pallas_call(
        final_kernel,
        grid_spec=pltpu.PrefetchScalarGridSpec(
            num_scalar_prefetch=1,
            grid=(4, TILE // CHUNK),
            in_specs=whole(7),
            out_specs=pl.BlockSpec((lines, 128), lambda i, h, info: (i * (TILE // CHUNK) + h, 0)),
            scratch_shapes=[pltpu.VMEM((CHUNK, LEAD), BF16)] * 2,
        ),
        out_shape=jax.ShapeDtypeStruct((4 * TILE * 8, 128), F32),
        name="final",
    )(info, u, v, wr, wc, yh, yl, ft)
    return out.reshape(4, 1, TILE, 2, 1, TILE)


def solution(mesh):
    return jax.shard_map(
        shards,
        mesh=mesh,
        in_specs=(P(None, None, ("row", "col")), P(None, ("row", "col")), P(("row", "col")), P()),
        out_specs=P(None, "row", None, None, "col", None),
        check_vma=False,
    )
```

```python
import functools

import jax
import jax.numpy as jnp
from jax import lax
from jax.experimental import pallas as pl
from jax.experimental.pallas import tpu as pltpu
from jax.sharding import PartitionSpec as P

SOFTENING_SQUARED = 0.0004
F32 = jnp.float32
BF16 = jnp.bfloat16
QUAD = 4
TILE = 512
FEAT = 48
LEAD = 1024
BASE = 128
STEP = 16
WINDOW = LEAD + BASE
HIGHEST = lax.Precision.HIGHEST


def split(value):
    high = value.astype(BF16)
    return high, (value - high.astype(F32)).astype(BF16)


def dot3(a_high, a_low, b_high, b_low):
    dot = functools.partial(jnp.dot, preferred_element_type=F32)
    return dot(a_high, b_high) + (dot(a_high, b_low) + dot(a_low, b_high))


def gather_shards(shard):
    rows, cols = lax.axis_size("row"), lax.axis_size("col")
    ys, xs = rows // 2, 4
    zs = cols // xs

    def send(value, move):
        pairs = []
        for source in range(rows * cols):
            row, col = divmod(source, cols)
            y, core, x, z = move(row // 2, row % 2, col // zs, col % zs)
            pairs.append((source, ((y % ys) * 2 + core % 2) * cols + (x % xs) * zs + z % zs))
        return lax.ppermute(value, ("row", "col"), pairs)

    held = shard[None]
    moves = [lambda y, c, x, z, k=k: (y, c, x, z + k) for k in range(1, zs)]
    held = jnp.concatenate([held] + [send(held, move) for move in moves], 0)
    moves = [lambda y, c, x, z, k=k: (y, c, x + k, z) for k in range(1, xs)]
    held = jnp.concatenate([held] + [send(held, move) for move in moves], 0)
    moves = [lambda y, c, x, z, k=k: (y + k, c, x, z) for k in range(1, ys)]
    held = jnp.concatenate([held] + [send(held, move) for move in moves], 0)
    return jnp.concatenate([held, send(held, lambda y, c, x, z: (y, c + 1, x, z))], 0)


def prep_kernel(where_ref, g0, g1, g2, g3, u_ref, v_ref, wr_ref, wc_ref, pad):
    geometry = jnp.concatenate([g0[...], g1[...], g2[...], g3[...]], axis=1)
    centred = geometry[0:12] - 0.5
    coarse = jnp.floor(centred * 256.0 + 0.5) * (1.0 / 256.0)
    fine = centred - coarse
    fine_high = fine.astype(BF16).astype(F32)
    fine_low = fine - fine_high
    per = lambda value: [value[4 * c : 4 * c + 4] for c in range(3)]
    coarse, fine, fine_high, fine_low = per(coarse), per(fine), per(fine_high), per(fine_low)
    norm = sum(c * c for c in coarse)
    norm_high = jnp.floor(norm * 256.0) * (1.0 / 256.0)
    norm_low = norm - norm_high
    mixed = sum(2.0 * c * f + f * f for c, f in zip(coarse, fine))

    def pieces(value):
        first = value.astype(BF16).astype(F32)
        second = (value - first).astype(BF16).astype(F32)
        return [first, second, value - first - second]

    one = jnp.ones_like(norm)
    twice = lambda values: [-2.0 * value for value in values]
    left = twice(coarse) + [norm_high, norm_low, one, one]
    left += twice(coarse) + twice(coarse) + twice(fine_high) + twice(fine_low)
    left += twice(fine_high) + twice(fine_high) + twice(fine_low)
    left += pieces(mixed) + [one] * 3
    right = coarse + [one, one, norm_high, norm_low]
    right += fine_high + fine_low + coarse + coarse
    right += fine_high + fine_low + fine_high
    right += [one] * 3 + pieces(mixed + SOFTENING_SQUARED)
    pad[...] = jnp.zeros_like(pad)
    for quad in range(QUAD):
        for k, value in enumerate(left):
            pad[k : k + 1, :] = value[quad : quad + 1, :]
        u_ref[quad] = jnp.transpose(pad[...])[:, :FEAT].astype(BF16)
        for k, value in enumerate(right):
            pad[k : k + 1, :] = value[quad : quad + 1, :]
        v_ref[quad] = pad[0:FEAT, :].astype(BF16)
    pad[0:8, :] = geometry[12:20]
    wr_ref[...] = jnp.transpose(pad[...])
    wc_ref[...] = geometry[12:20]


def assemble(u_ref, v_ref, wr_ref, wc_ref, left, right, start, count, cols=slice(0, TILE)):
    rows = pl.ds(start, count)
    total = None
    for first in range(QUAD):
        part = None
        for second in range(QUAD):
            squared = jnp.dot(u_ref[left, first, rows, :], v_ref[right, second, :, cols], preferred_element_type=F32)
            term = lax.rsqrt(squared) * wc_ref[right, second : second + 1, cols]
            part = term if part is None else part + term
        part = part * wr_ref[left, rows, first : first + 1]
        total = part if total is None else total + part
    return total


def with_shift(values, wr_ref, tile, start, count):
    row = start + lax.broadcasted_iota(jnp.int32, (count, TILE), 0)
    col = lax.broadcasted_iota(jnp.int32, (count, TILE), 1)
    return values + jnp.where(row == col, wr_ref[tile, pl.ds(start, count), 4:5], 0.0)


def split3(value):
    first = value.astype(BF16)
    rest = value - first.astype(F32)
    second = rest.astype(BF16)
    return first, second, (rest - second.astype(F32)).astype(BF16)


def dot_rows(left, right):
    return lax.dot_general(left, right, (((0,), (0,)), ((), ())), preferred_element_type=F32)


def eliminate_base(work, spread, solved, lines):
    lane = lax.broadcasted_iota(jnp.int32, (8, BASE), 1)
    sub = lax.broadcasted_iota(jnp.int32, (8, BASE), 0)
    repeat = lambda ref, i: ref[pl.ds(i, 8, stride=0), :]
    for step in range(BASE // STEP):
        low = step * STEP
        high = low + STEP
        a, c = [], [[], []]
        for half in range(2):
            left = work[low + 8 * half : low + 8 * half + 8, :]
            for j in range(STEP):
                column = jnp.broadcast_to(left[:, low + j : low + j + 1], (8, BASE))
                c[half].append(column)
            inside = (lane >= low) & (lane < high)
            a.append(jnp.where(inside, jnp.where(lane == sub + (low + 8 * half), 1.0, 0.0), left))
            lines[8 * half : 8 * half + 8, :] = a[half]
        d = []
        for half in range(2):
            diagonal = c[half][8 * half]
            for j in range(8 * half + 1, 8 * half + 8):
                diagonal = jnp.where(sub == j % 8, c[half][j], diagonal)
            d.append(diagonal)
            spread[0, 8 * half : 8 * half + 8, :] = diagonal
        pivot = repeat(spread.at[0], 0)
        for j in range(STEP):
            scale = lax.rsqrt(pivot)
            first = j // 8
            line = repeat(lines, j) * scale
            for half in range(first, 2):
                c[half][j] = c[half][j] * scale
                solved[j, 8 * half : 8 * half + 8, :] = c[half][j]
                if j + 2 < STEP:
                    d[half] = d[half] - c[half][j] * c[half][j]
                    spread[j + 1, 8 * half : 8 * half + 8, :] = d[half]
            for k in range(j + 1, STEP):
                factor = repeat(solved.at[j], k)
                if k == j + 1:
                    pivot = repeat(spread.at[j], k) - factor * factor
                for half in range(k // 8, 2):
                    c[half][k] = c[half][k] - c[half][j] * factor
            for half in range(first, 2):
                update = a[half] - c[half][j] * line
                if half == first:
                    update = jnp.where(sub > j % 8, update, jnp.where(sub == j % 8, line, a[half]))
                a[half] = update
                lines[8 * half : 8 * half + 8, :] = update
        for half in range(2):
            work[low + 8 * half : low + 8 * half + 8, :] = a[half]
        if high < BASE:
            w0, w1, w2 = split3(jnp.concatenate(a, 0))
            product = dot_rows(
                jnp.concatenate([w0, w0, w1, w0, w1, w2], 0), jnp.concatenate([w0, w1, w0, w2, w1, w0], 0)
            )
            rest = lax.broadcasted_iota(jnp.int32, (BASE - high, BASE), 1)
            kept = jnp.where((rest >= low) & (rest < high), 0.0, work[high:, :])
            work[high:, :] = kept - product[high:, :]


def chain_kernel(
    u_ref, v_ref, wr_ref, wc_ref,
    ft_ref, hh_ref, hl_ref, th_ref, tl_ref,
    state, work, spread, solved, lines, stack, tall,
):
    state[:, LEAD:] = jnp.zeros((LEAD + BASE, LEAD), F32)
    state[LEAD:, :LEAD] = jnp.zeros((BASE, LEAD), F32)
    lane = lax.broadcasted_iota(jnp.int32, (BASE, BASE), 1)
    row = lax.broadcasted_iota(jnp.int32, (BASE, BASE), 0)
    eye = (row == lane).astype(F32)
    for left, right in ((0, 0), (0, 1), (1, 1)):
        @pl.loop(0, TILE // 256)
        def _(chunk):
            start = pl.multiple_of(chunk * 256, 256)
            values = assemble(u_ref, v_ref, wr_ref, wc_ref, left, right, start, 256)
            if left == right:
                values = with_shift(values, wr_ref, left, start, 256)
            state[pl.ds(left * TILE + start, 256), right * TILE : (right + 1) * TILE] = values

    blocks = LEAD // BASE

    @pl.loop(0, blocks)
    def _(k):
        here = pl.multiple_of(k * BASE, BASE)
        rows = pl.ds(here, BASE)
        state[rows, pl.ds(pl.multiple_of(LEAD + here, BASE), BASE)] = eye
        work[...] = state[rows, pl.ds(here, BASE)]

        eliminate_base(work, spread, solved, lines)
        l0, l1, l2 = split3(jnp.where(row >= lane, work[...], 0.0))
        window = pl.ds(here, WINDOW)

        def load(values):
            first, second, third = split3(values)
            stack[0:128, :] = first
            stack[128:256, :] = second
            stack[256:384, :] = third
            stack[384:512, :] = first

        load(state[rows, window])
        both = jnp.concatenate
        two = jnp.dot(
            both([both([l0, l0], 1), both([l1, l1], 1)], 0), stack[0:256, :], preferred_element_type=F32
        )
        one = jnp.dot(both([l0, l2], 1), stack[256:512, :], preferred_element_type=F32)
        done = two[:BASE] + (two[BASE:] + one)
        state[rows, window] = done
        load(done)

        @pl.loop(0, blocks - 1 - k)
        def _(i):
            there = pl.multiple_of((i + 1) * BASE, BASE)
            first, second, third = split3(jnp.transpose(state[rows, pl.ds(pl.multiple_of(here + there, BASE), BASE)]))
            part = pl.ds(pl.multiple_of(i * BASE, BASE), BASE)
            tall[part, 0:128] = first
            tall[part, 128:256] = first
            tall[part, 256:384] = second
            tall[part, 384:512] = second
            tall[part, 512:640] = first
            tall[part, 640:768] = third

        @pl.loop(0, (blocks - k) // 2)
        def _(pair):
            part = pl.ds(pl.multiple_of(pair * 256, 256), 256)
            below = pl.ds(pl.multiple_of(here + BASE + pair * 256, BASE), 256)
            dot = functools.partial(jnp.dot, preferred_element_type=F32)
            update = dot(tall[part, 0:256], stack[0:256, :])
            update += dot(tall[part, 256:512], stack[0:256, :])
            update += dot(tall[part, 512:768], stack[256:512, :])
            state[below, window] = state[below, window] - update

    ft_ref[...] = state[:LEAD, :LEAD]

    @pl.loop(0, blocks)
    def _(k):
        rows = pl.ds(pl.multiple_of(k * BASE, BASE), BASE)
        slab = state[rows, LEAD:]
        hh_ref[rows, :], hl_ref[rows, :] = split(slab)
        th_ref[:, rows], tl_ref[:, rows] = split(jnp.transpose(slab))


def weights_kernel(info, u_ref, v_ref, wr_ref, wc_ref, hh, hl, th, tl, yh_ref, yl_ref, ah, al, zh, zl):
    slot = pl.program_id(0)
    column = info[slot]
    panel = column < 2
    top, low = pl.ds(0, TILE), pl.ds(TILE, TILE)

    @pl.when(jnp.logical_not(panel))
    def _():
        for half in range(2):
            @pl.loop(0, TILE // 256)
            def _(chunk):
                start = pl.multiple_of(chunk * 256, 256)
                values = assemble(u_ref, v_ref, wr_ref, wc_ref, half, 6 + slot, start, 256)
                rows = pl.ds(half * TILE + start, 256)
                ah[rows, :], al[rows, :] = split(values)
        zh[top, :], zl[top, :] = split(dot3(hh[top, top], hl[top, top], ah[top, :], al[top, :]))
        zh[low, :], zl[low, :] = split(dot3(hh[low, :], hl[low, :], ah[...], al[...]))

    @pl.when(panel)
    def _():
        row = lax.broadcasted_iota(jnp.int32, (LEAD, TILE), 0)
        col = lax.broadcasted_iota(jnp.int32, (LEAD, TILE), 1)
        zh[...] = jnp.where(row == col + column * TILE, -1.0, 0.0).astype(BF16)
        zl[...] = jnp.zeros((LEAD, TILE), BF16)

    yh_ref[top, :], yl_ref[top, :] = split(dot3(th[top, :], tl[top, :], zh[...], zl[...]))
    yh_ref[low, :], yl_ref[low, :] = split(dot3(th[low, low], tl[low, low], zh[low, :], zl[low, :]))


CHUNK = 256
ZERO, UPDATE, DIAGONAL, PANEL, FACTOR = range(5)


def final_kernel(info, u_ref, v_ref, wr_ref, wc_ref, yh, yl, ft_ref, out_ref, ah, al):
    slot, chunk = pl.program_id(0), pl.program_id(1)
    start = pl.multiple_of(chunk * CHUNK, CHUNK)
    kinds = [info[2 + slot * 2], info[3 + slot * 2]]

    def store(j, values):
        for q in range(TILE // 128):
            out_ref[pl.ds(j * 4 + q, CHUNK, stride=8), :] = values[:, q * 128 : (q + 1) * 128]

    needed = lambda kind: (kind != ZERO) & (kind != FACTOR)

    @pl.when(needed(kinds[0]) | needed(kinds[1]))
    def _():
        for half in range(2):
            values = assemble(u_ref, v_ref, wr_ref, wc_ref, 2 + slot, half, start, CHUNK)
            cols = pl.ds(half * TILE, TILE)
            ah[:, cols], al[:, cols] = split(values)

    for j in range(2):
        kind = kinds[j]

        @pl.when(kind == ZERO)
        def _():
            store(j, jnp.zeros((CHUNK, TILE), F32))

        @pl.when(kind == PANEL)
        def _():
            store(j, -dot3(ah[...], al[...], yh[j], yl[j]))

        @pl.when((kind == UPDATE) | (kind == DIAGONAL))
        def _():
            values = assemble(u_ref, v_ref, wr_ref, wc_ref, 2 + slot, 6 + j, start, CHUNK)
            row = start + lax.broadcasted_iota(jnp.int32, (CHUNK, TILE), 0)
            col = lax.broadcasted_iota(jnp.int32, (CHUNK, TILE), 1)
            shift = wr_ref[2 + slot, pl.ds(start, CHUNK), 4:5]
            values = values + jnp.where((row == col) & (kind == DIAGONAL), shift, 0.0)
            store(j, values - dot3(ah[...], al[...], yh[j], yl[j]))

        if j == 0:
            @pl.when(kind == FACTOR)
            def _():
                which = info[10]
                lanes = pl.ds(pl.multiple_of(which // 2 * TILE + start, CHUNK), CHUNK)
                rows = pl.ds(pl.multiple_of(which % 2 * TILE, TILE), TILE)
                values = jnp.transpose(ft_ref[rows, lanes])
                row = start + lax.broadcasted_iota(jnp.int32, (CHUNK, TILE), 0)
                col = lax.broadcasted_iota(jnp.int32, (CHUNK, TILE), 1)
                keep = (row >= col) | (which // 2 != which % 2)
                store(j, jnp.where(keep, values, 0.0))


def whole(count):
    return [pl.BlockSpec(memory_space=pltpu.VMEM)] * count


def shards(points, weights, shift, cluster_rank):
    rows, cols = lax.axis_size("row"), lax.axis_size("col")
    row, col = lax.axis_index("row"), lax.axis_index("col")
    width = shift.shape[0]
    fill = jnp.zeros((7, width), F32)
    shard = jnp.concatenate([points.reshape(12, width), weights, shift[None], fill], 0)
    gathered = gather_shards(shard)

    slots = jnp.arange(4, dtype=jnp.int32)
    tile_rows = row + rows * slots
    tile_cols = col + cols * slots[:2]
    wanted = jnp.concatenate([slots[:2], tile_rows, tile_cols])
    clusters = jnp.arange(cluster_rank.shape[0], dtype=jnp.int32)
    found = jnp.sum(jnp.where(cluster_rank[None, :] == wanted[:, None], clusters[None, :], 0), axis=1)
    from_row, from_x = found // 4, found % 4
    dy = (row // 2 - from_row // 2) % 4
    dc = (row % 2 - from_row % 2) % 2
    dx = (col // 4 - from_x) % 4
    dz = (col % 4 - slots) % 4
    where = ((((dc * 4 + dy) * 4 + dx) * 4)[:, None] + dz[None, :]).reshape(-1).astype(jnp.int32)

    part = lambda z: pl.BlockSpec((None, 24, width), lambda t, at: (at[4 * t + z], 0, 0))
    u, v, wr, wc = pl.pallas_call(
        prep_kernel,
        grid_spec=pltpu.PrefetchScalarGridSpec(
            num_scalar_prefetch=1,
            grid=(8,),
            in_specs=[part(z) for z in range(4)],
            out_specs=[
                pl.BlockSpec((None, QUAD, TILE, FEAT), lambda t, at: (t, 0, 0, 0)),
                pl.BlockSpec((None, QUAD, FEAT, TILE), lambda t, at: (t, 0, 0, 0)),
                pl.BlockSpec((None, TILE, 128), lambda t, at: (t, 0, 0)),
                pl.BlockSpec((None, 8, TILE), lambda t, at: (t, 0, 0)),
            ],
            scratch_shapes=[pltpu.VMEM((128, TILE), F32)],
        ),
        out_shape=[
            jax.ShapeDtypeStruct((8, QUAD, TILE, FEAT), BF16),
            jax.ShapeDtypeStruct((8, QUAD, FEAT, TILE), BF16),
            jax.ShapeDtypeStruct((8, TILE, 128), F32),
            jax.ShapeDtypeStruct((8, 8, TILE), F32),
        ],
        name="prep",
    )(where, *[gathered] * 4)

    square = jax.ShapeDtypeStruct((LEAD, LEAD), BF16)
    ft, hh, hl, th, tl = pl.pallas_call(
        chain_kernel,
        in_specs=whole(4),
        out_specs=whole(5),
        out_shape=[jax.ShapeDtypeStruct((LEAD, LEAD), F32)] + [square] * 4,
        scratch_shapes=[
            pltpu.VMEM((LEAD + BASE, 2 * LEAD), F32),
            pltpu.VMEM((BASE, BASE), F32),
            pltpu.VMEM((STEP, STEP, BASE), F32),
            pltpu.VMEM((STEP, STEP, BASE), F32),
            pltpu.VMEM((STEP, BASE), F32),
            pltpu.VMEM((4 * BASE, WINDOW), BF16),
            pltpu.VMEM((LEAD, 6 * BASE), BF16),
        ],
        name="chain",
    )(u, v, wr, wc)

    block_rows, block_cols = tile_rows[:, None], tile_cols[None, :]
    kinds = jnp.where(
        block_rows < block_cols,
        ZERO,
        jnp.where(
            block_cols >= 2,
            jnp.where(block_rows == block_cols, DIAGONAL, UPDATE),
            jnp.where(block_rows < 2, FACTOR, PANEL),
        ),
    )
    info = jnp.concatenate([tile_cols, kinds.reshape(-1), (row * 2 + col)[None]]).astype(jnp.int32)

    half = jax.ShapeDtypeStruct((2, LEAD, TILE), BF16)
    yh, yl = pl.pallas_call(
        weights_kernel,
        grid_spec=pltpu.PrefetchScalarGridSpec(
            num_scalar_prefetch=1,
            grid=(2,),
            in_specs=whole(8),
            out_specs=[pl.BlockSpec((None, LEAD, TILE), lambda j, info: (j, 0, 0))] * 2,
            scratch_shapes=[pltpu.VMEM((LEAD, TILE), BF16)] * 4,
        ),
        out_shape=[half, half],
        name="weights",
    )(info, u, v, wr, wc, hh, hl, th, tl)

    lines = CHUNK * 8
    out = pl.pallas_call(
        final_kernel,
        grid_spec=pltpu.PrefetchScalarGridSpec(
            num_scalar_prefetch=1,
            grid=(4, TILE // CHUNK),
            in_specs=whole(7),
            out_specs=pl.BlockSpec((lines, 128), lambda i, h, info: (i * (TILE // CHUNK) + h, 0)),
            scratch_shapes=[pltpu.VMEM((CHUNK, LEAD), BF16)] * 2,
        ),
        out_shape=jax.ShapeDtypeStruct((4 * TILE * 8, 128), F32),
        name="final",
    )(info, u, v, wr, wc, yh, yl, ft)
    return out.reshape(4, 1, TILE, 2, 1, TILE)


def solution(mesh):
    return jax.shard_map(
        shards,
        mesh=mesh,
        in_specs=(P(None, None, ("row", "col")), P(None, ("row", "col")), P(("row", "col")), P()),
        out_specs=P(None, "row", None, None, "col", None),
        check_vma=False,
    )
```

```python
import functools

import jax
import jax.numpy as jnp
from jax import lax
from jax.experimental import pallas as pl
from jax.experimental.pallas import tpu as pltpu
from jax.sharding import PartitionSpec as P

SOFTENING_SQUARED = 0.0004
F32 = jnp.float32
BF16 = jnp.bfloat16
QUAD = 4
TILE = 512
FEAT = 48
LEAD = 1024
BASE = 128
STEP = 16
WINDOW = LEAD + BASE
HIGHEST = lax.Precision.HIGHEST


def split(value):
    high = value.astype(BF16)
    return high, (value - high.astype(F32)).astype(BF16)


def dot3(a_high, a_low, b_high, b_low):
    dot = functools.partial(jnp.dot, preferred_element_type=F32)
    return dot(a_high, b_high) + (dot(a_high, b_low) + dot(a_low, b_high))


def send(value, move, rows, cols):
    ys, xs = rows // 2, 4
    zs = cols // xs
    pairs = []
    for source in range(rows * cols):
        row, col = divmod(source, cols)
        y, core, x, z = move(row // 2, row % 2, col // zs, col % zs)
        pairs.append((source, ((y % ys) * 2 + core % 2) * cols + (x % xs) * zs + z % zs))
    return lax.ppermute(value, ("row", "col"), pairs)


def gather_shards(shard):
    rows, cols = lax.axis_size("row"), lax.axis_size("col")
    held = shard[None]
    for axis in (3, 2, 0):
        moved = [held]
        for k in range(1, 4):
            move = lambda *at, k=k: [part + k * (i == axis) for i, part in enumerate(at)]
            moved.append(send(held, move, rows, cols))
        held = jnp.concatenate(moved, 0)
    return jnp.concatenate([held, send(held, lambda y, c, x, z: (y, c + 1, x, z), rows, cols)], 0)


def prep_kernel(where_ref, g0, g1, g2, g3, u_ref, v_ref, wr_ref, wc_ref, pad):
    geometry = jnp.concatenate([g0[...], g1[...], g2[...], g3[...]], axis=1)
    centred = geometry[0:12] - 0.5
    coarse = jnp.floor(centred * 256.0 + 0.5) * (1.0 / 256.0)
    fine = centred - coarse
    fine_high = fine.astype(BF16).astype(F32)
    fine_low = fine - fine_high
    per = lambda value: [value[4 * c : 4 * c + 4] for c in range(3)]
    coarse, fine, fine_high, fine_low = per(coarse), per(fine), per(fine_high), per(fine_low)
    norm = sum(c * c for c in coarse)
    norm_high = jnp.floor(norm * 256.0) * (1.0 / 256.0)
    norm_low = norm - norm_high
    mixed = sum(2.0 * c * f + f * f for c, f in zip(coarse, fine))

    def pieces(value):
        first = value.astype(BF16).astype(F32)
        second = (value - first).astype(BF16).astype(F32)
        return [first, second, value - first - second]

    one = jnp.ones_like(norm)
    twice = lambda values: [-2.0 * value for value in values]
    left = twice(coarse) + [norm_high, norm_low, one, one]
    left += twice(coarse) + twice(coarse) + twice(fine_high) + twice(fine_low)
    left += twice(fine_high) + twice(fine_high) + twice(fine_low)
    left += pieces(mixed) + [one] * 3
    right = coarse + [one, one, norm_high, norm_low]
    right += fine_high + fine_low + coarse + coarse
    right += fine_high + fine_low + fine_high
    right += [one] * 3 + pieces(mixed + SOFTENING_SQUARED)
    pad[...] = jnp.zeros_like(pad)
    tile = pl.program_id(0)

    @pl.when(tile < 6)
    def _():
        for quad in range(QUAD):
            for k, value in enumerate(left):
                pad[k : k + 1, :] = value[quad : quad + 1, :]
            u_ref[quad] = jnp.transpose(pad[...])[:, :FEAT].astype(BF16)

    @pl.when((tile < 2) | (tile >= 6))
    def _():
        for quad in range(QUAD):
            for k, value in enumerate(right):
                pad[k : k + 1, :] = value[quad : quad + 1, :]
            v_ref[quad] = pad[0:FEAT, :].astype(BF16)

    pad[0:8, :] = geometry[12:20]
    wr_ref[...] = jnp.transpose(pad[...])
    wc_ref[...] = geometry[12:20]


def assemble(u_ref, v_ref, wr_ref, wc_ref, left, right, start, count, cols=slice(0, TILE)):
    rows = pl.ds(start, count)
    total = None
    for first in range(QUAD):
        part = None
        for second in range(QUAD):
            squared = jnp.dot(u_ref[left, first, rows, :], v_ref[right, second, :, cols], preferred_element_type=F32)
            term = lax.rsqrt(squared) * wc_ref[right, second : second + 1, cols]
            part = term if part is None else part + term
        part = part * wr_ref[left, rows, first : first + 1]
        total = part if total is None else total + part
    return total


def split3(value):
    first = value.astype(BF16)
    rest = value - first.astype(F32)
    second = rest.astype(BF16)
    return first, second, (rest - second.astype(F32)).astype(BF16)


def dot_rows(left, right):
    return lax.dot_general(left, right, (((0,), (0,)), ((), ())), preferred_element_type=F32)


def eliminate_base(work, spread, solved, lines):
    lane = lax.broadcasted_iota(jnp.int32, (8, BASE), 1)
    sub = lax.broadcasted_iota(jnp.int32, (8, BASE), 0)
    repeat = lambda ref, i: ref[pl.ds(i, 8, stride=0), :]
    for step in range(BASE // STEP):
        low = step * STEP
        high = low + STEP
        a, c = [], [[], []]
        for half in range(2):
            left = work[low + 8 * half : low + 8 * half + 8, :]
            for j in range(STEP):
                column = jnp.broadcast_to(left[:, low + j : low + j + 1], (8, BASE))
                c[half].append(column)
            inside = (lane >= low) & (lane < high)
            a.append(jnp.where(inside, jnp.where(lane == sub + (low + 8 * half), 1.0, 0.0), left))
            lines[8 * half : 8 * half + 8, :] = a[half]
        d = []
        for half in range(2):
            diagonal = c[half][8 * half]
            for j in range(8 * half + 1, 8 * half + 8):
                diagonal = jnp.where(sub == j % 8, c[half][j], diagonal)
            d.append(diagonal)
            spread[0, 8 * half : 8 * half + 8, :] = diagonal
        pivot = repeat(spread.at[0], 0)
        for j in range(STEP):
            scale = lax.rsqrt(pivot)
            first = j // 8
            line = repeat(lines, j) * scale
            for half in range(first, 2):
                c[half][j] = c[half][j] * scale
                solved[j, 8 * half : 8 * half + 8, :] = c[half][j]
                if j + 2 < STEP:
                    d[half] = d[half] - c[half][j] * c[half][j]
                    spread[j + 1, 8 * half : 8 * half + 8, :] = d[half]
            for k in range(j + 1, STEP):
                factor = repeat(solved.at[j], k)
                if k == j + 1:
                    pivot = repeat(spread.at[j], k) - factor * factor
                for half in range(k // 8, 2):
                    c[half][k] = c[half][k] - c[half][j] * factor
            for half in range(first, 2):
                update = a[half] - c[half][j] * line
                if half == first:
                    update = jnp.where(sub > j % 8, update, jnp.where(sub == j % 8, line, a[half]))
                a[half] = update
                lines[8 * half : 8 * half + 8, :] = update
        for half in range(2):
            work[low + 8 * half : low + 8 * half + 8, :] = a[half]
        if high < BASE:
            w0, w1, w2 = split3(jnp.concatenate(a, 0))
            product = dot_rows(
                jnp.concatenate([w0, w0, w1, w0, w1, w2], 0), jnp.concatenate([w0, w1, w0, w2, w1, w0], 0)
            )
            rest = lax.broadcasted_iota(jnp.int32, (BASE - high, BASE), 1)
            kept = jnp.where((rest >= low) & (rest < high), 0.0, work[high:, :])
            work[high:, :] = kept - product[high:, :]


def chain_kernel(
    info, u_ref, v_ref, wr_ref, wc_ref,
    ft_ref, y_ref,
    state, side, work, spread, solved, lines, stack, tall,
):
    state[:, LEAD:] = jnp.zeros((LEAD + BASE, LEAD), F32)
    state[LEAD:, :LEAD] = jnp.zeros((BASE, LEAD), F32)
    side[LEAD:, :] = jnp.zeros((BASE, BASE), F32)
    lane = lax.broadcasted_iota(jnp.int32, (BASE, BASE), 1)
    row = lax.broadcasted_iota(jnp.int32, (BASE, BASE), 0)
    eye = (row == lane).astype(F32)
    geometry = (u_ref, v_ref, wr_ref, wc_ref)
    slot, column = info[0], info[1]
    offset = pl.multiple_of(info[2], BASE)

    @pl.loop(0, TILE // 256)
    def _(chunk):
        start = pl.multiple_of(chunk * 256, 256)
        rows = pl.ds(start, 256)
        for tile in range(2):
            here = pl.ds(pl.multiple_of(tile * TILE + start, 256), 256)
            low = tile * TILE
            values = assemble(*geometry, tile, tile, start, 256, slice(256, TILE))
            line = start + lax.broadcasted_iota(jnp.int32, (256, 256), 0)
            across = 256 + lax.broadcasted_iota(jnp.int32, (256, 256), 1)
            values = values + jnp.where(line == across, wr_ref[tile, rows, 4:5], 0.0)
            state[here, low + 256 : low + TILE] = values
            side[here, :] = assemble(*geometry, tile, 6 + slot, start, 256, pl.ds(offset, BASE))
        state[rows, TILE : 2 * TILE] = assemble(*geometry, 0, 1, start, 256)

    for tile in range(2):
        values = assemble(*geometry, tile, tile, 0, 256, slice(0, 256))
        line = lax.broadcasted_iota(jnp.int32, (256, 256), 0)
        across = lax.broadcasted_iota(jnp.int32, (256, 256), 1)
        values = values + jnp.where(line == across, wr_ref[tile, 0:256, 4:5], 0.0)
        state[tile * TILE : tile * TILE + 256, tile * TILE : tile * TILE + 256] = values

    blocks = LEAD // BASE
    both = jnp.concatenate
    dot = functools.partial(jnp.dot, preferred_element_type=F32)

    @pl.loop(0, blocks)
    def _(k):
        here = pl.multiple_of(k * BASE, BASE)
        rows = pl.ds(here, BASE)
        state[rows, pl.ds(pl.multiple_of(LEAD + here, BASE), BASE)] = eye
        work[...] = state[rows, pl.ds(here, BASE)]
        eliminate_base(work, spread, solved, lines)
        l0, l1, l2 = split3(jnp.where(row >= lane, work[...], 0.0))
        window = pl.ds(here, WINDOW)

        def load(values):
            first, second, third = split3(values)
            stack[0:128, :] = first
            stack[128:256, :] = second
            stack[256:384, :] = third
            stack[384:512, :] = first

        load(both([state[rows, window], side[rows, :]], 1))
        two = dot(both([both([l0, l0], 1), both([l1, l1], 1)], 0), stack[0:256, :])
        done = two[:BASE] + (two[BASE:] + dot(both([l0, l2], 1), stack[256:512, :]))
        state[rows, window] = done[:, :WINDOW]
        side[rows, :] = done[:, WINDOW:]
        load(done)

        @pl.loop(0, blocks - 1 - k)
        def _(i):
            there = pl.multiple_of((i + 1) * BASE, BASE)
            first, second, third = split3(jnp.transpose(state[rows, pl.ds(pl.multiple_of(here + there, BASE), BASE)]))
            part = pl.ds(pl.multiple_of(i * BASE, BASE), BASE)
            tall[part, 0:128] = first
            tall[part, 128:256] = first
            tall[part, 256:384] = second
            tall[part, 384:512] = second
            tall[part, 512:640] = first
            tall[part, 640:768] = third

        @pl.loop(0, (blocks - k) // 2)
        def _(pair):
            part = pl.ds(pl.multiple_of(pair * 256, 256), 256)
            below = pl.ds(pl.multiple_of(here + BASE + pair * 256, BASE), 256)
            update = dot(tall[part, 0:256], stack[0:256, :])
            update += dot(tall[part, 256:512], stack[0:256, :])
            update += dot(tall[part, 512:768], stack[256:512, :])
            state[below, window] = state[below, window] - update[:, :WINDOW]
            side[below, :] = side[below, :] - update[:, WINDOW:]

    ft_ref[...] = state[:LEAD, :LEAD]

    @pl.when(column < 2)
    def _():
        line = lax.broadcasted_iota(jnp.int32, (LEAD, BASE), 0)
        across = lax.broadcasted_iota(jnp.int32, (LEAD, BASE), 1)
        side[:LEAD, :] = jnp.where(line == across + (column * TILE + offset), -1.0, 0.0)

    for out in range(4):
        total = jnp.zeros((256, BASE), F32)
        for part in range(out, 4):
            rows = slice(part * 256, part * 256 + 256)
            factor = jnp.transpose(state[rows, LEAD + out * 256 : LEAD + out * 256 + 256])
            high, low = split(factor)
            z_high, z_low = split(side[rows, :])
            wide = dot(high, both([z_high, z_low], 1))
            total = total + (wide[:, :BASE] + (wide[:, BASE:] + dot(low, z_high)))
        y_ref[out * 256 : out * 256 + 256, :] = total


def panel_kernel(base, info, u_ref, v_ref, wr_ref, wc_ref, *refs):
    ah_ref, al_ref = refs[-2:]
    slot, chunk = base + pl.program_id(0), pl.program_id(1)
    start = pl.multiple_of(chunk * CHUNK, CHUNK)
    kinds = [info[3 + slot * 2], info[4 + slot * 2]]
    needed = lambda kind: (kind != ZERO) & (kind != FACTOR)

    @pl.when(needed(kinds[0]) | needed(kinds[1]))
    def _():
        for half in range(2):
            values = assemble(u_ref, v_ref, wr_ref, wc_ref, 2 + slot, half, start, CHUNK)
            cols = slice(half * TILE, half * TILE + TILE)
            ah_ref[:, cols], al_ref[:, cols] = split(values)


CHUNK = 256
ZERO, UPDATE, DIAGONAL, PANEL, FACTOR = range(5)


def final_kernel(info, u_ref, v_ref, wr_ref, wc_ref, ft_ref, *rest):
    parts, (ah, al, out_ref, yh, yl) = rest[:8], rest[8:]
    slot, chunk = pl.program_id(0), pl.program_id(1)
    start = pl.multiple_of(chunk * CHUNK, CHUNK)
    kinds = [info[3 + slot * 2], info[4 + slot * 2]]

    @pl.when((slot == 0) & (chunk == 0))
    def _():
        for p, part in enumerate(parts):
            source = info[12 + p]
            lanes = pl.ds(pl.multiple_of(source % 4 * 128, 128), 128)
            yh[source // 4, :, lanes], yl[source // 4, :, lanes] = split(part[...])

    def store(j, values):
        for q in range(TILE // 128):
            out_ref[pl.ds(j * 4 + q, CHUNK, stride=8), :] = values[:, q * 128 : (q + 1) * 128]

    for j in range(2):
        kind = kinds[j]

        @pl.when(kind == ZERO)
        def _():
            store(j, jnp.zeros((CHUNK, TILE), F32))

        @pl.when(kind == PANEL)
        def _():
            store(j, -dot3(ah[...], al[...], yh[j], yl[j]))

        @pl.when((kind == UPDATE) | (kind == DIAGONAL))
        def _():
            values = assemble(u_ref, v_ref, wr_ref, wc_ref, 2 + slot, 6 + j, start, CHUNK)
            row = start + lax.broadcasted_iota(jnp.int32, (CHUNK, TILE), 0)
            col = lax.broadcasted_iota(jnp.int32, (CHUNK, TILE), 1)
            shift = wr_ref[2 + slot, pl.ds(start, CHUNK), 4:5]
            values = values + jnp.where((row == col) & (kind == DIAGONAL), shift, 0.0)
            store(j, values - dot3(ah[...], al[...], yh[j], yl[j]))

        if j == 0:
            @pl.when(kind == FACTOR)
            def _():
                which = info[11]
                lanes = pl.ds(pl.multiple_of(which // 2 * TILE + start, CHUNK), CHUNK)
                rows = pl.ds(pl.multiple_of(which % 2 * TILE, TILE), TILE)
                values = jnp.transpose(ft_ref[rows, lanes])
                row = start + lax.broadcasted_iota(jnp.int32, (CHUNK, TILE), 0)
                col = lax.broadcasted_iota(jnp.int32, (CHUNK, TILE), 1)
                keep = (row >= col) | (which // 2 != which % 2)
                store(j, jnp.where(keep, values, 0.0))


def whole(count):
    return [pl.BlockSpec(memory_space=pltpu.VMEM)] * count


def shards(points, weights, shift, cluster_rank):
    rows, cols = lax.axis_size("row"), lax.axis_size("col")
    row, col = lax.axis_index("row"), lax.axis_index("col")
    width = shift.shape[0]
    fill = jnp.zeros((7, width), F32)
    shard = jnp.concatenate([points.reshape(12, width), weights, shift[None], fill], 0)
    gathered = gather_shards(shard)

    slots = jnp.arange(4, dtype=jnp.int32)
    tile_rows = row + rows * slots
    tile_cols = col + cols * slots[:2]
    wanted = jnp.concatenate([slots[:2], tile_rows, tile_cols])
    clusters = jnp.arange(cluster_rank.shape[0], dtype=jnp.int32)
    found = jnp.sum(jnp.where(cluster_rank[None, :] == wanted[:, None], clusters[None, :], 0), axis=1)
    from_row, from_x = found // 4, found % 4
    dy = (row // 2 - from_row // 2) % 4
    dc = (row % 2 - from_row % 2) % 2
    dx = (col // 4 - from_x) % 4
    dz = (col % 4 - slots) % 4
    where = ((((dc * 4 + dy) * 4 + dx) * 4)[:, None] + dz[None, :]).reshape(-1).astype(jnp.int32)

    part = lambda z: pl.BlockSpec((None, 24, width), lambda t, at: (at[4 * t + z], 0, 0))
    u, v, wr, wc = pl.pallas_call(
        prep_kernel,
        grid_spec=pltpu.PrefetchScalarGridSpec(
            num_scalar_prefetch=1,
            grid=(8,),
            in_specs=[part(z) for z in range(4)],
            out_specs=[
                pl.BlockSpec((None, QUAD, TILE, FEAT), lambda t, at: (t, 0, 0, 0)),
                pl.BlockSpec((None, QUAD, FEAT, TILE), lambda t, at: (t, 0, 0, 0)),
                pl.BlockSpec((None, TILE, 128), lambda t, at: (t, 0, 0)),
                pl.BlockSpec((None, 8, TILE), lambda t, at: (t, 0, 0)),
            ],
            scratch_shapes=[pltpu.VMEM((128, TILE), F32)],
        ),
        out_shape=[
            jax.ShapeDtypeStruct((8, QUAD, TILE, FEAT), BF16),
            jax.ShapeDtypeStruct((8, QUAD, FEAT, TILE), BF16),
            jax.ShapeDtypeStruct((8, TILE, 128), F32),
            jax.ShapeDtypeStruct((8, 8, TILE), F32),
        ],
        name="prep",
    )(where, *[gathered] * 4)

    block_rows, block_cols = tile_rows[:, None], tile_cols[None, :]
    kinds = jnp.where(
        block_rows < block_cols,
        ZERO,
        jnp.where(
            block_cols >= 2,
            jnp.where(block_rows == block_cols, DIAGONAL, UPDATE),
            jnp.where(block_rows < 2, FACTOR, PANEL),
        ),
    )
    mine = row // 4
    order = jnp.arange(8, dtype=jnp.int32)
    sources = (row // 2 - order % 4) % 4 * 2 + (row % 2 - order // 4) % 2
    head = jnp.stack([mine, col + cols * mine, row % 4 * BASE])
    info = jnp.concatenate([head, kinds.reshape(-1), (row * 2 + col)[None], sources]).astype(jnp.int32)

    smem = [pl.BlockSpec(memory_space=pltpu.SMEM)]
    ft, weights_part = pl.pallas_call(
        chain_kernel,
        in_specs=smem + whole(4),
        out_specs=whole(2),
        out_shape=[jax.ShapeDtypeStruct((LEAD, LEAD), F32), jax.ShapeDtypeStruct((LEAD, BASE), F32)],
        scratch_shapes=[
            pltpu.VMEM((LEAD + BASE, 2 * LEAD), F32),
            pltpu.VMEM((LEAD + BASE, BASE), F32),
            pltpu.VMEM((BASE, BASE), F32),
            pltpu.VMEM((STEP, STEP, BASE), F32),
            pltpu.VMEM((STEP, STEP, BASE), F32),
            pltpu.VMEM((STEP, BASE), F32),
            pltpu.VMEM((4 * BASE, WINDOW + BASE), BF16),
            pltpu.VMEM((LEAD, 6 * BASE), BF16),
        ],
        name="chain",
    )(info, u, v, wr, wc)

    tall = jax.ShapeDtypeStruct((4 * TILE, LEAD), BF16)
    chunks = TILE // CHUNK

    def panel(base, held):
        blocked = pl.BlockSpec((CHUNK, LEAD), lambda i, h, info: ((base + i) * chunks + h, 0))
        return pl.pallas_call(
            functools.partial(panel_kernel, base),
            grid_spec=pltpu.PrefetchScalarGridSpec(
                num_scalar_prefetch=1,
                grid=(2, chunks),
                in_specs=whole(4) + [pl.BlockSpec(memory_space=pl.ANY)] * len(held),
                out_specs=[blocked] * 2,
            ),
            out_shape=[tall] * 2,
            input_output_aliases={5 + i: i for i in range(len(held))},
            cost_estimate=pl.CostEstimate(
                flops=30_000_000_000, bytes_accessed=8_000_000, transcendentals=17_000_000
            ),
            name=f"panel{base}",
        )(info, u, v, wr, wc, *held)

    near = [send(weights_part, lambda y, c, x, z, k=k: (y + k, c, x, z), rows, cols) for k in range(1, 4)]
    *near, ah, al = lax.optimization_barrier((*near, *panel(0, [])))
    parts = [weights_part] + near
    parts = parts + [send(part, lambda y, c, x, z: (y, c + 1, x, z), rows, cols) for part in parts]
    *parts, ah, al = lax.optimization_barrier((*parts, *panel(2, [ah, al])))

    lines = CHUNK * 8
    out = pl.pallas_call(
        final_kernel,
        grid_spec=pltpu.PrefetchScalarGridSpec(
            num_scalar_prefetch=1,
            grid=(4, chunks),
            in_specs=whole(13)
            + [pl.BlockSpec((CHUNK, LEAD), lambda i, h, info: (i * chunks + h, 0))] * 2,
            out_specs=pl.BlockSpec((lines, 128), lambda i, h, info: (i * chunks + h, 0)),
            scratch_shapes=[pltpu.VMEM((2, LEAD, TILE), BF16)] * 2,
        ),
        out_shape=jax.ShapeDtypeStruct((4 * TILE * 8, 128), F32),
        name="final",
    )(info, u, v, wr, wc, ft, *parts, ah, al)
    return out.reshape(4, 1, TILE, 2, 1, TILE)


def solution(mesh):
    return jax.shard_map(
        shards,
        mesh=mesh,
        in_specs=(P(None, None, ("row", "col")), P(None, ("row", "col")), P(("row", "col")), P()),
        out_specs=P(None, "row", None, None, "col", None),
        check_vma=False,
    )
```

```python
import functools

import jax
import jax.numpy as jnp
from jax import lax
from jax.experimental import pallas as pl
from jax.experimental.pallas import tpu as pltpu
from jax.sharding import PartitionSpec as P

SOFTENING_SQUARED = 0.0004
F32 = jnp.float32
BF16 = jnp.bfloat16
QUAD = 4
TILE = 512
FEAT = 48
LEAD = 1024
BASE = 128
STEP = 16
WINDOW = LEAD + BASE
HIGHEST = lax.Precision.HIGHEST


def split(value):
    high = value.astype(BF16)
    return high, (value - high.astype(F32)).astype(BF16)


def dot3(a_high, a_low, b_high, b_low):
    dot = functools.partial(jnp.dot, preferred_element_type=F32)
    return dot(a_high, b_high) + (dot(a_high, b_low) + dot(a_low, b_high))


def send(value, move, rows, cols):
    ys, xs = rows // 2, 4
    zs = cols // xs
    pairs = []
    for source in range(rows * cols):
        row, col = divmod(source, cols)
        y, core, x, z = move(row // 2, row % 2, col // zs, col % zs)
        pairs.append((source, ((y % ys) * 2 + core % 2) * cols + (x % xs) * zs + z % zs))
    return lax.ppermute(value, ("row", "col"), pairs)


def gather_shards(shard):
    rows, cols = lax.axis_size("row"), lax.axis_size("col")
    held = shard[None]
    for axis in (3, 2, 0):
        moved = [held]
        for k in range(1, 4):
            move = lambda *at, k=k: [part + k * (i == axis) for i, part in enumerate(at)]
            moved.append(send(held, move, rows, cols))
        held = jnp.concatenate(moved, 0)
    return jnp.concatenate([held, send(held, lambda y, c, x, z: (y, c + 1, x, z), rows, cols)], 0)


def prep_kernel(where_ref, g0, g1, g2, g3, u_ref, v_ref, wr_ref, wc_ref, pad):
    geometry = jnp.concatenate([g0[...], g1[...], g2[...], g3[...]], axis=1)
    centred = geometry[0:12] - 0.5
    coarse = jnp.floor(centred * 256.0 + 0.5) * (1.0 / 256.0)
    fine = centred - coarse
    fine_high = fine.astype(BF16).astype(F32)
    fine_low = fine - fine_high
    per = lambda value: [value[4 * c : 4 * c + 4] for c in range(3)]
    coarse, fine, fine_high, fine_low = per(coarse), per(fine), per(fine_high), per(fine_low)
    norm = sum(c * c for c in coarse)
    norm_high = jnp.floor(norm * 256.0) * (1.0 / 256.0)
    norm_low = norm - norm_high
    mixed = sum(2.0 * c * f + f * f for c, f in zip(coarse, fine))

    def pieces(value):
        first = value.astype(BF16).astype(F32)
        second = (value - first).astype(BF16).astype(F32)
        return [first, second, value - first - second]

    one = jnp.ones_like(norm)
    twice = lambda values: [-2.0 * value for value in values]
    left = twice(coarse) + [norm_high, norm_low, one, one]
    left += twice(coarse) + twice(coarse) + twice(fine_high) + twice(fine_low)
    left += twice(fine_high) + twice(fine_high) + twice(fine_low)
    left += pieces(mixed) + [one] * 3
    right = coarse + [one, one, norm_high, norm_low]
    right += fine_high + fine_low + coarse + coarse
    right += fine_high + fine_low + fine_high
    right += [one] * 3 + pieces(mixed + SOFTENING_SQUARED)
    pad[...] = jnp.zeros_like(pad)
    tile = pl.program_id(0)

    @pl.when(tile < 6)
    def _():
        for quad in range(QUAD):
            for k, value in enumerate(left):
                pad[k : k + 1, :] = value[quad : quad + 1, :]
            u_ref[quad] = jnp.transpose(pad[...])[:, :FEAT].astype(BF16)

    @pl.when((tile < 2) | (tile >= 6))
    def _():
        for quad in range(QUAD):
            for k, value in enumerate(right):
                pad[k : k + 1, :] = value[quad : quad + 1, :]
            v_ref[quad] = pad[0:FEAT, :].astype(BF16)

    pad[0:8, :] = geometry[12:20]
    wr_ref[...] = jnp.transpose(pad[...])
    wc_ref[...] = geometry[12:20]


def assemble(u_ref, v_ref, wr_ref, wc_ref, left, right, start, count, cols=slice(0, TILE)):
    rows = pl.ds(start, count)
    total = None
    for first in range(QUAD):
        part = None
        for second in range(QUAD):
            squared = jnp.dot(u_ref[left, first, rows, :], v_ref[right, second, :, cols], preferred_element_type=F32)
            term = lax.rsqrt(squared) * wc_ref[right, second : second + 1, cols]
            part = term if part is None else part + term
        part = part * wr_ref[left, rows, first : first + 1]
        total = part if total is None else total + part
    return total


def split3(value):
    first = value.astype(BF16)
    rest = value - first.astype(F32)
    second = rest.astype(BF16)
    return first, second, (rest - second.astype(F32)).astype(BF16)


def dot_rows(left, right):
    return lax.dot_general(left, right, (((0,), (0,)), ((), ())), preferred_element_type=F32)


def eliminate_base(work, spread, solved, lines):
    lane = lax.broadcasted_iota(jnp.int32, (8, BASE), 1)
    sub = lax.broadcasted_iota(jnp.int32, (8, BASE), 0)
    repeat = lambda ref, i: ref[pl.ds(i, 8, stride=0), :]
    for step in range(BASE // STEP):
        low = step * STEP
        high = low + STEP
        a, c = [], [[], []]
        for half in range(2):
            left = work[low + 8 * half : low + 8 * half + 8, :]
            for j in range(STEP):
                column = jnp.broadcast_to(left[:, low + j : low + j + 1], (8, BASE))
                c[half].append(column)
            inside = (lane >= low) & (lane < high)
            a.append(jnp.where(inside, jnp.where(lane == sub + (low + 8 * half), 1.0, 0.0), left))
            lines[8 * half : 8 * half + 8, :] = a[half]
        d = []
        for half in range(2):
            diagonal = c[half][8 * half]
            for j in range(8 * half + 1, 8 * half + 8):
                diagonal = jnp.where(sub == j % 8, c[half][j], diagonal)
            d.append(diagonal)
            spread[0, 8 * half : 8 * half + 8, :] = diagonal
        pivot = repeat(spread.at[0], 0)
        for j in range(STEP):
            scale = lax.rsqrt(pivot)
            first = j // 8
            line = repeat(lines, j) * scale
            for half in range(first, 2):
                c[half][j] = c[half][j] * scale
                solved[j, 8 * half : 8 * half + 8, :] = c[half][j]
                if j + 2 < STEP:
                    d[half] = d[half] - c[half][j] * c[half][j]
                    spread[j + 1, 8 * half : 8 * half + 8, :] = d[half]
            for k in range(j + 1, STEP):
                factor = repeat(solved.at[j], k)
                if k == j + 1:
                    pivot = repeat(spread.at[j], k) - factor * factor
                for half in range(k // 8, 2):
                    c[half][k] = c[half][k] - c[half][j] * factor
            for half in range(first, 2):
                update = a[half] - c[half][j] * line
                if half == first:
                    update = jnp.where(sub > j % 8, update, jnp.where(sub == j % 8, line, a[half]))
                a[half] = update
                lines[8 * half : 8 * half + 8, :] = update
        for half in range(2):
            work[low + 8 * half : low + 8 * half + 8, :] = a[half]
        if high < BASE:
            w0, w1, w2 = split3(jnp.concatenate(a, 0))
            product = dot_rows(
                jnp.concatenate([w0, w0, w1, w0, w1, w2], 0), jnp.concatenate([w0, w1, w0, w2, w1, w0], 0)
            )
            rest = lax.broadcasted_iota(jnp.int32, (BASE - high, BASE), 1)
            kept = jnp.where((rest >= low) & (rest < high), 0.0, work[high:, :])
            work[high:, :] = kept - product[high:, :]


def chain_kernel(
    info, u_ref, v_ref, wr_ref, wc_ref, vj_ref, wj_ref,
    f_ref, y_ref,
    state, side, work, spread, solved, lines, stack, tall,
):
    state[:, LEAD:] = jnp.zeros((LEAD + BASE, LEAD), F32)
    state[LEAD:, :LEAD] = jnp.zeros((BASE, LEAD), F32)
    side[LEAD:, :] = jnp.zeros((BASE, BASE), F32)
    lane = lax.broadcasted_iota(jnp.int32, (BASE, BASE), 1)
    row = lax.broadcasted_iota(jnp.int32, (BASE, BASE), 0)
    eye = (row == lane).astype(F32)
    geometry = (u_ref, v_ref, wr_ref, wc_ref)
    column = info[1]
    offset = pl.multiple_of(info[2], BASE)

    @pl.loop(0, TILE // 256)
    def _(chunk):
        start = pl.multiple_of(chunk * 256, 256)
        rows = pl.ds(start, 256)
        for tile in range(2):
            here = pl.ds(pl.multiple_of(tile * TILE + start, 256), 256)
            low = tile * TILE
            values = assemble(*geometry, tile, tile, start, 256, slice(256, TILE))
            line = start + lax.broadcasted_iota(jnp.int32, (256, 256), 0)
            across = 256 + lax.broadcasted_iota(jnp.int32, (256, 256), 1)
            values = values + jnp.where(line == across, wr_ref[tile, rows, 4:5], 0.0)
            state[here, low + 256 : low + TILE] = values
            side[here, :] = assemble(u_ref, vj_ref, wr_ref, wj_ref, tile, 0, start, 256, pl.ds(offset, BASE))
        state[rows, TILE : 2 * TILE] = assemble(*geometry, 0, 1, start, 256)

    for tile in range(2):
        values = assemble(*geometry, tile, tile, 0, 256, slice(0, 256))
        line = lax.broadcasted_iota(jnp.int32, (256, 256), 0)
        across = lax.broadcasted_iota(jnp.int32, (256, 256), 1)
        values = values + jnp.where(line == across, wr_ref[tile, 0:256, 4:5], 0.0)
        state[tile * TILE : tile * TILE + 256, tile * TILE : tile * TILE + 256] = values

    blocks = LEAD // BASE
    both = jnp.concatenate
    dot = functools.partial(jnp.dot, preferred_element_type=F32)

    @pl.loop(0, blocks)
    def _(k):
        here = pl.multiple_of(k * BASE, BASE)
        rows = pl.ds(here, BASE)
        state[rows, pl.ds(pl.multiple_of(LEAD + here, BASE), BASE)] = eye
        work[...] = state[rows, pl.ds(here, BASE)]
        eliminate_base(work, spread, solved, lines)
        l0, l1, l2 = split3(jnp.where(row >= lane, work[...], 0.0))
        window = pl.ds(here, WINDOW)

        def load(values):
            first, second, third = split3(values)
            stack[0:128, :] = first
            stack[128:256, :] = second
            stack[256:384, :] = third
            stack[384:512, :] = first

        load(both([state[rows, window], side[rows, :]], 1))
        two = dot(both([both([l0, l0], 1), both([l1, l1], 1)], 0), stack[0:256, :])
        done = two[:BASE] + (two[BASE:] + dot(both([l0, l2], 1), stack[256:512, :]))
        state[rows, window] = done[:, :WINDOW]
        side[rows, :] = done[:, WINDOW:]
        load(done)

        @pl.loop(0, blocks - 1 - k)
        def _(i):
            there = pl.multiple_of((i + 1) * BASE, BASE)
            first, second, third = split3(jnp.transpose(state[rows, pl.ds(pl.multiple_of(here + there, BASE), BASE)]))
            part = pl.ds(pl.multiple_of(i * BASE, BASE), BASE)
            tall[part, 0:128] = first
            tall[part, 128:256] = first
            tall[part, 256:384] = second
            tall[part, 384:512] = second
            tall[part, 512:640] = first
            tall[part, 640:768] = third

        @pl.loop(0, (blocks - k) // 2)
        def _(pair):
            part = pl.ds(pl.multiple_of(pair * 256, 256), 256)
            below = pl.ds(pl.multiple_of(here + BASE + pair * 256, BASE), 256)
            update = dot(tall[part, 0:256], stack[0:256, :])
            update += dot(tall[part, 256:512], stack[0:256, :])
            update += dot(tall[part, 512:768], stack[256:512, :])
            state[below, window] = state[below, window] - update[:, :WINDOW]
            side[below, :] = side[below, :] - update[:, WINDOW:]

    which = info[11]

    @pl.when((which == 0) | (which == 2) | (which == 3))
    def _():
        from_rows = pl.ds(pl.multiple_of(which % 2 * TILE, TILE), TILE)
        for chunk in range(TILE // BASE):
            from_cols = pl.ds(pl.multiple_of(which // 2 * TILE + chunk * BASE, BASE), BASE)
            values = jnp.transpose(state[from_rows, from_cols])
            line = chunk * BASE + lax.broadcasted_iota(jnp.int32, (BASE, TILE), 0)
            across = lax.broadcasted_iota(jnp.int32, (BASE, TILE), 1)
            keep = (line >= across) | (which == 2)
            f_ref[chunk * BASE : chunk * BASE + BASE, :] = jnp.where(keep, values, 0.0)

    @pl.when(column < 2)
    def _():
        line = lax.broadcasted_iota(jnp.int32, (LEAD, BASE), 0)
        across = lax.broadcasted_iota(jnp.int32, (LEAD, BASE), 1)
        side[:LEAD, :] = jnp.where(line == across + (column * TILE + offset), -1.0, 0.0)

    for out in range(4):
        total = jnp.zeros((256, BASE), F32)
        for part in range(out, 4):
            rows = slice(part * 256, part * 256 + 256)
            factor = jnp.transpose(state[rows, LEAD + out * 256 : LEAD + out * 256 + 256])
            high, low = split(factor)
            z_high, z_low = split(side[rows, :])
            wide = dot(high, both([z_high, z_low], 1))
            total = total + (wide[:, :BASE] + (wide[:, BASE:] + dot(low, z_high)))
        y_ref[out * 256 : out * 256 + 256, :] = total


def panel_kernel(base, info, u_ref, v_ref, wr_ref, wc_ref, *refs):
    ah_ref, al_ref = refs[-2:]
    slot, chunk = base + pl.program_id(0), pl.program_id(1)
    start = pl.multiple_of(chunk * CHUNK, CHUNK)
    kinds = [info[3 + slot * 2], info[4 + slot * 2]]
    needed = lambda kind: (kind != ZERO) & (kind != FACTOR)

    @pl.when(needed(kinds[0]) | needed(kinds[1]))
    def _():
        for half in range(2):
            values = assemble(u_ref, v_ref, wr_ref, wc_ref, 0, half, start, CHUNK)
            cols = slice(half * TILE, half * TILE + TILE)
            ah_ref[:, cols], al_ref[:, cols] = split(values)


CHUNK = 256
ZERO, UPDATE, DIAGONAL, PANEL, FACTOR = range(5)


def final_kernel(info, u_ref, v_ref, wr_ref, wc_ref, f_ref, *rest):
    parts, (ah, al, out_ref, yh, yl) = rest[:8], rest[8:]
    slot, chunk = pl.program_id(0), pl.program_id(1)
    start = pl.multiple_of(chunk * CHUNK, CHUNK)
    kinds = [info[3 + slot * 2], info[4 + slot * 2]]

    @pl.when((slot == 0) & (chunk == 0))
    def _():
        for p, part in enumerate(parts):
            source = info[12 + p]
            lanes = pl.ds(pl.multiple_of(source % 4 * 128, 128), 128)
            yh[source // 4, :, lanes], yl[source // 4, :, lanes] = split(part[...])

    def store(j, values):
        for q in range(TILE // 128):
            out_ref[pl.ds(j * 4 + q, CHUNK, stride=8), :] = values[:, q * 128 : (q + 1) * 128]

    for j in range(2):
        kind = kinds[j]

        @pl.when(kind == ZERO)
        def _():
            store(j, jnp.zeros((CHUNK, TILE), F32))

        @pl.when(kind == PANEL)
        def _():
            store(j, -dot3(ah[...], al[...], yh[j], yl[j]))

        @pl.when((kind == UPDATE) | (kind == DIAGONAL))
        def _():
            values = assemble(u_ref, v_ref, wr_ref, wc_ref, 0, j, start, CHUNK)
            row = start + lax.broadcasted_iota(jnp.int32, (CHUNK, TILE), 0)
            col = lax.broadcasted_iota(jnp.int32, (CHUNK, TILE), 1)
            shift = wr_ref[0, pl.ds(start, CHUNK), 4:5]
            values = values + jnp.where((row == col) & (kind == DIAGONAL), shift, 0.0)
            store(j, values - dot3(ah[...], al[...], yh[j], yl[j]))

        if j == 0:
            @pl.when(kind == FACTOR)
            def _():
                store(j, f_ref[pl.ds(start, CHUNK), :])


def whole(count):
    return [pl.BlockSpec(memory_space=pltpu.VMEM)] * count


def shards(points, weights, shift, cluster_rank):
    rows, cols = lax.axis_size("row"), lax.axis_size("col")
    row, col = lax.axis_index("row"), lax.axis_index("col")
    width = shift.shape[0]
    fill = jnp.zeros((7, width), F32)
    shard = jnp.concatenate([points.reshape(12, width), weights, shift[None], fill], 0)
    gathered = gather_shards(shard)

    slots = jnp.arange(4, dtype=jnp.int32)
    tile_rows = row + rows * slots
    tile_cols = col + cols * slots[:2]
    wanted = jnp.concatenate([slots[:2], tile_rows, tile_cols])
    clusters = jnp.arange(cluster_rank.shape[0], dtype=jnp.int32)
    found = jnp.sum(jnp.where(cluster_rank[None, :] == wanted[:, None], clusters[None, :], 0), axis=1)
    from_row, from_x = found // 4, found % 4
    dy = (row // 2 - from_row // 2) % 4
    dc = (row % 2 - from_row % 2) % 2
    dx = (col // 4 - from_x) % 4
    dz = (col % 4 - slots) % 4
    where = ((((dc * 4 + dy) * 4 + dx) * 4)[:, None] + dz[None, :]).reshape(-1).astype(jnp.int32)

    part = lambda z: pl.BlockSpec((None, 24, width), lambda t, at: (at[4 * t + z], 0, 0))
    u, v, wr, wc = pl.pallas_call(
        prep_kernel,
        grid_spec=pltpu.PrefetchScalarGridSpec(
            num_scalar_prefetch=1,
            grid=(8,),
            in_specs=[part(z) for z in range(4)],
            out_specs=[
                pl.BlockSpec((None, QUAD, TILE, FEAT), lambda t, at: (t, 0, 0, 0)),
                pl.BlockSpec((None, QUAD, FEAT, TILE), lambda t, at: (t, 0, 0, 0)),
                pl.BlockSpec((None, TILE, 128), lambda t, at: (t, 0, 0)),
                pl.BlockSpec((None, 8, TILE), lambda t, at: (t, 0, 0)),
            ],
            scratch_shapes=[pltpu.VMEM((128, TILE), F32)],
        ),
        out_shape=[
            jax.ShapeDtypeStruct((8, QUAD, TILE, FEAT), BF16),
            jax.ShapeDtypeStruct((8, QUAD, FEAT, TILE), BF16),
            jax.ShapeDtypeStruct((8, TILE, 128), F32),
            jax.ShapeDtypeStruct((8, 8, TILE), F32),
        ],
        name="prep",
    )(where, *[gathered] * 4)

    block_rows, block_cols = tile_rows[:, None], tile_cols[None, :]
    kinds = jnp.where(
        block_rows < block_cols,
        ZERO,
        jnp.where(
            block_cols >= 2,
            jnp.where(block_rows == block_cols, DIAGONAL, UPDATE),
            jnp.where(block_rows < 2, FACTOR, PANEL),
        ),
    )
    mine = row // 4
    order = jnp.arange(8, dtype=jnp.int32)
    sources = (row // 2 - order % 4) % 4 * 2 + (row % 2 - order // 4) % 2
    head = jnp.stack([mine, col + cols * mine, row % 4 * BASE])
    info = jnp.concatenate([head, kinds.reshape(-1), jnp.where((row < 2) & (col < 2), row * 2 + col, 1)[None], sources]).astype(jnp.int32)

    def geometry(left, right, held):
        return [
            pl.BlockSpec((held, QUAD, TILE, FEAT), lambda *at: (left(*at), 0, 0, 0)),
            pl.BlockSpec((2, QUAD, FEAT, TILE), lambda *at: (right, 0, 0, 0)),
            pl.BlockSpec((held, TILE, 128), lambda *at: (left(*at), 0, 0)),
            pl.BlockSpec((2, 8, TILE), lambda *at: (right, 0, 0)),
        ]

    factor, weights_part = pl.pallas_call(
        chain_kernel,
        grid_spec=pltpu.PrefetchScalarGridSpec(
            num_scalar_prefetch=1,
            grid=(1,),
            in_specs=geometry(lambda *at: 0, 0, 2)
            + [
                pl.BlockSpec((1, QUAD, FEAT, TILE), lambda i, info: (6 + info[0], 0, 0, 0)),
                pl.BlockSpec((1, 8, TILE), lambda i, info: (6 + info[0], 0, 0)),
            ],
            out_specs=[
                pl.BlockSpec((TILE, TILE), lambda i, info: (0, 0)),
                pl.BlockSpec((LEAD, BASE), lambda i, info: (0, 0)),
            ],
            scratch_shapes=[
                pltpu.VMEM((LEAD + BASE, 2 * LEAD), F32),
                pltpu.VMEM((LEAD + BASE, BASE), F32),
                pltpu.VMEM((BASE, BASE), F32),
                pltpu.VMEM((STEP, STEP, BASE), F32),
                pltpu.VMEM((STEP, STEP, BASE), F32),
                pltpu.VMEM((STEP, BASE), F32),
                pltpu.VMEM((4 * BASE, WINDOW + BASE), BF16),
                pltpu.VMEM((LEAD, 6 * BASE), BF16),
            ],
        ),
        out_shape=[jax.ShapeDtypeStruct((TILE, TILE), F32), jax.ShapeDtypeStruct((LEAD, BASE), F32)],
        name="chain",
    )(info, u, v, wr, wc, v, wc)

    tall = jax.ShapeDtypeStruct((4 * TILE, LEAD), BF16)
    chunks = TILE // CHUNK

    def panel(base, count, held):
        blocked = pl.BlockSpec((CHUNK, LEAD), lambda i, h, info: ((base + i) * chunks + h, 0))
        return pl.pallas_call(
            functools.partial(panel_kernel, base),
            grid_spec=pltpu.PrefetchScalarGridSpec(
                num_scalar_prefetch=1,
                grid=(count, chunks),
                in_specs=geometry(lambda i, h, info: 2 + base + i, 0, 1)
                + [pl.BlockSpec(memory_space=pl.ANY)] * len(held),
                out_specs=[blocked] * 2,
            ),
            out_shape=[tall] * 2,
            input_output_aliases={5 + i: i for i in range(len(held))},
            cost_estimate=pl.CostEstimate(
                flops=count * 15_000_000_000, bytes_accessed=count * 4_000_000, transcendentals=count * 8_000_000
            ),
            name=f"panel{base}",
        )(info, u, v, wr, wc, *held)

    near = [send(weights_part, lambda y, c, x, z, k=k: (y + k, c, x, z), rows, cols) for k in range(1, 4)]
    *near, ah, al = lax.optimization_barrier((*near, *panel(0, 3, [])))
    parts = [weights_part] + near
    parts = parts + [send(part, lambda y, c, x, z: (y, c + 1, x, z), rows, cols) for part in parts]
    *parts, ah, al = lax.optimization_barrier((*parts, *panel(3, 1, [ah, al])))

    lines = CHUNK * 8
    out = pl.pallas_call(
        final_kernel,
        grid_spec=pltpu.PrefetchScalarGridSpec(
            num_scalar_prefetch=1,
            grid=(4, chunks),
            in_specs=geometry(lambda i, h, info: 2 + i, 3, 1)
            + whole(9)
            + [pl.BlockSpec((CHUNK, LEAD), lambda i, h, info: (i * chunks + h, 0))] * 2,
            out_specs=pl.BlockSpec((lines, 128), lambda i, h, info: (i * chunks + h, 0)),
            scratch_shapes=[pltpu.VMEM((2, LEAD, TILE), BF16)] * 2,
        ),
        out_shape=jax.ShapeDtypeStruct((4 * TILE * 8, 128), F32),
        name="final",
    )(info, u, v, wr, wc, factor, *parts, ah, al)
    return out.reshape(4, 1, TILE, 2, 1, TILE)


def solution(mesh):
    return jax.shard_map(
        shards,
        mesh=mesh,
        in_specs=(P(None, None, ("row", "col")), P(None, ("row", "col")), P(("row", "col")), P()),
        out_specs=P(None, "row", None, None, "col", None),
        check_vma=False,
    )
```

```python
import functools

import jax
import jax.numpy as jnp
from jax import lax
from jax.experimental import pallas as pl
from jax.experimental.pallas import tpu as pltpu
from jax.sharding import PartitionSpec as P

SOFTENING_SQUARED = 0.0004
F32 = jnp.float32
BF16 = jnp.bfloat16
QUAD = 4
TILE = 512
FEAT = 48
LEAD = 1024
BASE = 128
STEP = 32
HALVES = STEP // 8
WINDOW = LEAD + BASE
HIGHEST = lax.Precision.HIGHEST


def split(value):
    high = value.astype(BF16)
    return high, (value - high.astype(F32)).astype(BF16)


def dot3(a_high, a_low, b_high, b_low):
    dot = functools.partial(jnp.dot, preferred_element_type=F32)
    return dot(a_high, b_high) + (dot(a_high, b_low) + dot(a_low, b_high))


def send(value, move, rows, cols):
    ys, xs = rows // 2, 4
    zs = cols // xs
    pairs = []
    for source in range(rows * cols):
        row, col = divmod(source, cols)
        y, core, x, z = move(row // 2, row % 2, col // zs, col % zs)
        pairs.append((source, ((y % ys) * 2 + core % 2) * cols + (x % xs) * zs + z % zs))
    return lax.ppermute(value, ("row", "col"), pairs)


def gather_shards(shard):
    rows, cols = lax.axis_size("row"), lax.axis_size("col")
    held = shard[None]
    for axis in (3, 2, 0):
        moved = [held]
        for k in range(1, 4):
            move = lambda *at, k=k: [part + k * (i == axis) for i, part in enumerate(at)]
            moved.append(send(held, move, rows, cols))
        held = jnp.concatenate(moved, 0)
    return jnp.concatenate([held, send(held, lambda y, c, x, z: (y, c + 1, x, z), rows, cols)], 0)


def prep_kernel(where_ref, g_ref, u_ref, v_ref, wr_ref, wc_ref, pad):
    tile = pl.program_id(0)
    geometry = jnp.concatenate([g_ref[where_ref[4 * tile + z], :, 0, :] for z in range(4)], axis=1)
    centred = geometry[0:12] - 0.5
    coarse = jnp.floor(centred * 256.0 + 0.5) * (1.0 / 256.0)
    fine = centred - coarse
    fine_high = fine.astype(BF16).astype(F32)
    fine_low = fine - fine_high
    per = lambda value: [value[4 * c : 4 * c + 4] for c in range(3)]
    coarse, fine, fine_high, fine_low = per(coarse), per(fine), per(fine_high), per(fine_low)
    norm = sum(c * c for c in coarse)
    norm_high = jnp.floor(norm * 256.0) * (1.0 / 256.0)
    norm_low = norm - norm_high
    mixed = sum(2.0 * c * f + f * f for c, f in zip(coarse, fine))

    def pieces(value):
        first = value.astype(BF16).astype(F32)
        second = (value - first).astype(BF16).astype(F32)
        return [first, second, value - first - second]

    one = jnp.ones_like(norm)
    twice = lambda values: [-2.0 * value for value in values]
    left = twice(coarse) + [norm_high, norm_low, one, one]
    left += twice(coarse) + twice(coarse) + twice(fine_high) + twice(fine_low)
    left += twice(fine_high) + twice(fine_high) + twice(fine_low)
    left += pieces(mixed) + [one] * 3
    right = coarse + [one, one, norm_high, norm_low]
    right += fine_high + fine_low + coarse + coarse
    right += fine_high + fine_low + fine_high
    right += [one] * 3 + pieces(mixed + SOFTENING_SQUARED)
    pad[...] = jnp.zeros_like(pad)
    @pl.when(tile < 6)
    def _():
        for quad in range(QUAD):
            for k, value in enumerate(left):
                pad[k : k + 1, :] = value[quad : quad + 1, :]
            u_ref[quad] = jnp.transpose(pad[...])[:, :FEAT].astype(BF16)

    @pl.when((tile < 2) | (tile >= 6))
    def _():
        for quad in range(QUAD):
            for k, value in enumerate(right):
                pad[k : k + 1, :] = value[quad : quad + 1, :]
            v_ref[quad] = pad[0:FEAT, :].astype(BF16)

    pad[0:5, :] = geometry[12:17]
    wr_ref[...] = jnp.transpose(pad[...])
    wc_ref[0:5, :] = geometry[12:17]


def assemble(u_ref, v_ref, wr_ref, wc_ref, left, right, start, count, cols=slice(0, TILE)):
    rows = pl.ds(start, count)
    total = None
    for first in range(QUAD):
        part = None
        for second in range(QUAD):
            squared = jnp.dot(u_ref[left, first, rows, :], v_ref[right, second, :, cols], preferred_element_type=F32)
            term = lax.rsqrt(squared) * wc_ref[right, second : second + 1, cols]
            part = term if part is None else part + term
        part = part * wr_ref[left, rows, first : first + 1]
        total = part if total is None else total + part
    return total


def split3(value):
    first = value.astype(BF16)
    rest = value - first.astype(F32)
    second = rest.astype(BF16)
    return first, second, (rest - second.astype(F32)).astype(BF16)


def dot_rows(left, right):
    return lax.dot_general(left, right, (((0,), (0,)), ((), ())), preferred_element_type=F32)


def eliminate_base(work, spread, solved, lines):
    lane = lax.broadcasted_iota(jnp.int32, (8, BASE), 1)
    sub = lax.broadcasted_iota(jnp.int32, (8, BASE), 0)
    repeat = lambda ref, i: ref[pl.ds(i, 8, stride=0), :]
    for step in range(BASE // STEP):
        low = step * STEP
        high = low + STEP
        a, c = [], [[] for _ in range(HALVES)]
        for half in range(HALVES):
            left = work[low + 8 * half : low + 8 * half + 8, :]
            for j in range(STEP):
                column = jnp.broadcast_to(left[:, low + j : low + j + 1], (8, BASE))
                c[half].append(column)
            inside = (lane >= low) & (lane < high)
            a.append(jnp.where(inside, jnp.where(lane == sub + (low + 8 * half), 1.0, 0.0), left))
            lines[8 * half : 8 * half + 8, :] = a[half]
        d = []
        for half in range(HALVES):
            diagonal = c[half][8 * half]
            for j in range(8 * half + 1, 8 * half + 8):
                diagonal = jnp.where(sub == j % 8, c[half][j], diagonal)
            d.append(diagonal)
            spread[0, 8 * half : 8 * half + 8, :] = diagonal
        pivot = repeat(spread.at[0], 0)
        for j in range(STEP):
            scale = lax.rsqrt(pivot)
            first = j // 8
            line = repeat(lines, j) * scale
            for half in range(first, HALVES):
                c[half][j] = c[half][j] * scale
                solved[j, 8 * half : 8 * half + 8, :] = c[half][j]
                if j + 2 < STEP:
                    d[half] = d[half] - c[half][j] * c[half][j]
                    spread[j + 1, 8 * half : 8 * half + 8, :] = d[half]
            for k in range(j + 1, STEP):
                factor = repeat(solved.at[j], k)
                if k == j + 1:
                    pivot = repeat(spread.at[j], k) - factor * factor
                for half in range(k // 8, HALVES):
                    c[half][k] = c[half][k] - c[half][j] * factor
            for half in range(first, HALVES):
                update = a[half] - c[half][j] * line
                if half == first:
                    update = jnp.where(sub > j % 8, update, jnp.where(sub == j % 8, line, a[half]))
                a[half] = update
                lines[8 * half : 8 * half + 8, :] = update
        for half in range(HALVES):
            work[low + 8 * half : low + 8 * half + 8, :] = a[half]
        if high < BASE:
            w0, w1, w2 = split3(jnp.concatenate(a, 0))
            product = dot_rows(
                jnp.concatenate([w0, w0, w1, w0, w1, w2], 0), jnp.concatenate([w0, w1, w0, w2, w1, w0], 0)
            )
            rest = lax.broadcasted_iota(jnp.int32, (BASE - high, BASE), 1)
            kept = jnp.where((rest >= low) & (rest < high), 0.0, work[high:, :])
            work[high:, :] = kept - product[high:, :]


def chain_kernel(
    info, u_ref, v_ref, wr_ref, wc_ref, vj_ref, wj_ref,
    f_ref, y_ref,
    state, side, work, spread, solved, lines, stack, tall,
):
    state[:, LEAD:] = jnp.zeros((LEAD + BASE, LEAD), F32)
    state[LEAD:, :LEAD] = jnp.zeros((BASE, LEAD), F32)
    side[LEAD:, :] = jnp.zeros((BASE, BASE), F32)
    lane = lax.broadcasted_iota(jnp.int32, (BASE, BASE), 1)
    row = lax.broadcasted_iota(jnp.int32, (BASE, BASE), 0)
    eye = (row == lane).astype(F32)
    geometry = (u_ref, v_ref, wr_ref, wc_ref)
    column = info[1]
    offset = pl.multiple_of(info[2], BASE)

    @pl.loop(0, TILE // 256)
    def _(chunk):
        start = pl.multiple_of(chunk * 256, 256)
        rows = pl.ds(start, 256)
        for tile in range(2):
            here = pl.ds(pl.multiple_of(tile * TILE + start, 256), 256)
            low = tile * TILE
            values = assemble(*geometry, tile, tile, start, 256, slice(256, TILE))
            line = start + lax.broadcasted_iota(jnp.int32, (256, 256), 0)
            across = 256 + lax.broadcasted_iota(jnp.int32, (256, 256), 1)
            values = values + jnp.where(line == across, wr_ref[tile, rows, 4:5], 0.0)
            state[here, low + 256 : low + TILE] = values
            side[here, :] = assemble(u_ref, vj_ref, wr_ref, wj_ref, tile, 0, start, 256, pl.ds(offset, BASE))
        state[rows, TILE : 2 * TILE] = assemble(*geometry, 0, 1, start, 256)

    for tile in range(2):
        values = assemble(*geometry, tile, tile, 0, 256, slice(0, 256))
        line = lax.broadcasted_iota(jnp.int32, (256, 256), 0)
        across = lax.broadcasted_iota(jnp.int32, (256, 256), 1)
        values = values + jnp.where(line == across, wr_ref[tile, 0:256, 4:5], 0.0)
        state[tile * TILE : tile * TILE + 256, tile * TILE : tile * TILE + 256] = values

    blocks = LEAD // BASE
    both = jnp.concatenate
    dot = functools.partial(jnp.dot, preferred_element_type=F32)

    @pl.loop(0, blocks)
    def _(k):
        here = pl.multiple_of(k * BASE, BASE)
        rows = pl.ds(here, BASE)
        state[rows, pl.ds(pl.multiple_of(LEAD + here, BASE), BASE)] = eye
        work[...] = state[rows, pl.ds(here, BASE)]
        eliminate_base(work, spread, solved, lines)
        l0, l1, l2 = split3(jnp.where(row >= lane, work[...], 0.0))
        window = pl.ds(here, WINDOW)

        def load(values):
            first, second, third = split3(values)
            stack[0:128, :] = first
            stack[128:256, :] = second
            stack[256:384, :] = third
            stack[384:512, :] = first

        load(both([state[rows, window], side[rows, :]], 1))
        two = dot(both([both([l0, l0], 1), both([l1, l1], 1)], 0), stack[0:256, :])
        done = two[:BASE] + (two[BASE:] + dot(both([l0, l2], 1), stack[256:512, :]))
        state[rows, window] = done[:, :WINDOW]
        side[rows, :] = done[:, WINDOW:]
        load(done)

        @pl.loop(0, blocks - 1 - k)
        def _(i):
            there = pl.multiple_of((i + 1) * BASE, BASE)
            parts = split3(jnp.transpose(state[rows, pl.ds(pl.multiple_of(here + there, BASE), BASE)]))
            for n, part in enumerate(parts):
                tall[pl.ds(pl.multiple_of(i * BASE, BASE), BASE), n * 128 : n * 128 + 128] = part

        for pair in range(blocks // 2):
            @pl.when(pair < (blocks - k) // 2)
            def _():
                skip = pair * 256
                below = pl.ds(pl.multiple_of(here + BASE + skip, BASE), 256)
                t0, t1, t2 = [tall[skip : skip + 256, n * 128 : n * 128 + 128] for n in range(3)]
                update = dot(both([t0, t0], 1), stack[0:256, skip:])
                update += dot(both([t1, t1], 1), stack[0:256, skip:])
                update += dot(both([t0, t2], 1), stack[256:512, skip:])
                width = WINDOW - skip
                into = pl.ds(pl.multiple_of(here + skip, BASE), width)
                state[below, into] = state[below, into] - update[:, :width]
                side[below, :] = side[below, :] - update[:, width:]

    which = info[11]

    @pl.when((which == 0) | (which == 2) | (which == 3))
    def _():
        from_rows = pl.ds(pl.multiple_of(which % 2 * TILE, TILE), TILE)
        for chunk in range(TILE // BASE):
            from_cols = pl.ds(pl.multiple_of(which // 2 * TILE + chunk * BASE, BASE), BASE)
            values = jnp.transpose(state[from_rows, from_cols])
            line = chunk * BASE + lax.broadcasted_iota(jnp.int32, (BASE, TILE), 0)
            across = lax.broadcasted_iota(jnp.int32, (BASE, TILE), 1)
            keep = (line >= across) | (which == 2)
            f_ref[chunk * BASE : chunk * BASE + BASE, :] = jnp.where(keep, values, 0.0)

    @pl.when(column < 2)
    def _():
        line = lax.broadcasted_iota(jnp.int32, (LEAD, BASE), 0)
        across = lax.broadcasted_iota(jnp.int32, (LEAD, BASE), 1)
        side[:LEAD, :] = jnp.where(line == across + (column * TILE + offset), -1.0, 0.0)

    for out in range(4):
        total = jnp.zeros((256, BASE), F32)
        for part in range(out, 4):
            rows = slice(part * 256, part * 256 + 256)
            factor = jnp.transpose(state[rows, LEAD + out * 256 : LEAD + out * 256 + 256])
            high, low = split(factor)
            z_high, z_low = split(side[rows, :])
            wide = dot(high, both([z_high, z_low], 1))
            total = total + (wide[:, :BASE] + (wide[:, BASE:] + dot(low, z_high)))
        y_ref[out * 256 : out * 256 + 256, :] = total


def panel_kernel(base, info, u_ref, v_ref, wr_ref, wc_ref, *refs):
    ah_ref, al_ref = refs[-2:]
    slot, chunk = base + pl.program_id(0), pl.program_id(1)
    start = pl.multiple_of(chunk * CHUNK, CHUNK)
    kinds = [info[3 + slot * 2], info[4 + slot * 2]]
    needed = lambda kind: (kind != ZERO) & (kind != FACTOR)

    @pl.when(needed(kinds[0]) | needed(kinds[1]))
    def _():
        for half in range(2):
            values = assemble(u_ref, v_ref, wr_ref, wc_ref, 0, half, start, CHUNK)
            cols = slice(half * TILE, half * TILE + TILE)
            ah_ref[:, cols], al_ref[:, cols] = split(values)


CHUNK = 256
ZERO, UPDATE, DIAGONAL, PANEL, FACTOR = range(5)


def final_kernel(info, u_ref, v_ref, wr_ref, wc_ref, f_ref, *rest):
    parts, (ah, al, out_ref, yh, yl) = rest[:8], rest[8:]
    slot, chunk = pl.program_id(0), pl.program_id(1)
    start = pl.multiple_of(chunk * CHUNK, CHUNK)
    kinds = [info[3 + slot * 2], info[4 + slot * 2]]

    @pl.when((slot == 0) & (chunk == 0))
    def _():
        for p, part in enumerate(parts):
            source = info[12 + p]
            lanes = pl.ds(pl.multiple_of(source % 4 * 128, 128), 128)
            yh[source // 4, :, lanes], yl[source // 4, :, lanes] = split(part[...])

    def store(j, values):
        for q in range(TILE // 128):
            out_ref[pl.ds(j * 4 + q, CHUNK, stride=8), :] = values[:, q * 128 : (q + 1) * 128]

    for j in range(2):
        kind = kinds[j]

        @pl.when(kind == ZERO)
        def _():
            store(j, jnp.zeros((CHUNK, TILE), F32))

        @pl.when(kind == PANEL)
        def _():
            store(j, -dot3(ah[...], al[...], yh[j], yl[j]))

        @pl.when((kind == UPDATE) | (kind == DIAGONAL))
        def _():
            values = assemble(u_ref, v_ref, wr_ref, wc_ref, 0, j, start, CHUNK)
            row = start + lax.broadcasted_iota(jnp.int32, (CHUNK, TILE), 0)
            col = lax.broadcasted_iota(jnp.int32, (CHUNK, TILE), 1)
            shift = wr_ref[0, pl.ds(start, CHUNK), 4:5]
            values = values + jnp.where((row == col) & (kind == DIAGONAL), shift, 0.0)
            store(j, values - dot3(ah[...], al[...], yh[j], yl[j]))

        if j == 0:
            @pl.when(kind == FACTOR)
            def _():
                store(j, f_ref[pl.ds(start, CHUNK), :])


def whole(count):
    return [pl.BlockSpec(memory_space=pltpu.VMEM)] * count


def shards(points, weights, shift, cluster_rank):
    rows, cols = lax.axis_size("row"), lax.axis_size("col")
    row, col = lax.axis_index("row"), lax.axis_index("col")
    width = shift.shape[0]
    shard = jnp.concatenate([points.reshape(12, width), weights, shift[None]], 0)[:, None]
    gathered = gather_shards(shard)

    slots = jnp.arange(4, dtype=jnp.int32)
    tile_rows = row + rows * slots
    tile_cols = col + cols * slots[:2]
    wanted = jnp.concatenate([slots[:2], tile_rows, tile_cols])
    clusters = jnp.arange(cluster_rank.shape[0], dtype=jnp.int32)
    found = jnp.sum(jnp.where(cluster_rank[None, :] == wanted[:, None], clusters[None, :], 0), axis=1)
    from_row, from_x = found // 4, found % 4
    dy = (row // 2 - from_row // 2) % 4
    dc = (row % 2 - from_row % 2) % 2
    dx = (col // 4 - from_x) % 4
    dz = (col % 4 - slots) % 4
    where = ((((dc * 4 + dy) * 4 + dx) * 4)[:, None] + dz[None, :]).reshape(-1).astype(jnp.int32)

    u, v, wr, wc = pl.pallas_call(
        prep_kernel,
        grid_spec=pltpu.PrefetchScalarGridSpec(
            num_scalar_prefetch=1,
            grid=(8,),
            in_specs=whole(1),
            out_specs=[
                pl.BlockSpec((None, QUAD, TILE, FEAT), lambda t, at: (t, 0, 0, 0)),
                pl.BlockSpec((None, QUAD, FEAT, TILE), lambda t, at: (t, 0, 0, 0)),
                pl.BlockSpec((None, TILE, 128), lambda t, at: (t, 0, 0)),
                pl.BlockSpec((None, 8, TILE), lambda t, at: (t, 0, 0)),
            ],
            scratch_shapes=[pltpu.VMEM((128, TILE), F32)],
        ),
        out_shape=[
            jax.ShapeDtypeStruct((8, QUAD, TILE, FEAT), BF16),
            jax.ShapeDtypeStruct((8, QUAD, FEAT, TILE), BF16),
            jax.ShapeDtypeStruct((8, TILE, 128), F32),
            jax.ShapeDtypeStruct((8, 8, TILE), F32),
        ],
        name="prep",
        compiler_params=pltpu.CompilerParams(vmem_limit_bytes=16 << 20),
    )(where, gathered)

    block_rows, block_cols = tile_rows[:, None], tile_cols[None, :]
    kinds = jnp.where(
        block_rows < block_cols,
        ZERO,
        jnp.where(
            block_cols >= 2,
            jnp.where(block_rows == block_cols, DIAGONAL, UPDATE),
            jnp.where(block_rows < 2, FACTOR, PANEL),
        ),
    )
    mine = row // 4
    order = jnp.arange(8, dtype=jnp.int32)
    sources = (row // 2 - order % 4) % 4 * 2 + (row % 2 - order // 4) % 2
    head = jnp.stack([mine, col + cols * mine, row % 4 * BASE])
    info = jnp.concatenate([head, kinds.reshape(-1), jnp.where((row < 2) & (col < 2), row * 2 + col, 1)[None], sources]).astype(jnp.int32)

    def geometry(left, right, held):
        return [
            pl.BlockSpec((held, QUAD, TILE, FEAT), lambda *at: (left(*at), 0, 0, 0)),
            pl.BlockSpec((2, QUAD, FEAT, TILE), lambda *at: (right, 0, 0, 0)),
            pl.BlockSpec((held, TILE, 128), lambda *at: (left(*at), 0, 0)),
            pl.BlockSpec((2, 8, TILE), lambda *at: (right, 0, 0)),
        ]

    factor, weights_part = pl.pallas_call(
        chain_kernel,
        grid_spec=pltpu.PrefetchScalarGridSpec(
            num_scalar_prefetch=1,
            grid=(1,),
            in_specs=geometry(lambda *at: 0, 0, 2)
            + [
                pl.BlockSpec((1, QUAD, FEAT, TILE), lambda i, info: (6 + info[0], 0, 0, 0)),
                pl.BlockSpec((1, 8, TILE), lambda i, info: (6 + info[0], 0, 0)),
            ],
            out_specs=[
                pl.BlockSpec((TILE, TILE), lambda i, info: (0, 0)),
                pl.BlockSpec((LEAD, BASE), lambda i, info: (0, 0)),
            ],
            scratch_shapes=[
                pltpu.VMEM((LEAD + BASE, 2 * LEAD), F32),
                pltpu.VMEM((LEAD + BASE, BASE), F32),
                pltpu.VMEM((BASE, BASE), F32),
                pltpu.VMEM((STEP, STEP, BASE), F32),
                pltpu.VMEM((STEP, STEP, BASE), F32),
                pltpu.VMEM((STEP, BASE), F32),
                pltpu.VMEM((4 * BASE, WINDOW + BASE), BF16),
                pltpu.VMEM((LEAD, 3 * BASE), BF16),
            ],
        ),
        out_shape=[jax.ShapeDtypeStruct((TILE, TILE), F32), jax.ShapeDtypeStruct((LEAD, BASE), F32)],
        name="chain",
        compiler_params=pltpu.CompilerParams(vmem_limit_bytes=36 << 20),
    )(info, u, v, wr, wc, v, wc)

    tall = jax.ShapeDtypeStruct((4 * TILE, LEAD), BF16)
    chunks = TILE // CHUNK

    def panel(base, count, held):
        blocked = pl.BlockSpec((CHUNK, LEAD), lambda i, h, info: ((base + i) * chunks + h, 0))
        return pl.pallas_call(
            functools.partial(panel_kernel, base),
            grid_spec=pltpu.PrefetchScalarGridSpec(
                num_scalar_prefetch=1,
                grid=(count, chunks),
                in_specs=geometry(lambda i, h, info: 2 + base + i, 0, 1)
                + [pl.BlockSpec(memory_space=pl.ANY)] * len(held),
                out_specs=[blocked] * 2,
            ),
            out_shape=[tall] * 2,
            input_output_aliases={5 + i: i for i in range(len(held))},
            cost_estimate=pl.CostEstimate(
                flops=count * 15_000_000_000, bytes_accessed=count * 4_000_000, transcendentals=count * 8_000_000
            ),
            name=f"panel{base}",
            compiler_params=pltpu.CompilerParams(vmem_limit_bytes=20 << 20),
        )(info, u, v, wr, wc, *held)

    near = [send(weights_part, lambda y, c, x, z, k=k: (y + k, c, x, z), rows, cols) for k in range(1, 4)]
    *near, ah, al = lax.optimization_barrier((*near, *panel(0, 3, [])))
    parts = [weights_part] + near
    parts = parts + [send(part, lambda y, c, x, z: (y, c + 1, x, z), rows, cols) for part in parts]
    *parts, ah, al = lax.optimization_barrier((*parts, *panel(3, 1, [ah, al])))

    lines = CHUNK * 8
    out = pl.pallas_call(
        final_kernel,
        grid_spec=pltpu.PrefetchScalarGridSpec(
            num_scalar_prefetch=1,
            grid=(4, chunks),
            in_specs=geometry(lambda i, h, info: 2 + i, 3, 1)
            + whole(9)
            + [pl.BlockSpec((CHUNK, LEAD), lambda i, h, info: (i * chunks + h, 0))] * 2,
            out_specs=pl.BlockSpec((lines, 128), lambda i, h, info: (i * chunks + h, 0)),
            scratch_shapes=[pltpu.VMEM((2, LEAD, TILE), BF16)] * 2,
        ),
        out_shape=jax.ShapeDtypeStruct((4 * TILE * 8, 128), F32),
        name="final",
        compiler_params=pltpu.CompilerParams(vmem_limit_bytes=24 << 20),
    )(info, u, v, wr, wc, factor, *parts, ah, al)
    return out.reshape(4, 1, TILE, 2, 1, TILE)


def solution(mesh):
    return jax.shard_map(
        shards,
        mesh=mesh,
        in_specs=(P(None, None, ("row", "col")), P(None, ("row", "col")), P(("row", "col")), P()),
        out_specs=P(None, "row", None, None, "col", None),
        check_vma=False,
    )
```

```python
import functools

import jax
import jax.numpy as jnp
from jax import lax
from jax.experimental import pallas as pl
from jax.experimental.pallas import tpu as pltpu
from jax.sharding import PartitionSpec as P

SOFTENING_SQUARED = 0.0004
F32 = jnp.float32
BF16 = jnp.bfloat16
QUAD = 4
TILE = 512
FEAT = 48
LEAD = 1024
BASE = 128
STEP = 32
HALVES = STEP // 8
WINDOW = LEAD + BASE
HIGHEST = lax.Precision.HIGHEST


def split(value):
    high = value.astype(BF16)
    return high, (value - high.astype(F32)).astype(BF16)


def dot3(a_high, a_low, b_high, b_low):
    dot = functools.partial(jnp.dot, preferred_element_type=F32)
    return dot(a_high, b_high) + (dot(a_high, b_low) + dot(a_low, b_high))


def send(value, move, rows, cols):
    ys, xs = rows // 2, 4
    zs = cols // xs
    pairs = []
    for source in range(rows * cols):
        row, col = divmod(source, cols)
        y, core, x, z = move(row // 2, row % 2, col // zs, col % zs)
        pairs.append((source, ((y % ys) * 2 + core % 2) * cols + (x % xs) * zs + z % zs))
    return lax.ppermute(value, ("row", "col"), pairs)


def gather_shards(shard):
    rows, cols = lax.axis_size("row"), lax.axis_size("col")
    held = shard[None]
    for axis in (3, 0):
        for bit in (1, 2):
            move = lambda *at: [part ^ (bit * (i == axis)) for i, part in enumerate(at)]
            held = jnp.concatenate([held, send(held, move, rows, cols)], 0)
    moved = [held] + [send(held, lambda y, c, x, z, k=k: (y, c, x + k, z), rows, cols) for k in range(1, 4)]
    held = jnp.concatenate(moved, 0)
    return jnp.concatenate([held, send(held, lambda y, c, x, z: (y, c + 1, x, z), rows, cols)], 0)


def prep_kernel(where_ref, g_ref, u_ref, v_ref, wr_ref, wc_ref, pad):
    tile = pl.program_id(0)
    geometry = jnp.concatenate([g_ref[where_ref[4 * tile + z], :, 0, :] for z in range(4)], axis=1)
    centred = geometry[0:12] - 0.5
    coarse = jnp.floor(centred * 256.0 + 0.5) * (1.0 / 256.0)
    fine = centred - coarse
    fine_high = fine.astype(BF16).astype(F32)
    fine_low = fine - fine_high
    per = lambda value: [value[4 * c : 4 * c + 4] for c in range(3)]
    coarse, fine, fine_high, fine_low = per(coarse), per(fine), per(fine_high), per(fine_low)
    norm = sum(c * c for c in coarse)
    norm_high = jnp.floor(norm * 256.0) * (1.0 / 256.0)
    norm_low = norm - norm_high
    mixed = sum(2.0 * c * f + f * f for c, f in zip(coarse, fine))

    def pieces(value):
        first = value.astype(BF16).astype(F32)
        second = (value - first).astype(BF16).astype(F32)
        return [first, second, value - first - second]

    one = jnp.ones_like(norm)
    twice = lambda values: [-2.0 * value for value in values]
    left = twice(coarse) + [norm_high, norm_low, one, one]
    left += twice(coarse) + twice(coarse) + twice(fine_high) + twice(fine_low)
    left += twice(fine_high) + twice(fine_high) + twice(fine_low)
    left += pieces(mixed) + [one] * 3
    right = coarse + [one, one, norm_high, norm_low]
    right += fine_high + fine_low + coarse + coarse
    right += fine_high + fine_low + fine_high
    right += [one] * 3 + pieces(mixed + SOFTENING_SQUARED)
    pad[...] = jnp.zeros_like(pad)
    @pl.when(tile < 6)
    def _():
        for quad in range(QUAD):
            for k, value in enumerate(left):
                pad[k : k + 1, :] = value[quad : quad + 1, :]
            u_ref[quad] = jnp.transpose(pad[...])[:, :FEAT].astype(BF16)

    @pl.when((tile < 2) | (tile >= 6))
    def _():
        for quad in range(QUAD):
            for k, value in enumerate(right):
                pad[k : k + 1, :] = value[quad : quad + 1, :]
            v_ref[quad] = pad[0:FEAT, :].astype(BF16)

    pad[0:5, :] = geometry[12:17]
    wr_ref[...] = jnp.transpose(pad[...])
    wc_ref[0:5, :] = geometry[12:17]


def assemble(u_ref, v_ref, wr_ref, wc_ref, left, right, start, count, cols=slice(0, TILE)):
    rows = pl.ds(start, count)
    total = None
    for first in range(QUAD):
        part = None
        for second in range(QUAD):
            squared = jnp.dot(u_ref[left, first, rows, :], v_ref[right, second, :, cols], preferred_element_type=F32)
            term = lax.rsqrt(squared) * wc_ref[right, second : second + 1, cols]
            part = term if part is None else part + term
        part = part * wr_ref[left, rows, first : first + 1]
        total = part if total is None else total + part
    return total


def split3(value):
    first = value.astype(BF16)
    rest = value - first.astype(F32)
    second = rest.astype(BF16)
    return first, second, (rest - second.astype(F32)).astype(BF16)


def dot_rows(left, right):
    return lax.dot_general(left, right, (((0,), (0,)), ((), ())), preferred_element_type=F32)


def eliminate_base(work, spread, solved, lines):
    lane = lax.broadcasted_iota(jnp.int32, (8, BASE), 1)
    sub = lax.broadcasted_iota(jnp.int32, (8, BASE), 0)
    repeat = lambda ref, i: ref[pl.ds(i, 8, stride=0), :]
    for step in range(BASE // STEP):
        low = step * STEP
        high = low + STEP
        a, c = [], [[] for _ in range(HALVES)]
        for half in range(HALVES):
            left = work[low + 8 * half : low + 8 * half + 8, :]
            for j in range(STEP):
                column = jnp.broadcast_to(left[:, low + j : low + j + 1], (8, BASE))
                c[half].append(column)
            inside = (lane >= low) & (lane < high)
            a.append(jnp.where(inside, jnp.where(lane == sub + (low + 8 * half), 1.0, 0.0), left))
            lines[8 * half : 8 * half + 8, :] = a[half]
        d = []
        for half in range(HALVES):
            diagonal = c[half][8 * half]
            for j in range(8 * half + 1, 8 * half + 8):
                diagonal = jnp.where(sub == j % 8, c[half][j], diagonal)
            d.append(diagonal)
            spread[0, 8 * half : 8 * half + 8, :] = diagonal
        pivot = repeat(spread.at[0], 0)
        for j in range(STEP):
            scale = lax.rsqrt(pivot)
            first = j // 8
            line = repeat(lines, j) * scale
            for half in range(first, HALVES):
                c[half][j] = c[half][j] * scale
                solved[j, 8 * half : 8 * half + 8, :] = c[half][j]
                if j + 2 < STEP:
                    d[half] = d[half] - c[half][j] * c[half][j]
                    spread[j + 1, 8 * half : 8 * half + 8, :] = d[half]
            for k in range(j + 1, STEP):
                factor = repeat(solved.at[j], k)
                if k == j + 1:
                    pivot = repeat(spread.at[j], k) - factor * factor
                for half in range(k // 8, HALVES):
                    c[half][k] = c[half][k] - c[half][j] * factor
            for half in range(first, HALVES):
                update = a[half] - c[half][j] * line
                if half == first:
                    update = jnp.where(sub > j % 8, update, jnp.where(sub == j % 8, line, a[half]))
                a[half] = update
                lines[8 * half : 8 * half + 8, :] = update
        for half in range(HALVES):
            work[low + 8 * half : low + 8 * half + 8, :] = a[half]
        if high < BASE:
            w0, w1, w2 = split3(jnp.concatenate(a, 0))
            product = dot_rows(
                jnp.concatenate([w0, w0, w1, w0, w1, w2], 0), jnp.concatenate([w0, w1, w0, w2, w1, w0], 0)
            )
            rest = lax.broadcasted_iota(jnp.int32, (BASE - high, BASE), 1)
            kept = jnp.where((rest >= low) & (rest < high), 0.0, work[high:, :])
            work[high:, :] = kept - product[high:, :]


def chain_kernel(
    info, u_ref, v_ref, wr_ref, wc_ref, vj_ref, wj_ref,
    f_ref, y_ref,
    state, side, work, spread, solved, lines, stack, tall,
):
    state[:, LEAD:] = jnp.zeros((LEAD + BASE, LEAD), F32)
    state[LEAD:, :LEAD] = jnp.zeros((BASE, LEAD), F32)
    side[LEAD:, :] = jnp.zeros((BASE, BASE), F32)
    lane = lax.broadcasted_iota(jnp.int32, (BASE, BASE), 1)
    row = lax.broadcasted_iota(jnp.int32, (BASE, BASE), 0)
    eye = (row == lane).astype(F32)
    geometry = (u_ref, v_ref, wr_ref, wc_ref)
    column = info[1]
    offset = pl.multiple_of(info[2], BASE)

    @pl.loop(0, TILE // 256)
    def _(chunk):
        start = pl.multiple_of(chunk * 256, 256)
        rows = pl.ds(start, 256)
        for tile in range(2):
            here = pl.ds(pl.multiple_of(tile * TILE + start, 256), 256)
            low = tile * TILE
            values = assemble(*geometry, tile, tile, start, 256, slice(256, TILE))
            line = start + lax.broadcasted_iota(jnp.int32, (256, 256), 0)
            across = 256 + lax.broadcasted_iota(jnp.int32, (256, 256), 1)
            values = values + jnp.where(line == across, wr_ref[tile, rows, 4:5], 0.0)
            state[here, low + 256 : low + TILE] = values
            side[here, :] = assemble(u_ref, vj_ref, wr_ref, wj_ref, tile, 0, start, 256, pl.ds(offset, BASE))
        state[rows, TILE : 2 * TILE] = assemble(*geometry, 0, 1, start, 256)

    for tile in range(2):
        values = assemble(*geometry, tile, tile, 0, 256, slice(0, 256))
        line = lax.broadcasted_iota(jnp.int32, (256, 256), 0)
        across = lax.broadcasted_iota(jnp.int32, (256, 256), 1)
        values = values + jnp.where(line == across, wr_ref[tile, 0:256, 4:5], 0.0)
        state[tile * TILE : tile * TILE + 256, tile * TILE : tile * TILE + 256] = values

    blocks = LEAD // BASE
    both = jnp.concatenate
    dot = functools.partial(jnp.dot, preferred_element_type=F32)

    @pl.loop(0, blocks)
    def _(k):
        here = pl.multiple_of(k * BASE, BASE)
        rows = pl.ds(here, BASE)
        state[rows, pl.ds(pl.multiple_of(LEAD + here, BASE), BASE)] = eye
        work[...] = state[rows, pl.ds(here, BASE)]
        eliminate_base(work, spread, solved, lines)
        l0, l1 = split(jnp.where(row >= lane, work[...], 0.0))
        window = pl.ds(here, WINDOW)

        def load(values):
            first, second = split(values)
            stack[0:128, :] = first
            stack[128:256, :] = second

        load(both([state[rows, window], side[rows, :]], 1))
        done = dot(both([l0, l0], 1), stack[...]) + dot(l1, stack[0:128, :])
        state[rows, window] = done[:, :WINDOW]
        side[rows, :] = done[:, WINDOW:]
        load(done)

        @pl.loop(0, blocks - 1 - k)
        def _(i):
            there = pl.multiple_of((i + 1) * BASE, BASE)
            parts = split(jnp.transpose(state[rows, pl.ds(pl.multiple_of(here + there, BASE), BASE)]))
            for n, part in enumerate(parts):
                tall[pl.ds(pl.multiple_of(i * BASE, BASE), BASE), n * 128 : n * 128 + 128] = part

        for pair in range(blocks // 2):
            @pl.when(pair < (blocks - k) // 2)
            def _():
                skip = pair * 256
                below = pl.ds(pl.multiple_of(here + BASE + skip, BASE), 256)
                t0, t1 = [tall[skip : skip + 256, n * 128 : n * 128 + 128] for n in range(2)]
                update = dot(both([t0, t0], 1), stack[:, skip:]) + dot(t1, stack[0:128, skip:])
                width = WINDOW - skip
                into = pl.ds(pl.multiple_of(here + skip, BASE), width)
                state[below, into] = state[below, into] - update[:, :width]
                side[below, :] = side[below, :] - update[:, width:]

    which = info[11]

    @pl.when((which == 0) | (which == 2) | (which == 3))
    def _():
        from_rows = pl.ds(pl.multiple_of(which % 2 * TILE, TILE), TILE)
        for chunk in range(TILE // BASE):
            from_cols = pl.ds(pl.multiple_of(which // 2 * TILE + chunk * BASE, BASE), BASE)
            values = jnp.transpose(state[from_rows, from_cols])
            line = chunk * BASE + lax.broadcasted_iota(jnp.int32, (BASE, TILE), 0)
            across = lax.broadcasted_iota(jnp.int32, (BASE, TILE), 1)
            keep = (line >= across) | (which == 2)
            f_ref[chunk * BASE : chunk * BASE + BASE, :] = jnp.where(keep, values, 0.0)

    @pl.when(column < 2)
    def _():
        line = lax.broadcasted_iota(jnp.int32, (LEAD, BASE), 0)
        across = lax.broadcasted_iota(jnp.int32, (LEAD, BASE), 1)
        side[:LEAD, :] = jnp.where(line == across + (column * TILE + offset), -1.0, 0.0)

    for out in range(4):
        total = jnp.zeros((256, BASE), F32)
        for part in range(out, 4):
            rows = slice(part * 256, part * 256 + 256)
            factor = jnp.transpose(state[rows, LEAD + out * 256 : LEAD + out * 256 + 256])
            high, low = split(factor)
            z_high, z_low = split(side[rows, :])
            wide = dot(high, both([z_high, z_low], 1))
            total = total + (wide[:, :BASE] + (wide[:, BASE:] + dot(low, z_high)))
        y_ref[out * 256 : out * 256 + 256, :] = total


def panel_kernel(info, u_ref, v_ref, wr_ref, wc_ref, ah_ref, al_ref):
    slot, chunk = pl.program_id(0), pl.program_id(1)
    start = pl.multiple_of(chunk * CHUNK, CHUNK)
    kinds = [info[3 + slot * 2], info[4 + slot * 2]]
    needed = lambda kind: (kind != ZERO) & (kind != FACTOR)

    @pl.when(needed(kinds[0]) | needed(kinds[1]))
    def _():
        for half in range(2):
            values = assemble(u_ref, v_ref, wr_ref, wc_ref, 0, half, start, CHUNK)
            cols = slice(half * TILE, half * TILE + TILE)
            ah_ref[:, cols], al_ref[:, cols] = split(values)


def own_kernel(info, u_ref, v_ref, wr_ref, wc_ref, own_ref):
    slot, chunk = pl.program_id(0), pl.program_id(1)
    start = pl.multiple_of(chunk * CHUNK, CHUNK)
    for j in range(2):
        kind = info[3 + slot * 2 + j]

        @pl.when((kind == UPDATE) | (kind == DIAGONAL))
        def _():
            values = assemble(u_ref, v_ref, wr_ref, wc_ref, 0, j, start, CHUNK)
            row = start + lax.broadcasted_iota(jnp.int32, (CHUNK, TILE), 0)
            col = lax.broadcasted_iota(jnp.int32, (CHUNK, TILE), 1)
            shift = wr_ref[0, pl.ds(start, CHUNK), 4:5]
            values = values + jnp.where((row == col) & (kind == DIAGONAL), shift, 0.0)
            own_ref[:, j * TILE : j * TILE + TILE] = values


CHUNK = 256
ZERO, UPDATE, DIAGONAL, PANEL, FACTOR = range(5)


def final_kernel(info, f_ref, *rest):
    parts, (ah, al, own, out_ref, yh, yl) = rest[:8], rest[8:]
    slot, chunk = pl.program_id(0), pl.program_id(1)
    start = pl.multiple_of(chunk * CHUNK, CHUNK)
    kinds = [info[3 + slot * 2], info[4 + slot * 2]]

    @pl.when((slot == 0) & (chunk == 0))
    def _():
        for p, part in enumerate(parts):
            source = info[12 + p]
            lanes = pl.ds(pl.multiple_of(source % 4 * 128, 128), 128)
            yh[source // 4, :, lanes], yl[source // 4, :, lanes] = split(part[...])

    def store(j, values):
        for q in range(TILE // 128):
            out_ref[pl.ds(j * 4 + q, CHUNK, stride=8), :] = values[:, q * 128 : (q + 1) * 128]

    for j in range(2):
        kind = kinds[j]

        @pl.when(kind == ZERO)
        def _():
            store(j, jnp.zeros((CHUNK, TILE), F32))

        @pl.when(kind == PANEL)
        def _():
            store(j, -dot3(ah[...], al[...], yh[j], yl[j]))

        @pl.when((kind == UPDATE) | (kind == DIAGONAL))
        def _():
            values = own[:, j * TILE : j * TILE + TILE]
            store(j, values - dot3(ah[...], al[...], yh[j], yl[j]))

        if j == 0:
            @pl.when(kind == FACTOR)
            def _():
                store(j, f_ref[pl.ds(start, CHUNK), :])


def whole(count):
    return [pl.BlockSpec(memory_space=pltpu.VMEM)] * count


def shards(points, weights, shift, cluster_rank):
    rows, cols = lax.axis_size("row"), lax.axis_size("col")
    row, col = lax.axis_index("row"), lax.axis_index("col")
    width = shift.shape[0]
    shard = jnp.concatenate([points.reshape(12, width), weights, shift[None]], 0)[:, None]
    gathered = gather_shards(shard)

    slots = jnp.arange(4, dtype=jnp.int32)
    tile_rows = row + rows * slots
    tile_cols = col + cols * slots[:2]
    wanted = jnp.concatenate([slots[:2], tile_rows, tile_cols])
    clusters = jnp.arange(cluster_rank.shape[0], dtype=jnp.int32)
    found = jnp.sum(jnp.where(cluster_rank[None, :] == wanted[:, None], clusters[None, :], 0), axis=1)
    from_row, from_x = found // 4, found % 4
    dy = (row // 2) ^ (from_row // 2)
    dc = (row % 2 - from_row % 2) % 2
    dx = (col // 4 - from_x) % 4
    dz = (col % 4) ^ slots
    where = ((((dc * 4 + dx) * 4 + dy) * 4)[:, None] + dz[None, :]).reshape(-1).astype(jnp.int32)

    u, v, wr, wc = pl.pallas_call(
        prep_kernel,
        grid_spec=pltpu.PrefetchScalarGridSpec(
            num_scalar_prefetch=1,
            grid=(8,),
            in_specs=whole(1),
            out_specs=[
                pl.BlockSpec((None, QUAD, TILE, FEAT), lambda t, at: (t, 0, 0, 0)),
                pl.BlockSpec((None, QUAD, FEAT, TILE), lambda t, at: (t, 0, 0, 0)),
                pl.BlockSpec((None, TILE, 128), lambda t, at: (t, 0, 0)),
                pl.BlockSpec((None, 8, TILE), lambda t, at: (t, 0, 0)),
            ],
            scratch_shapes=[pltpu.VMEM((128, TILE), F32)],
        ),
        out_shape=[
            jax.ShapeDtypeStruct((8, QUAD, TILE, FEAT), BF16),
            jax.ShapeDtypeStruct((8, QUAD, FEAT, TILE), BF16),
            jax.ShapeDtypeStruct((8, TILE, 128), F32),
            jax.ShapeDtypeStruct((8, 8, TILE), F32),
        ],
        name="prep",
        compiler_params=pltpu.CompilerParams(vmem_limit_bytes=16 << 20),
    )(where, gathered)

    block_rows, block_cols = tile_rows[:, None], tile_cols[None, :]
    kinds = jnp.where(
        block_rows < block_cols,
        ZERO,
        jnp.where(
            block_cols >= 2,
            jnp.where(block_rows == block_cols, DIAGONAL, UPDATE),
            jnp.where(block_rows < 2, FACTOR, PANEL),
        ),
    )
    mine = row // 4
    order = jnp.arange(8, dtype=jnp.int32)
    sources = (row // 2 - order % 4) % 4 * 2 + (row % 2 - order // 4) % 2
    head = jnp.stack([mine, col + cols * mine, row % 4 * BASE])
    info = jnp.concatenate([head, kinds.reshape(-1), jnp.where((row < 2) & (col < 2), row * 2 + col, 1)[None], sources]).astype(jnp.int32)

    def geometry(left, right, held):
        return [
            pl.BlockSpec((held, QUAD, TILE, FEAT), lambda *at: (left(*at), 0, 0, 0)),
            pl.BlockSpec((2, QUAD, FEAT, TILE), lambda *at: (right, 0, 0, 0)),
            pl.BlockSpec((held, TILE, 128), lambda *at: (left(*at), 0, 0)),
            pl.BlockSpec((2, 8, TILE), lambda *at: (right, 0, 0)),
        ]

    factor, weights_part = pl.pallas_call(
        chain_kernel,
        grid_spec=pltpu.PrefetchScalarGridSpec(
            num_scalar_prefetch=1,
            grid=(1,),
            in_specs=geometry(lambda *at: 0, 0, 2)
            + [
                pl.BlockSpec((1, QUAD, FEAT, TILE), lambda i, info: (6 + info[0], 0, 0, 0)),
                pl.BlockSpec((1, 8, TILE), lambda i, info: (6 + info[0], 0, 0)),
            ],
            out_specs=[
                pl.BlockSpec((TILE, TILE), lambda i, info: (0, 0)),
                pl.BlockSpec((LEAD, BASE), lambda i, info: (0, 0)),
            ],
            scratch_shapes=[
                pltpu.VMEM((LEAD + BASE, 2 * LEAD), F32),
                pltpu.VMEM((LEAD + BASE, BASE), F32),
                pltpu.VMEM((BASE, BASE), F32),
                pltpu.VMEM((STEP, STEP, BASE), F32),
                pltpu.VMEM((STEP, STEP, BASE), F32),
                pltpu.VMEM((STEP, BASE), F32),
                pltpu.VMEM((2 * BASE, WINDOW + BASE), BF16),
                pltpu.VMEM((LEAD, 2 * BASE), BF16),
            ],
        ),
        out_shape=[jax.ShapeDtypeStruct((TILE, TILE), F32), jax.ShapeDtypeStruct((LEAD, BASE), F32)],
        name="chain",
        compiler_params=pltpu.CompilerParams(vmem_limit_bytes=36 << 20),
    )(info, u, v, wr, wc, v, wc)

    tall = jax.ShapeDtypeStruct((4 * TILE, LEAD), BF16)
    chunks = TILE // CHUNK

    blocked = pl.BlockSpec((CHUNK, LEAD), lambda i, h, info: (i * chunks + h, 0))

    def assembled(kernel, right, shapes, tiles, name):
        return pl.pallas_call(
            kernel,
            grid_spec=pltpu.PrefetchScalarGridSpec(
                num_scalar_prefetch=1,
                grid=(4, chunks),
                in_specs=geometry(lambda i, h, info: 2 + i, right, 1),
                out_specs=[blocked] * len(shapes),
            ),
            out_shape=shapes,
            cost_estimate=pl.CostEstimate(
                flops=tiles * 7_500_000_000, bytes_accessed=tiles * 2_000_000, transcendentals=tiles * 4_000_000
            ),
            name=name,
            compiler_params=pltpu.CompilerParams(vmem_limit_bytes=20 << 20),
        )(info, u, v, wr, wc)

    near = [send(weights_part, lambda y, c, x, z, k=k: (y + k, c, x, z), rows, cols) for k in range(1, 4)]
    panels = assembled(panel_kernel, 0, [tall] * 2, 8, "panel")
    *near, ah, al = lax.optimization_barrier((*near, *panels))
    parts = [weights_part] + near
    parts = parts + [send(part, lambda y, c, x, z: (y, c + 1, x, z), rows, cols) for part in parts]
    own = assembled(own_kernel, 3, [jax.ShapeDtypeStruct((4 * TILE, LEAD), F32)], 6, "own")
    *parts, own = lax.optimization_barrier((*parts, *own))

    lines = CHUNK * 8
    out = pl.pallas_call(
        final_kernel,
        grid_spec=pltpu.PrefetchScalarGridSpec(
            num_scalar_prefetch=1,
            grid=(4, chunks),
            in_specs=whole(9) + [blocked] * 3,
            out_specs=pl.BlockSpec((lines, 128), lambda i, h, info: (i * chunks + h, 0)),
            scratch_shapes=[pltpu.VMEM((2, LEAD, TILE), BF16)] * 2,
        ),
        out_shape=jax.ShapeDtypeStruct((4 * TILE * 8, 128), F32),
        name="final",
        compiler_params=pltpu.CompilerParams(vmem_limit_bytes=24 << 20),
    )(info, factor, *parts, ah, al, own)
    return out.reshape(4, 1, TILE, 2, 1, TILE)


def solution(mesh):
    return jax.shard_map(
        shards,
        mesh=mesh,
        in_specs=(P(None, None, ("row", "col")), P(None, ("row", "col")), P(("row", "col")), P()),
        out_specs=P(None, "row", None, None, "col", None),
        check_vma=False,
    )
```

```python
import functools

import jax
import jax.numpy as jnp
from jax import lax
from jax.experimental import pallas as pl
from jax.experimental.pallas import tpu as pltpu
from jax.sharding import PartitionSpec as P

SOFTENING_SQUARED = 0.0004
F32 = jnp.float32
BF16 = jnp.bfloat16
QUAD = 4
TILE = 512
FEAT = 48
LEAD = 1024
BASE = 128
STEP = 32
HALVES = STEP // 8
WINDOW = LEAD + BASE
HIGHEST = lax.Precision.HIGHEST


def split(value):
    high = value.astype(BF16)
    return high, (value - high.astype(F32)).astype(BF16)


def dot3(a_high, a_low, b_high, b_low):
    dot = functools.partial(jnp.dot, preferred_element_type=F32)
    return dot(a_high, b_high) + (dot(a_high, b_low) + dot(a_low, b_high))


def send(value, move, rows, cols):
    ys, xs = rows // 2, 4
    zs = cols // xs
    pairs = []
    for source in range(rows * cols):
        row, col = divmod(source, cols)
        y, core, x, z = move(row // 2, row % 2, col // zs, col % zs)
        pairs.append((source, ((y % ys) * 2 + core % 2) * cols + (x % xs) * zs + z % zs))
    return lax.ppermute(value, ("row", "col"), pairs)


def gather_shards(shard):
    rows, cols = lax.axis_size("row"), lax.axis_size("col")
    held = shard[None]
    for axis in (3, 2, 0):
        moved = [held]
        for k in range(1, 4):
            move = lambda *at, k=k: [part + k * (i == axis) for i, part in enumerate(at)]
            moved.append(send(held, move, rows, cols))
        held = jnp.concatenate(moved, 0)
    return jnp.concatenate([held, send(held, lambda y, c, x, z: (y, c + 1, x, z), rows, cols)], 0)


def prep_kernel(where_ref, g_ref, u_ref, v_ref, wr_ref, wc_ref, pad):
    tile = pl.program_id(0)
    geometry = jnp.concatenate([g_ref[where_ref[4 * tile + z], :, 0, :] for z in range(4)], axis=1)
    centred = geometry[0:12] - 0.5
    coarse = jnp.floor(centred * 256.0 + 0.5) * (1.0 / 256.0)
    fine = centred - coarse
    fine_high = fine.astype(BF16).astype(F32)
    fine_low = fine - fine_high
    per = lambda value: [value[4 * c : 4 * c + 4] for c in range(3)]
    coarse, fine, fine_high, fine_low = per(coarse), per(fine), per(fine_high), per(fine_low)
    norm = sum(c * c for c in coarse)
    norm_high = jnp.floor(norm * 256.0) * (1.0 / 256.0)
    norm_low = norm - norm_high
    mixed = sum(2.0 * c * f + f * f for c, f in zip(coarse, fine))

    def pieces(value):
        first = value.astype(BF16).astype(F32)
        second = (value - first).astype(BF16).astype(F32)
        return [first, second, value - first - second]

    one = jnp.ones_like(norm)
    twice = lambda values: [-2.0 * value for value in values]
    left = twice(coarse) + [norm_high, norm_low, one, one]
    left += twice(coarse) + twice(coarse) + twice(fine_high) + twice(fine_low)
    left += twice(fine_high) + twice(fine_high) + twice(fine_low)
    left += pieces(mixed) + [one] * 3
    right = coarse + [one, one, norm_high, norm_low]
    right += fine_high + fine_low + coarse + coarse
    right += fine_high + fine_low + fine_high
    right += [one] * 3 + pieces(mixed + SOFTENING_SQUARED)
    pad[...] = jnp.zeros_like(pad)
    @pl.when(tile < 6)
    def _():
        for quad in range(QUAD):
            for k, value in enumerate(left):
                pad[k : k + 1, :] = value[quad : quad + 1, :]
            u_ref[quad] = jnp.transpose(pad[...])[:, :FEAT].astype(BF16)

    @pl.when((tile < 2) | (tile >= 6))
    def _():
        for quad in range(QUAD):
            for k, value in enumerate(right):
                pad[k : k + 1, :] = value[quad : quad + 1, :]
            v_ref[quad] = pad[0:FEAT, :].astype(BF16)

    pad[0:5, :] = geometry[12:17]
    wr_ref[...] = jnp.transpose(pad[...])
    wc_ref[0:5, :] = geometry[12:17]


def assemble(u_ref, v_ref, wr_ref, wc_ref, left, right, start, count, cols=slice(0, TILE)):
    rows = pl.ds(start, count)
    total = None
    for first in range(QUAD):
        part = None
        for second in range(QUAD):
            squared = jnp.dot(u_ref[left, first, rows, :], v_ref[right, second, :, cols], preferred_element_type=F32)
            term = lax.rsqrt(squared) * wc_ref[right, second : second + 1, cols]
            part = term if part is None else part + term
        part = part * wr_ref[left, rows, first : first + 1]
        total = part if total is None else total + part
    return total


def split3(value):
    first = value.astype(BF16)
    rest = value - first.astype(F32)
    second = rest.astype(BF16)
    return first, second, (rest - second.astype(F32)).astype(BF16)


def dot_rows(left, right):
    return lax.dot_general(left, right, (((0,), (0,)), ((), ())), preferred_element_type=F32)


def eliminate_base(work, spread, solved, lines, raw):
    lane = lax.broadcasted_iota(jnp.int32, (8, BASE), 1)
    sub = lax.broadcasted_iota(jnp.int32, (8, BASE), 0)
    repeat = lambda ref, i: ref[pl.ds(i, 8, stride=0), :]
    for step in range(BASE // STEP):
        low = step * STEP
        high = low + STEP
        a, c = [], [[] for _ in range(HALVES)]
        for half in range(HALVES):
            left = work[low + 8 * half : low + 8 * half + 8, :]
            for j in range(STEP):
                column = jnp.broadcast_to(left[:, low + j : low + j + 1], (8, BASE))
                c[half].append(column)
            inside = (lane >= low) & (lane < high)
            a.append(jnp.where(inside, jnp.where(lane == sub + (low + 8 * half), 1.0, 0.0), left))
            lines[8 * half : 8 * half + 8, :] = a[half]
        d = []
        for half in range(HALVES):
            diagonal = c[half][8 * half]
            for j in range(8 * half + 1, 8 * half + 8):
                diagonal = jnp.where(sub == j % 8, c[half][j], diagonal)
            d.append(diagonal)
            spread[0, 8 * half : 8 * half + 8, :] = diagonal
        pivot = repeat(spread.at[0], 0)
        raw[0] = c[0][0]
        for j in range(STEP):
            scale = lax.rsqrt(pivot)
            if j + 1 < STEP:
                below = repeat(raw.at[j], (j + 1) % 8)
                pivot = repeat(spread.at[j], j + 1) - (below * below) * (scale * scale)
            first = j // 8
            line = repeat(lines, j) * scale
            for half in range(first, HALVES):
                c[half][j] = c[half][j] * scale
                solved[j, 8 * half : 8 * half + 8, :] = c[half][j]
                if j + 2 < STEP:
                    d[half] = d[half] - c[half][j] * c[half][j]
                    spread[j + 1, 8 * half : 8 * half + 8, :] = d[half]
            for k in range(j + 1, STEP):
                factor = repeat(solved.at[j], k)
                for half in range(k // 8, HALVES):
                    c[half][k] = c[half][k] - c[half][j] * factor
                if k == j + 1 and k + 1 < STEP:
                    raw[k] = c[(k + 1) // 8][k]
            for half in range(first, HALVES):
                update = a[half] - c[half][j] * line
                if half == first:
                    update = jnp.where(sub > j % 8, update, jnp.where(sub == j % 8, line, a[half]))
                a[half] = update
                lines[8 * half : 8 * half + 8, :] = update
        for half in range(HALVES):
            work[low + 8 * half : low + 8 * half + 8, :] = a[half]
        if high < BASE:
            w0, w1, w2 = split3(jnp.concatenate(a, 0))
            product = dot_rows(
                jnp.concatenate([w0, w0, w1, w0, w1, w2], 0), jnp.concatenate([w0, w1, w0, w2, w1, w0], 0)
            )
            rest = lax.broadcasted_iota(jnp.int32, (BASE - high, BASE), 1)
            kept = jnp.where((rest >= low) & (rest < high), 0.0, work[high:, :])
            work[high:, :] = kept - product[high:, :]


def chain_kernel(
    info, u_ref, v_ref, wr_ref, wc_ref, vj_ref, wj_ref,
    f_ref, y_ref,
    state, side, work, spread, solved, lines, raw, stack, tall,
):
    state[:, LEAD:] = jnp.zeros((LEAD + BASE, LEAD), F32)
    state[LEAD:, :LEAD] = jnp.zeros((BASE, LEAD), F32)
    side[LEAD:, :] = jnp.zeros((BASE, BASE), F32)
    lane = lax.broadcasted_iota(jnp.int32, (BASE, BASE), 1)
    row = lax.broadcasted_iota(jnp.int32, (BASE, BASE), 0)
    eye = (row == lane).astype(F32)
    geometry = (u_ref, v_ref, wr_ref, wc_ref)
    column = info[1]
    offset = pl.multiple_of(info[2], BASE)

    @pl.loop(0, TILE // 256)
    def _(chunk):
        start = pl.multiple_of(chunk * 256, 256)
        rows = pl.ds(start, 256)
        for tile in range(2):
            here = pl.ds(pl.multiple_of(tile * TILE + start, 256), 256)
            low = tile * TILE
            values = assemble(*geometry, tile, tile, start, 256, slice(256, TILE))
            line = start + lax.broadcasted_iota(jnp.int32, (256, 256), 0)
            across = 256 + lax.broadcasted_iota(jnp.int32, (256, 256), 1)
            values = values + jnp.where(line == across, wr_ref[tile, rows, 4:5], 0.0)
            state[here, low + 256 : low + TILE] = values
            side[here, :] = assemble(u_ref, vj_ref, wr_ref, wj_ref, tile, 0, start, 256, pl.ds(offset, BASE))
        state[rows, TILE : 2 * TILE] = assemble(*geometry, 0, 1, start, 256)

    for tile in range(2):
        values = assemble(*geometry, tile, tile, 0, 256, slice(0, 256))
        line = lax.broadcasted_iota(jnp.int32, (256, 256), 0)
        across = lax.broadcasted_iota(jnp.int32, (256, 256), 1)
        values = values + jnp.where(line == across, wr_ref[tile, 0:256, 4:5], 0.0)
        state[tile * TILE : tile * TILE + 256, tile * TILE : tile * TILE + 256] = values

    blocks = LEAD // BASE
    both = jnp.concatenate
    dot = functools.partial(jnp.dot, preferred_element_type=F32)

    @pl.loop(0, blocks)
    def _(k):
        here = pl.multiple_of(k * BASE, BASE)
        rows = pl.ds(here, BASE)
        state[rows, pl.ds(pl.multiple_of(LEAD + here, BASE), BASE)] = eye
        work[...] = state[rows, pl.ds(here, BASE)]
        eliminate_base(work, spread, solved, lines, raw)
        l0, l1 = split(jnp.where(row >= lane, work[...], 0.0))
        window = pl.ds(here, WINDOW)

        def load(values):
            first, second = split(values)
            stack[0:128, :] = first
            stack[128:256, :] = second

        load(both([state[rows, window], side[rows, :]], 1))
        done = dot(both([l0, l0], 1), stack[...]) + dot(l1, stack[0:128, :])
        state[rows, window] = done[:, :WINDOW]
        side[rows, :] = done[:, WINDOW:]
        load(done)

        @pl.loop(0, blocks - 1 - k)
        def _(i):
            there = pl.multiple_of((i + 1) * BASE, BASE)
            parts = split(jnp.transpose(state[rows, pl.ds(pl.multiple_of(here + there, BASE), BASE)]))
            for n, part in enumerate(parts):
                tall[pl.ds(pl.multiple_of(i * BASE, BASE), BASE), n * 128 : n * 128 + 128] = part

        for pair in range(blocks // 2):
            @pl.when(pair < (blocks - k) // 2)
            def _():
                skip = pair * 256
                below = pl.ds(pl.multiple_of(here + BASE + skip, BASE), 256)
                t0, t1 = [tall[skip : skip + 256, n * 128 : n * 128 + 128] for n in range(2)]
                update = dot(both([t0, t0], 1), stack[:, skip:]) + dot(t1, stack[0:128, skip:])
                width = WINDOW - skip
                into = pl.ds(pl.multiple_of(here + skip, BASE), width)
                state[below, into] = state[below, into] - update[:, :width]
                side[below, :] = side[below, :] - update[:, width:]

    which = info[11]

    @pl.when((which == 0) | (which == 2) | (which == 3))
    def _():
        from_rows = pl.ds(pl.multiple_of(which % 2 * TILE, TILE), TILE)
        for chunk in range(TILE // BASE):
            from_cols = pl.ds(pl.multiple_of(which // 2 * TILE + chunk * BASE, BASE), BASE)
            values = jnp.transpose(state[from_rows, from_cols])
            line = chunk * BASE + lax.broadcasted_iota(jnp.int32, (BASE, TILE), 0)
            across = lax.broadcasted_iota(jnp.int32, (BASE, TILE), 1)
            keep = (line >= across) | (which == 2)
            f_ref[chunk * BASE : chunk * BASE + BASE, :] = jnp.where(keep, values, 0.0)

    @pl.when(column < 2)
    def _():
        line = lax.broadcasted_iota(jnp.int32, (LEAD, BASE), 0)
        across = lax.broadcasted_iota(jnp.int32, (LEAD, BASE), 1)
        side[:LEAD, :] = jnp.where(line == across + (column * TILE + offset), -1.0, 0.0)

    for out in range(4):
        total = jnp.zeros((256, BASE), F32)
        for part in range(out, 4):
            rows = slice(part * 256, part * 256 + 256)
            factor = jnp.transpose(state[rows, LEAD + out * 256 : LEAD + out * 256 + 256])
            high, low = split(factor)
            z_high, z_low = split(side[rows, :])
            wide = dot(high, both([z_high, z_low], 1))
            total = total + (wide[:, :BASE] + (wide[:, BASE:] + dot(low, z_high)))
        y_ref[out * 256 : out * 256 + 256, :] = total


def panel_kernel(info, u_ref, v_ref, wr_ref, wc_ref, ah_ref, al_ref):
    slot, chunk = pl.program_id(0), pl.program_id(1)
    start = pl.multiple_of(chunk * CHUNK, CHUNK)
    kinds = [info[3 + slot * 2], info[4 + slot * 2]]
    needed = lambda kind: (kind != ZERO) & (kind != FACTOR)

    @pl.when(needed(kinds[0]) | needed(kinds[1]))
    def _():
        for half in range(2):
            values = assemble(u_ref, v_ref, wr_ref, wc_ref, 0, half, start, CHUNK)
            cols = slice(half * TILE, half * TILE + TILE)
            ah_ref[:, cols], al_ref[:, cols] = split(values)


def own_kernel(info, u_ref, v_ref, wr_ref, wc_ref, own_ref):
    slot, chunk = pl.program_id(0), pl.program_id(1)
    start = pl.multiple_of(chunk * CHUNK, CHUNK)
    for j in range(2):
        kind = info[3 + slot * 2 + j]

        @pl.when((kind == UPDATE) | (kind == DIAGONAL))
        def _():
            values = assemble(u_ref, v_ref, wr_ref, wc_ref, 0, j, start, CHUNK)
            row = start + lax.broadcasted_iota(jnp.int32, (CHUNK, TILE), 0)
            col = lax.broadcasted_iota(jnp.int32, (CHUNK, TILE), 1)
            shift = wr_ref[0, pl.ds(start, CHUNK), 4:5]
            values = values + jnp.where((row == col) & (kind == DIAGONAL), shift, 0.0)
            own_ref[:, j * TILE : j * TILE + TILE] = values


CHUNK = 256
ZERO, UPDATE, DIAGONAL, PANEL, FACTOR = range(5)


def final_kernel(info, f_ref, *rest):
    parts, (ah, al, own, out_ref, yh, yl) = rest[:8], rest[8:]
    slot, chunk = pl.program_id(0), pl.program_id(1)
    start = pl.multiple_of(chunk * CHUNK, CHUNK)
    kinds = [info[3 + slot * 2], info[4 + slot * 2]]

    @pl.when((slot == 0) & (chunk == 0))
    def _():
        for p, part in enumerate(parts):
            source = info[12 + p]
            lanes = pl.ds(pl.multiple_of(source % 4 * 128, 128), 128)
            yh[source // 4, :, lanes], yl[source // 4, :, lanes] = split(part[...])

    def store(j, values):
        for q in range(TILE // 128):
            out_ref[pl.ds(j * 4 + q, CHUNK, stride=8), :] = values[:, q * 128 : (q + 1) * 128]

    for j in range(2):
        kind = kinds[j]

        @pl.when(kind == ZERO)
        def _():
            store(j, jnp.zeros((CHUNK, TILE), F32))

        @pl.when(kind == PANEL)
        def _():
            store(j, -dot3(ah[...], al[...], yh[j], yl[j]))

        @pl.when((kind == UPDATE) | (kind == DIAGONAL))
        def _():
            values = own[:, j * TILE : j * TILE + TILE]
            store(j, values - dot3(ah[...], al[...], yh[j], yl[j]))

        if j == 0:
            @pl.when(kind == FACTOR)
            def _():
                store(j, f_ref[pl.ds(start, CHUNK), :])


def whole(count):
    return [pl.BlockSpec(memory_space=pltpu.VMEM)] * count


def shards(points, weights, shift, cluster_rank):
    rows, cols = lax.axis_size("row"), lax.axis_size("col")
    row, col = lax.axis_index("row"), lax.axis_index("col")
    width = shift.shape[0]
    shard = jnp.concatenate([points.reshape(12, width), weights, shift[None]], 0)[:, None]
    gathered = gather_shards(shard)

    slots = jnp.arange(4, dtype=jnp.int32)
    tile_rows = row + rows * slots
    tile_cols = col + cols * slots[:2]
    wanted = jnp.concatenate([slots[:2], tile_rows, tile_cols])
    clusters = jnp.arange(cluster_rank.shape[0], dtype=jnp.int32)
    found = jnp.sum(jnp.where(cluster_rank[None, :] == wanted[:, None], clusters[None, :], 0), axis=1)
    from_row, from_x = found // 4, found % 4
    dy = (row // 2 - from_row // 2) % 4
    dc = (row % 2 - from_row % 2) % 2
    dx = (col // 4 - from_x) % 4
    dz = (col % 4 - slots) % 4
    where = ((((dc * 4 + dy) * 4 + dx) * 4)[:, None] + dz[None, :]).reshape(-1).astype(jnp.int32)

    u, v, wr, wc = pl.pallas_call(
        prep_kernel,
        grid_spec=pltpu.PrefetchScalarGridSpec(
            num_scalar_prefetch=1,
            grid=(8,),
            in_specs=whole(1),
            out_specs=[
                pl.BlockSpec((None, QUAD, TILE, FEAT), lambda t, at: (t, 0, 0, 0)),
                pl.BlockSpec((None, QUAD, FEAT, TILE), lambda t, at: (t, 0, 0, 0)),
                pl.BlockSpec((None, TILE, 128), lambda t, at: (t, 0, 0)),
                pl.BlockSpec((None, 8, TILE), lambda t, at: (t, 0, 0)),
            ],
            scratch_shapes=[pltpu.VMEM((128, TILE), F32)],
        ),
        out_shape=[
            jax.ShapeDtypeStruct((8, QUAD, TILE, FEAT), BF16),
            jax.ShapeDtypeStruct((8, QUAD, FEAT, TILE), BF16),
            jax.ShapeDtypeStruct((8, TILE, 128), F32),
            jax.ShapeDtypeStruct((8, 8, TILE), F32),
        ],
        name="prep",
        compiler_params=pltpu.CompilerParams(vmem_limit_bytes=16 << 20),
    )(where, gathered)

    block_rows, block_cols = tile_rows[:, None], tile_cols[None, :]
    kinds = jnp.where(
        block_rows < block_cols,
        ZERO,
        jnp.where(
            block_cols >= 2,
            jnp.where(block_rows == block_cols, DIAGONAL, UPDATE),
            jnp.where(block_rows < 2, FACTOR, PANEL),
        ),
    )
    mine = row // 4
    order = jnp.arange(8, dtype=jnp.int32)
    sources = (row // 2 - order % 4) % 4 * 2 + (row % 2 - order // 4) % 2
    head = jnp.stack([mine, col + cols * mine, row % 4 * BASE])
    info = jnp.concatenate([head, kinds.reshape(-1), jnp.where((row < 2) & (col < 2), row * 2 + col, 1)[None], sources]).astype(jnp.int32)

    def geometry(left, right, held):
        return [
            pl.BlockSpec((held, QUAD, TILE, FEAT), lambda *at: (left(*at), 0, 0, 0)),
            pl.BlockSpec((2, QUAD, FEAT, TILE), lambda *at: (right, 0, 0, 0)),
            pl.BlockSpec((held, TILE, 128), lambda *at: (left(*at), 0, 0)),
            pl.BlockSpec((2, 8, TILE), lambda *at: (right, 0, 0)),
        ]

    factor, weights_part = pl.pallas_call(
        chain_kernel,
        grid_spec=pltpu.PrefetchScalarGridSpec(
            num_scalar_prefetch=1,
            grid=(1,),
            in_specs=geometry(lambda *at: 0, 0, 2)
            + [
                pl.BlockSpec((1, QUAD, FEAT, TILE), lambda i, info: (6 + info[0], 0, 0, 0)),
                pl.BlockSpec((1, 8, TILE), lambda i, info: (6 + info[0], 0, 0)),
            ],
            out_specs=[
                pl.BlockSpec((TILE, TILE), lambda i, info: (0, 0)),
                pl.BlockSpec((LEAD, BASE), lambda i, info: (0, 0)),
            ],
            scratch_shapes=[
                pltpu.VMEM((LEAD + BASE, 2 * LEAD), F32),
                pltpu.VMEM((LEAD + BASE, BASE), F32),
                pltpu.VMEM((BASE, BASE), F32),
                pltpu.VMEM((STEP, STEP, BASE), F32),
                pltpu.VMEM((STEP, STEP, BASE), F32),
                pltpu.VMEM((STEP, BASE), F32),
                pltpu.VMEM((STEP, 8, BASE), F32),
                pltpu.VMEM((2 * BASE, WINDOW + BASE), BF16),
                pltpu.VMEM((LEAD, 2 * BASE), BF16),
            ],
        ),
        out_shape=[jax.ShapeDtypeStruct((TILE, TILE), F32), jax.ShapeDtypeStruct((LEAD, BASE), F32)],
        name="chain",
        compiler_params=pltpu.CompilerParams(vmem_limit_bytes=36 << 20),
    )(info, u, v, wr, wc, v, wc)

    tall = jax.ShapeDtypeStruct((4 * TILE, LEAD), BF16)
    chunks = TILE // CHUNK

    blocked = pl.BlockSpec((CHUNK, LEAD), lambda i, h, info: (i * chunks + h, 0))

    def assembled(kernel, right, shapes, tiles, name):
        return pl.pallas_call(
            kernel,
            grid_spec=pltpu.PrefetchScalarGridSpec(
                num_scalar_prefetch=1,
                grid=(4, chunks),
                in_specs=geometry(lambda i, h, info: 2 + i, right, 1),
                out_specs=[blocked] * len(shapes),
            ),
            out_shape=shapes,
            cost_estimate=pl.CostEstimate(
                flops=tiles * 7_500_000_000, bytes_accessed=tiles * 2_000_000, transcendentals=tiles * 4_000_000
            ),
            name=name,
            compiler_params=pltpu.CompilerParams(vmem_limit_bytes=20 << 20),
        )(info, u, v, wr, wc)

    near = [send(weights_part, lambda y, c, x, z, k=k: (y + k, c, x, z), rows, cols) for k in range(1, 4)]
    panels = assembled(panel_kernel, 0, [tall] * 2, 8, "panel")
    *near, ah, al = lax.optimization_barrier((*near, *panels))
    parts = [weights_part] + near
    parts = parts + [send(part, lambda y, c, x, z: (y, c + 1, x, z), rows, cols) for part in parts]
    own = assembled(own_kernel, 3, [jax.ShapeDtypeStruct((4 * TILE, LEAD), F32)], 6, "own")
    *parts, own = lax.optimization_barrier((*parts, *own))

    lines = CHUNK * 8
    out = pl.pallas_call(
        final_kernel,
        grid_spec=pltpu.PrefetchScalarGridSpec(
            num_scalar_prefetch=1,
            grid=(4, chunks),
            in_specs=whole(9) + [blocked] * 3,
            out_specs=pl.BlockSpec((lines, 128), lambda i, h, info: (i * chunks + h, 0)),
            scratch_shapes=[pltpu.VMEM((2, LEAD, TILE), BF16)] * 2,
        ),
        out_shape=jax.ShapeDtypeStruct((4 * TILE * 8, 128), F32),
        name="final",
        compiler_params=pltpu.CompilerParams(vmem_limit_bytes=24 << 20),
    )(info, factor, *parts, ah, al, own)
    return out.reshape(4, 1, TILE, 2, 1, TILE)


def solution(mesh):
    return jax.shard_map(
        shards,
        mesh=mesh,
        in_specs=(P(None, None, ("row", "col")), P(None, ("row", "col")), P(("row", "col")), P()),
        out_specs=P(None, "row", None, None, "col", None),
        check_vma=False,
    )
```

```python
import functools

import jax
import jax.numpy as jnp
from jax import lax
from jax.experimental import pallas as pl
from jax.experimental.pallas import tpu as pltpu
from jax.sharding import PartitionSpec as P

SOFTENING_SQUARED = 0.0004
F32 = jnp.float32
BF16 = jnp.bfloat16
QUAD = 4
TILE = 512
FEAT = 48
LEAD = 1024
BASE = 128
STEP = 32
HALVES = STEP // 8
WINDOW = LEAD + BASE
HIGHEST = lax.Precision.HIGHEST


def split(value):
    high = value.astype(BF16)
    return high, (value - high.astype(F32)).astype(BF16)


def dot3(a_high, a_low, b_high, b_low):
    dot = functools.partial(jnp.dot, preferred_element_type=F32)
    return dot(a_high, b_high) + (dot(a_high, b_low) + dot(a_low, b_high))


def send(value, move, rows, cols):
    ys, xs = rows // 2, 4
    zs = cols // xs
    pairs = []
    for source in range(rows * cols):
        row, col = divmod(source, cols)
        y, core, x, z = move(row // 2, row % 2, col // zs, col % zs)
        pairs.append((source, ((y % ys) * 2 + core % 2) * cols + (x % xs) * zs + z % zs))
    return lax.ppermute(value, ("row", "col"), pairs)


def gather_shards(shard):
    rows, cols = lax.axis_size("row"), lax.axis_size("col")
    copies = jnp.broadcast_to(shard[None], (cols, *shard.shape))
    held = lax.all_to_all(copies, "col", 0, 0, tiled=True)
    moved = [held] + [send(held, lambda y, c, x, z, k=k: (y + k, c, x, z), rows, cols) for k in range(1, 4)]
    held = jnp.concatenate(moved, 0)
    return jnp.concatenate([held, send(held, lambda y, c, x, z: (y, c + 1, x, z), rows, cols)], 0)


def prep_kernel(where_ref, g_ref, u_ref, v_ref, wr_ref, wc_ref, pad):
    tile = pl.program_id(0)
    geometry = jnp.concatenate([g_ref[where_ref[4 * tile + z], :, 0, :] for z in range(4)], axis=1)
    centred = geometry[0:12] - 0.5
    coarse = jnp.floor(centred * 256.0 + 0.5) * (1.0 / 256.0)
    fine = centred - coarse
    fine_high = fine.astype(BF16).astype(F32)
    fine_low = fine - fine_high
    per = lambda value: [value[4 * c : 4 * c + 4] for c in range(3)]
    coarse, fine, fine_high, fine_low = per(coarse), per(fine), per(fine_high), per(fine_low)
    norm = sum(c * c for c in coarse)
    norm_high = jnp.floor(norm * 256.0) * (1.0 / 256.0)
    norm_low = norm - norm_high
    mixed = sum(2.0 * c * f + f * f for c, f in zip(coarse, fine))

    def pieces(value):
        first = value.astype(BF16).astype(F32)
        second = (value - first).astype(BF16).astype(F32)
        return [first, second, value - first - second]

    one = jnp.ones_like(norm)
    twice = lambda values: [-2.0 * value for value in values]
    left = twice(coarse) + [norm_high, norm_low, one, one]
    left += twice(coarse) + twice(coarse) + twice(fine_high) + twice(fine_low)
    left += twice(fine_high) + twice(fine_high) + twice(fine_low)
    left += pieces(mixed) + [one] * 3
    right = coarse + [one, one, norm_high, norm_low]
    right += fine_high + fine_low + coarse + coarse
    right += fine_high + fine_low + fine_high
    right += [one] * 3 + pieces(mixed + SOFTENING_SQUARED)
    pad[...] = jnp.zeros_like(pad)
    @pl.when(tile < 6)
    def _():
        for quad in range(QUAD):
            for k, value in enumerate(left):
                pad[k : k + 1, :] = value[quad : quad + 1, :]
            u_ref[quad] = jnp.transpose(pad[...])[:, :FEAT].astype(BF16)

    @pl.when((tile < 2) | (tile >= 6))
    def _():
        for quad in range(QUAD):
            for k, value in enumerate(right):
                pad[k : k + 1, :] = value[quad : quad + 1, :]
            v_ref[quad] = pad[0:FEAT, :].astype(BF16)

    pad[0:5, :] = geometry[12:17]
    wr_ref[...] = jnp.transpose(pad[...])
    wc_ref[0:5, :] = geometry[12:17]


def assemble(u_ref, v_ref, wr_ref, wc_ref, left, right, start, count, cols=slice(0, TILE)):
    rows = pl.ds(start, count)
    total = None
    for first in range(QUAD):
        part = None
        for second in range(QUAD):
            squared = jnp.dot(u_ref[left, first, rows, :], v_ref[right, second, :, cols], preferred_element_type=F32)
            term = lax.rsqrt(squared) * wc_ref[right, second : second + 1, cols]
            part = term if part is None else part + term
        part = part * wr_ref[left, rows, first : first + 1]
        total = part if total is None else total + part
    return total


def split3(value):
    first = value.astype(BF16)
    rest = value - first.astype(F32)
    second = rest.astype(BF16)
    return first, second, (rest - second.astype(F32)).astype(BF16)


def dot_rows(left, right):
    return lax.dot_general(left, right, (((0,), (0,)), ((), ())), preferred_element_type=F32)


def eliminate_base(work, spread, solved, lines, raw):
    lane = lax.broadcasted_iota(jnp.int32, (8, BASE), 1)
    sub = lax.broadcasted_iota(jnp.int32, (8, BASE), 0)
    repeat = lambda ref, i: ref[pl.ds(i, 8, stride=0), :]
    for step in range(BASE // STEP):
        low = step * STEP
        high = low + STEP
        a, c = [], [[] for _ in range(HALVES)]
        for half in range(HALVES):
            left = work[low + 8 * half : low + 8 * half + 8, :]
            for j in range(STEP):
                column = jnp.broadcast_to(left[:, low + j : low + j + 1], (8, BASE))
                c[half].append(column)
            inside = (lane >= low) & (lane < high)
            a.append(jnp.where(inside, jnp.where(lane == sub + (low + 8 * half), 1.0, 0.0), left))
            lines[8 * half : 8 * half + 8, :] = a[half]
        d = []
        for half in range(HALVES):
            diagonal = c[half][8 * half]
            for j in range(8 * half + 1, 8 * half + 8):
                diagonal = jnp.where(sub == j % 8, c[half][j], diagonal)
            d.append(diagonal)
            spread[0, 8 * half : 8 * half + 8, :] = diagonal
        pivot = repeat(spread.at[0], 0)
        raw[0] = c[0][0]
        for j in range(STEP):
            scale = lax.rsqrt(pivot)
            if j + 1 < STEP:
                below = repeat(raw.at[j], (j + 1) % 8)
                pivot = repeat(spread.at[j], j + 1) - (below * below) * (scale * scale)
            first = j // 8
            line = repeat(lines, j) * scale
            for half in range(first, HALVES):
                c[half][j] = c[half][j] * scale
                solved[j, 8 * half : 8 * half + 8, :] = c[half][j]
                if j + 2 < STEP:
                    d[half] = d[half] - c[half][j] * c[half][j]
                    spread[j + 1, 8 * half : 8 * half + 8, :] = d[half]
            for k in range(j + 1, STEP):
                factor = repeat(solved.at[j], k)
                for half in range(k // 8, HALVES):
                    c[half][k] = c[half][k] - c[half][j] * factor
                if k == j + 1 and k + 1 < STEP:
                    raw[k] = c[(k + 1) // 8][k]
            for half in range(first, HALVES):
                update = a[half] - c[half][j] * line
                if half == first:
                    update = jnp.where(sub > j % 8, update, jnp.where(sub == j % 8, line, a[half]))
                a[half] = update
                lines[8 * half : 8 * half + 8, :] = update
        for half in range(HALVES):
            work[low + 8 * half : low + 8 * half + 8, :] = a[half]
        if high < BASE:
            w0, w1, w2 = split3(jnp.concatenate(a, 0))
            product = dot_rows(
                jnp.concatenate([w0, w0, w1, w0, w1, w2], 0), jnp.concatenate([w0, w1, w0, w2, w1, w0], 0)
            )
            rest = lax.broadcasted_iota(jnp.int32, (BASE - high, BASE), 1)
            kept = jnp.where((rest >= low) & (rest < high), 0.0, work[high:, :])
            work[high:, :] = kept - product[high:, :]


def chain_kernel(
    info, u_ref, v_ref, wr_ref, wc_ref, vj_ref, wj_ref,
    f_ref, y_ref,
    state, side, work, spread, solved, lines, raw, stack, tall,
):
    state[:, LEAD:] = jnp.zeros((LEAD + BASE, LEAD), F32)
    state[LEAD:, :LEAD] = jnp.zeros((BASE, LEAD), F32)
    side[LEAD:, :] = jnp.zeros((BASE, BASE), F32)
    lane = lax.broadcasted_iota(jnp.int32, (BASE, BASE), 1)
    row = lax.broadcasted_iota(jnp.int32, (BASE, BASE), 0)
    eye = (row == lane).astype(F32)
    geometry = (u_ref, v_ref, wr_ref, wc_ref)
    column = info[1]
    offset = pl.multiple_of(info[2], BASE)

    @pl.loop(0, TILE // 256)
    def _(chunk):
        start = pl.multiple_of(chunk * 256, 256)
        rows = pl.ds(start, 256)
        for tile in range(2):
            here = pl.ds(pl.multiple_of(tile * TILE + start, 256), 256)
            low = tile * TILE
            values = assemble(*geometry, tile, tile, start, 256, slice(256, TILE))
            line = start + lax.broadcasted_iota(jnp.int32, (256, 256), 0)
            across = 256 + lax.broadcasted_iota(jnp.int32, (256, 256), 1)
            values = values + jnp.where(line == across, wr_ref[tile, rows, 4:5], 0.0)
            state[here, low + 256 : low + TILE] = values
            side[here, :] = assemble(u_ref, vj_ref, wr_ref, wj_ref, tile, 0, start, 256, pl.ds(offset, BASE))
        state[rows, TILE : 2 * TILE] = assemble(*geometry, 0, 1, start, 256)

    for tile in range(2):
        values = assemble(*geometry, tile, tile, 0, 256, slice(0, 256))
        line = lax.broadcasted_iota(jnp.int32, (256, 256), 0)
        across = lax.broadcasted_iota(jnp.int32, (256, 256), 1)
        values = values + jnp.where(line == across, wr_ref[tile, 0:256, 4:5], 0.0)
        state[tile * TILE : tile * TILE + 256, tile * TILE : tile * TILE + 256] = values

    blocks = LEAD // BASE
    both = jnp.concatenate
    dot = functools.partial(jnp.dot, preferred_element_type=F32)

    @pl.loop(0, blocks)
    def _(k):
        here = pl.multiple_of(k * BASE, BASE)
        rows = pl.ds(here, BASE)
        state[rows, pl.ds(pl.multiple_of(LEAD + here, BASE), BASE)] = eye
        work[...] = state[rows, pl.ds(here, BASE)]
        eliminate_base(work, spread, solved, lines, raw)
        l0, l1 = split(jnp.where(row >= lane, work[...], 0.0))
        window = pl.ds(here, WINDOW)

        def load(values):
            first, second = split(values)
            stack[0:128, :] = first
            stack[128:256, :] = second

        load(both([state[rows, window], side[rows, :]], 1))
        done = dot(both([l0, l0], 1), stack[...]) + dot(l1, stack[0:128, :])
        state[rows, window] = done[:, :WINDOW]
        side[rows, :] = done[:, WINDOW:]
        load(done)

        @pl.loop(0, blocks - 1 - k)
        def _(i):
            there = pl.multiple_of((i + 1) * BASE, BASE)
            parts = split(jnp.transpose(state[rows, pl.ds(pl.multiple_of(here + there, BASE), BASE)]))
            for n, part in enumerate(parts):
                tall[pl.ds(pl.multiple_of(i * BASE, BASE), BASE), n * 128 : n * 128 + 128] = part

        for pair in range(blocks // 2):
            @pl.when(pair < (blocks - k) // 2)
            def _():
                skip = pair * 256
                below = pl.ds(pl.multiple_of(here + BASE + skip, BASE), 256)
                t0, t1 = [tall[skip : skip + 256, n * 128 : n * 128 + 128] for n in range(2)]
                update = dot(both([t0, t0], 1), stack[:, skip:]) + dot(t1, stack[0:128, skip:])
                width = WINDOW - skip
                into = pl.ds(pl.multiple_of(here + skip, BASE), width)
                state[below, into] = state[below, into] - update[:, :width]
                side[below, :] = side[below, :] - update[:, width:]

    which = info[11]

    @pl.when((which == 0) | (which == 2) | (which == 3))
    def _():
        from_rows = pl.ds(pl.multiple_of(which % 2 * TILE, TILE), TILE)
        for chunk in range(TILE // BASE):
            from_cols = pl.ds(pl.multiple_of(which // 2 * TILE + chunk * BASE, BASE), BASE)
            values = jnp.transpose(state[from_rows, from_cols])
            line = chunk * BASE + lax.broadcasted_iota(jnp.int32, (BASE, TILE), 0)
            across = lax.broadcasted_iota(jnp.int32, (BASE, TILE), 1)
            keep = (line >= across) | (which == 2)
            f_ref[chunk * BASE : chunk * BASE + BASE, :] = jnp.where(keep, values, 0.0)

    @pl.when(column < 2)
    def _():
        line = lax.broadcasted_iota(jnp.int32, (LEAD, BASE), 0)
        across = lax.broadcasted_iota(jnp.int32, (LEAD, BASE), 1)
        side[:LEAD, :] = jnp.where(line == across + (column * TILE + offset), -1.0, 0.0)

    for out in range(4):
        total = jnp.zeros((256, BASE), F32)
        for part in range(out, 4):
            rows = slice(part * 256, part * 256 + 256)
            factor = jnp.transpose(state[rows, LEAD + out * 256 : LEAD + out * 256 + 256])
            high, low = split(factor)
            z_high, z_low = split(side[rows, :])
            wide = dot(high, both([z_high, z_low], 1))
            total = total + (wide[:, :BASE] + (wide[:, BASE:] + dot(low, z_high)))
        y_ref[out * 256 : out * 256 + 256, :] = total


def panel_kernel(info, u_ref, v_ref, wr_ref, wc_ref, ah_ref, al_ref):
    slot, chunk = pl.program_id(0), pl.program_id(1)
    start = pl.multiple_of(chunk * CHUNK, CHUNK)
    kinds = [info[3 + slot * 2], info[4 + slot * 2]]
    needed = lambda kind: (kind != ZERO) & (kind != FACTOR)

    @pl.when(needed(kinds[0]) | needed(kinds[1]))
    def _():
        for half in range(2):
            values = assemble(u_ref, v_ref, wr_ref, wc_ref, 0, half, start, CHUNK)
            cols = slice(half * TILE, half * TILE + TILE)
            ah_ref[:, cols], al_ref[:, cols] = split(values)


def own_kernel(info, u_ref, v_ref, wr_ref, wc_ref, own_ref):
    slot, chunk = pl.program_id(0), pl.program_id(1)
    start = pl.multiple_of(chunk * CHUNK, CHUNK)
    for j in range(2):
        kind = info[3 + slot * 2 + j]

        @pl.when((kind == UPDATE) | (kind == DIAGONAL))
        def _():
            values = assemble(u_ref, v_ref, wr_ref, wc_ref, 0, j, start, CHUNK)
            row = start + lax.broadcasted_iota(jnp.int32, (CHUNK, TILE), 0)
            col = lax.broadcasted_iota(jnp.int32, (CHUNK, TILE), 1)
            shift = wr_ref[0, pl.ds(start, CHUNK), 4:5]
            values = values + jnp.where((row == col) & (kind == DIAGONAL), shift, 0.0)
            own_ref[:, j * TILE : j * TILE + TILE] = values


CHUNK = 256
ZERO, UPDATE, DIAGONAL, PANEL, FACTOR = range(5)


def final_kernel(info, f_ref, *rest):
    parts, (ah, al, own, out_ref, yh, yl) = rest[:8], rest[8:]
    slot, chunk = pl.program_id(0), pl.program_id(1)
    start = pl.multiple_of(chunk * CHUNK, CHUNK)
    kinds = [info[3 + slot * 2], info[4 + slot * 2]]

    @pl.when((slot == 0) & (chunk == 0))
    def _():
        for p, part in enumerate(parts):
            source = info[12 + p]
            lanes = pl.ds(pl.multiple_of(source % 4 * 128, 128), 128)
            yh[source // 4, :, lanes], yl[source // 4, :, lanes] = split(part[...])

    def store(j, values):
        for q in range(TILE // 128):
            out_ref[pl.ds(j * 4 + q, CHUNK, stride=8), :] = values[:, q * 128 : (q + 1) * 128]

    for j in range(2):
        kind = kinds[j]

        @pl.when(kind == ZERO)
        def _():
            store(j, jnp.zeros((CHUNK, TILE), F32))

        @pl.when(kind == PANEL)
        def _():
            store(j, -dot3(ah[...], al[...], yh[j], yl[j]))

        @pl.when((kind == UPDATE) | (kind == DIAGONAL))
        def _():
            values = own[:, j * TILE : j * TILE + TILE]
            store(j, values - dot3(ah[...], al[...], yh[j], yl[j]))

        if j == 0:
            @pl.when(kind == FACTOR)
            def _():
                store(j, f_ref[pl.ds(start, CHUNK), :])


def whole(count):
    return [pl.BlockSpec(memory_space=pltpu.VMEM)] * count


def shards(points, weights, shift, cluster_rank):
    rows, cols = lax.axis_size("row"), lax.axis_size("col")
    row, col = lax.axis_index("row"), lax.axis_index("col")
    width = shift.shape[0]
    shard = jnp.concatenate([points.reshape(12, width), weights, shift[None]], 0)[:, None]
    gathered = gather_shards(shard)

    slots = jnp.arange(4, dtype=jnp.int32)
    tile_rows = row + rows * slots
    tile_cols = col + cols * slots[:2]
    wanted = jnp.concatenate([slots[:2], tile_rows, tile_cols])
    clusters = jnp.arange(cluster_rank.shape[0], dtype=jnp.int32)
    found = jnp.sum(jnp.where(cluster_rank[None, :] == wanted[:, None], clusters[None, :], 0), axis=1)
    from_row, from_x = found // 4, found % 4
    dy = (row // 2 - from_row // 2) % 4
    dc = (row % 2 - from_row % 2) % 2
    first = (dc * 4 + dy) * cols + from_x * 4
    where = (first[:, None] + slots[None, :]).reshape(-1).astype(jnp.int32)

    u, v, wr, wc = pl.pallas_call(
        prep_kernel,
        grid_spec=pltpu.PrefetchScalarGridSpec(
            num_scalar_prefetch=1,
            grid=(8,),
            in_specs=whole(1),
            out_specs=[
                pl.BlockSpec((None, QUAD, TILE, FEAT), lambda t, at: (t, 0, 0, 0)),
                pl.BlockSpec((None, QUAD, FEAT, TILE), lambda t, at: (t, 0, 0, 0)),
                pl.BlockSpec((None, TILE, 128), lambda t, at: (t, 0, 0)),
                pl.BlockSpec((None, 8, TILE), lambda t, at: (t, 0, 0)),
            ],
            scratch_shapes=[pltpu.VMEM((128, TILE), F32)],
        ),
        out_shape=[
            jax.ShapeDtypeStruct((8, QUAD, TILE, FEAT), BF16),
            jax.ShapeDtypeStruct((8, QUAD, FEAT, TILE), BF16),
            jax.ShapeDtypeStruct((8, TILE, 128), F32),
            jax.ShapeDtypeStruct((8, 8, TILE), F32),
        ],
        name="prep",
        compiler_params=pltpu.CompilerParams(vmem_limit_bytes=16 << 20),
    )(where, gathered)

    block_rows, block_cols = tile_rows[:, None], tile_cols[None, :]
    kinds = jnp.where(
        block_rows < block_cols,
        ZERO,
        jnp.where(
            block_cols >= 2,
            jnp.where(block_rows == block_cols, DIAGONAL, UPDATE),
            jnp.where(block_rows < 2, FACTOR, PANEL),
        ),
    )
    mine = row // 4
    order = jnp.arange(8, dtype=jnp.int32)
    sources = (row // 2 - order % 4) % 4 * 2 + (row % 2 - order // 4) % 2
    head = jnp.stack([mine, col + cols * mine, row % 4 * BASE])
    info = jnp.concatenate([head, kinds.reshape(-1), jnp.where((row < 2) & (col < 2), row * 2 + col, 1)[None], sources]).astype(jnp.int32)

    def geometry(left, right, held):
        return [
            pl.BlockSpec((held, QUAD, TILE, FEAT), lambda *at: (left(*at), 0, 0, 0)),
            pl.BlockSpec((2, QUAD, FEAT, TILE), lambda *at: (right, 0, 0, 0)),
            pl.BlockSpec((held, TILE, 128), lambda *at: (left(*at), 0, 0)),
            pl.BlockSpec((2, 8, TILE), lambda *at: (right, 0, 0)),
        ]

    factor, weights_part = pl.pallas_call(
        chain_kernel,
        grid_spec=pltpu.PrefetchScalarGridSpec(
            num_scalar_prefetch=1,
            grid=(1,),
            in_specs=geometry(lambda *at: 0, 0, 2)
            + [
                pl.BlockSpec((1, QUAD, FEAT, TILE), lambda i, info: (6 + info[0], 0, 0, 0)),
                pl.BlockSpec((1, 8, TILE), lambda i, info: (6 + info[0], 0, 0)),
            ],
            out_specs=[
                pl.BlockSpec((TILE, TILE), lambda i, info: (0, 0)),
                pl.BlockSpec((LEAD, BASE), lambda i, info: (0, 0)),
            ],
            scratch_shapes=[
                pltpu.VMEM((LEAD + BASE, 2 * LEAD), F32),
                pltpu.VMEM((LEAD + BASE, BASE), F32),
                pltpu.VMEM((BASE, BASE), F32),
                pltpu.VMEM((STEP, STEP, BASE), F32),
                pltpu.VMEM((STEP, STEP, BASE), F32),
                pltpu.VMEM((STEP, BASE), F32),
                pltpu.VMEM((STEP, 8, BASE), F32),
                pltpu.VMEM((2 * BASE, WINDOW + BASE), BF16),
                pltpu.VMEM((LEAD, 2 * BASE), BF16),
            ],
        ),
        out_shape=[jax.ShapeDtypeStruct((TILE, TILE), F32), jax.ShapeDtypeStruct((LEAD, BASE), F32)],
        name="chain",
        compiler_params=pltpu.CompilerParams(vmem_limit_bytes=36 << 20),
    )(info, u, v, wr, wc, v, wc)

    tall = jax.ShapeDtypeStruct((4 * TILE, LEAD), BF16)
    chunks = TILE // CHUNK

    blocked = pl.BlockSpec((CHUNK, LEAD), lambda i, h, info: (i * chunks + h, 0))

    def assembled(kernel, right, shapes, tiles, name):
        return pl.pallas_call(
            kernel,
            grid_spec=pltpu.PrefetchScalarGridSpec(
                num_scalar_prefetch=1,
                grid=(4, chunks),
                in_specs=geometry(lambda i, h, info: 2 + i, right, 1),
                out_specs=[blocked] * len(shapes),
            ),
            out_shape=shapes,
            cost_estimate=pl.CostEstimate(
                flops=tiles * 7_500_000_000, bytes_accessed=tiles * 2_000_000, transcendentals=tiles * 4_000_000
            ),
            name=name,
            compiler_params=pltpu.CompilerParams(vmem_limit_bytes=20 << 20),
        )(info, u, v, wr, wc)

    near = [send(weights_part, lambda y, c, x, z, k=k: (y + k, c, x, z), rows, cols) for k in range(1, 4)]
    panels = assembled(panel_kernel, 0, [tall] * 2, 8, "panel")
    *near, ah, al = lax.optimization_barrier((*near, *panels))
    parts = [weights_part] + near
    parts = parts + [send(part, lambda y, c, x, z: (y, c + 1, x, z), rows, cols) for part in parts]
    own = assembled(own_kernel, 3, [jax.ShapeDtypeStruct((4 * TILE, LEAD), F32)], 6, "own")
    *parts, own = lax.optimization_barrier((*parts, *own))

    lines = CHUNK * 8
    out = pl.pallas_call(
        final_kernel,
        grid_spec=pltpu.PrefetchScalarGridSpec(
            num_scalar_prefetch=1,
            grid=(4, chunks),
            in_specs=whole(9) + [blocked] * 3,
            out_specs=pl.BlockSpec((lines, 128), lambda i, h, info: (i * chunks + h, 0)),
            scratch_shapes=[pltpu.VMEM((2, LEAD, TILE), BF16)] * 2,
        ),
        out_shape=jax.ShapeDtypeStruct((4 * TILE * 8, 128), F32),
        name="final",
        compiler_params=pltpu.CompilerParams(vmem_limit_bytes=24 << 20),
    )(info, factor, *parts, ah, al, own)
    return out.reshape(4, 1, TILE, 2, 1, TILE)


def solution(mesh):
    return jax.shard_map(
        shards,
        mesh=mesh,
        in_specs=(P(None, None, ("row", "col")), P(None, ("row", "col")), P(("row", "col")), P()),
        out_specs=P(None, "row", None, None, "col", None),
        check_vma=False,
    )
```

```python
import functools

import jax
import jax.numpy as jnp
from jax import lax
from jax.experimental import pallas as pl
from jax.experimental.pallas import tpu as pltpu
from jax.sharding import PartitionSpec as P

SOFTENING_SQUARED = 0.0004
F32 = jnp.float32
BF16 = jnp.bfloat16
QUAD = 4
TILE = 512
FEAT = 48
LEAD = 1024
BASE = 128
STEP = 32
HALVES = STEP // 8
WINDOW = LEAD + BASE
HIGHEST = lax.Precision.HIGHEST


def split(value):
    high = value.astype(BF16)
    return high, (value - high.astype(F32)).astype(BF16)


def dot3(a_high, a_low, b_high, b_low):
    dot = functools.partial(jnp.dot, preferred_element_type=F32)
    return dot(a_high, b_high) + (dot(a_high, b_low) + dot(a_low, b_high))


def send(value, move, rows, cols):
    ys, xs = rows // 2, 4
    zs = cols // xs
    pairs = []
    for source in range(rows * cols):
        row, col = divmod(source, cols)
        y, core, x, z = move(row // 2, row % 2, col // zs, col % zs)
        pairs.append((source, ((y % ys) * 2 + core % 2) * cols + (x % xs) * zs + z % zs))
    return lax.ppermute(value, ("row", "col"), pairs)


def gather_shards(shard):
    rows, cols = lax.axis_size("row"), lax.axis_size("col")
    copies = jnp.broadcast_to(shard[None], (cols, *shard.shape))
    held = lax.all_to_all(copies, "col", 0, 0, tiled=True)
    moved = [held] + [send(held, lambda y, c, x, z, k=k: (y + k, c, x, z), rows, cols) for k in range(1, 4)]
    held = jnp.concatenate(moved, 0)
    return jnp.concatenate([held, send(held, lambda y, c, x, z: (y, c + 1, x, z), rows, cols)], 0)


def prep_kernel(where_ref, g_ref, u_ref, v_ref, wr_ref, wc_ref, pad):
    tile = pl.program_id(0)
    geometry = jnp.concatenate([g_ref[where_ref[4 * tile + z], :, 0, :] for z in range(4)], axis=1)
    centred = geometry[0:12] - 0.5
    coarse = jnp.floor(centred * 256.0 + 0.5) * (1.0 / 256.0)
    fine = centred - coarse
    fine_high = fine.astype(BF16).astype(F32)
    fine_low = fine - fine_high
    per = lambda value: [value[4 * c : 4 * c + 4] for c in range(3)]
    coarse, fine, fine_high, fine_low = per(coarse), per(fine), per(fine_high), per(fine_low)
    norm = sum(c * c for c in coarse)
    norm_high = jnp.floor(norm * 256.0) * (1.0 / 256.0)
    norm_low = norm - norm_high
    mixed = sum(2.0 * c * f + f * f for c, f in zip(coarse, fine))

    def pieces(value):
        first = value.astype(BF16).astype(F32)
        second = (value - first).astype(BF16).astype(F32)
        return [first, second, value - first - second]

    one = jnp.ones_like(norm)
    twice = lambda values: [-2.0 * value for value in values]
    left = twice(coarse) + [norm_high, norm_low, one, one]
    left += twice(coarse) + twice(coarse) + twice(fine_high) + twice(fine_low)
    left += twice(fine_high) + twice(fine_high) + twice(fine_low)
    left += pieces(mixed) + [one] * 3
    right = coarse + [one, one, norm_high, norm_low]
    right += fine_high + fine_low + coarse + coarse
    right += fine_high + fine_low + fine_high
    right += [one] * 3 + pieces(mixed + SOFTENING_SQUARED)
    pad[...] = jnp.zeros_like(pad)
    @pl.when(tile < 6)
    def _():
        for quad in range(QUAD):
            for k, value in enumerate(left):
                pad[k : k + 1, :] = value[quad : quad + 1, :]
            u_ref[quad] = jnp.transpose(pad[...])[:, :FEAT].astype(BF16)

    @pl.when((tile < 2) | (tile >= 6))
    def _():
        for quad in range(QUAD):
            for k, value in enumerate(right):
                pad[k : k + 1, :] = value[quad : quad + 1, :]
            v_ref[quad] = pad[0:FEAT, :].astype(BF16)

    pad[0:5, :] = geometry[12:17]
    wr_ref[...] = jnp.transpose(pad[...])
    wc_ref[0:5, :] = geometry[12:17]


def assemble(u_ref, v_ref, wr_ref, wc_ref, left, right, start, count, cols=slice(0, TILE)):
    rows = pl.ds(start, count)
    total = None
    for first in range(QUAD):
        part = None
        for second in range(QUAD):
            squared = jnp.dot(u_ref[left, first, rows, :], v_ref[right, second, :, cols], preferred_element_type=F32)
            term = lax.rsqrt(squared) * wc_ref[right, second : second + 1, cols]
            part = term if part is None else part + term
        part = part * wr_ref[left, rows, first : first + 1]
        total = part if total is None else total + part
    return total


def split3(value):
    first = value.astype(BF16)
    rest = value - first.astype(F32)
    second = rest.astype(BF16)
    return first, second, (rest - second.astype(F32)).astype(BF16)


def dot_rows(left, right):
    return lax.dot_general(left, right, (((0,), (0,)), ((), ())), preferred_element_type=F32)


def eliminate_base(work, spread, solved, lines, raw):
    lane = lax.broadcasted_iota(jnp.int32, (8, BASE), 1)
    sub = lax.broadcasted_iota(jnp.int32, (8, BASE), 0)
    repeat = lambda ref, i: ref[pl.ds(i, 8, stride=0), :]
    for step in range(BASE // STEP):
        low = step * STEP
        high = low + STEP
        a, c = [], [[] for _ in range(HALVES)]
        for half in range(HALVES):
            left = work[low + 8 * half : low + 8 * half + 8, :]
            for j in range(STEP):
                column = jnp.broadcast_to(left[:, low + j : low + j + 1], (8, BASE))
                c[half].append(column)
            inside = (lane >= low) & (lane < high)
            a.append(jnp.where(inside, jnp.where(lane == sub + (low + 8 * half), 1.0, 0.0), left))
            lines[8 * half : 8 * half + 8, :] = a[half]
        d = []
        for half in range(HALVES):
            diagonal = c[half][8 * half]
            for j in range(8 * half + 1, 8 * half + 8):
                diagonal = jnp.where(sub == j % 8, c[half][j], diagonal)
            d.append(diagonal)
            spread[0, 8 * half : 8 * half + 8, :] = diagonal
        pivot = repeat(spread.at[0], 0)
        raw[0] = c[0][0]
        for j in range(STEP):
            scale = lax.rsqrt(pivot)
            if j + 1 < STEP:
                below = repeat(raw.at[j], (j + 1) % 8)
                pivot = repeat(spread.at[j], j + 1) - (below * below) * (scale * scale)
            first = j // 8
            line = repeat(lines, j) * scale
            for half in range(first, HALVES):
                c[half][j] = c[half][j] * scale
                solved[j, 8 * half : 8 * half + 8, :] = c[half][j]
                if j + 2 < STEP:
                    d[half] = d[half] - c[half][j] * c[half][j]
                    spread[j + 1, 8 * half : 8 * half + 8, :] = d[half]
            for k in range(j + 1, STEP):
                factor = repeat(solved.at[j], k)
                for half in range(k // 8, HALVES):
                    c[half][k] = c[half][k] - c[half][j] * factor
                if k == j + 1 and k + 1 < STEP:
                    raw[k] = c[(k + 1) // 8][k]
            for half in range(first, HALVES):
                update = a[half] - c[half][j] * line
                if half == first:
                    update = jnp.where(sub > j % 8, update, jnp.where(sub == j % 8, line, a[half]))
                a[half] = update
                lines[8 * half : 8 * half + 8, :] = update
        for half in range(HALVES):
            work[low + 8 * half : low + 8 * half + 8, :] = a[half]
        if high < BASE:
            w0, w1, w2 = split3(jnp.concatenate(a, 0))
            product = dot_rows(
                jnp.concatenate([w0, w0, w1, w0, w1, w2], 0), jnp.concatenate([w0, w1, w0, w2, w1, w0], 0)
            )
            rest = lax.broadcasted_iota(jnp.int32, (BASE - high, BASE), 1)
            kept = jnp.where((rest >= low) & (rest < high), 0.0, work[high:, :])
            work[high:, :] = kept - product[high:, :]


def chain_kernel(
    info, u_ref, v_ref, wr_ref, wc_ref, vj_ref, wj_ref,
    f_ref, y_ref,
    state, side, work, spread, solved, lines, raw, stack, tall,
):
    state[:, LEAD:] = jnp.zeros((LEAD + BASE, LEAD), F32)
    state[LEAD:, :LEAD] = jnp.zeros((BASE, LEAD), F32)
    side[LEAD:, :] = jnp.zeros((BASE, BASE), F32)
    lane = lax.broadcasted_iota(jnp.int32, (BASE, BASE), 1)
    row = lax.broadcasted_iota(jnp.int32, (BASE, BASE), 0)
    eye = (row == lane).astype(F32)
    geometry = (u_ref, v_ref, wr_ref, wc_ref)
    column = info[1]
    offset = pl.multiple_of(info[2], BASE)

    @pl.loop(0, TILE // 256)
    def _(chunk):
        start = pl.multiple_of(chunk * 256, 256)
        rows = pl.ds(start, 256)
        for tile in range(2):
            here = pl.ds(pl.multiple_of(tile * TILE + start, 256), 256)
            low = tile * TILE
            values = assemble(*geometry, tile, tile, start, 256, slice(256, TILE))
            line = start + lax.broadcasted_iota(jnp.int32, (256, 256), 0)
            across = 256 + lax.broadcasted_iota(jnp.int32, (256, 256), 1)
            values = values + jnp.where(line == across, wr_ref[tile, rows, 4:5], 0.0)
            state[here, low + 256 : low + TILE] = values
            side[here, :] = assemble(u_ref, vj_ref, wr_ref, wj_ref, tile, 0, start, 256, pl.ds(offset, BASE))
        state[rows, TILE : 2 * TILE] = assemble(*geometry, 0, 1, start, 256)

    for tile in range(2):
        values = assemble(*geometry, tile, tile, 0, 256, slice(0, 256))
        line = lax.broadcasted_iota(jnp.int32, (256, 256), 0)
        across = lax.broadcasted_iota(jnp.int32, (256, 256), 1)
        values = values + jnp.where(line == across, wr_ref[tile, 0:256, 4:5], 0.0)
        state[tile * TILE : tile * TILE + 256, tile * TILE : tile * TILE + 256] = values

    blocks = LEAD // BASE
    both = jnp.concatenate
    dot = functools.partial(jnp.dot, preferred_element_type=F32)

    @pl.loop(0, blocks)
    def _(k):
        here = pl.multiple_of(k * BASE, BASE)
        rows = pl.ds(here, BASE)
        state[rows, pl.ds(pl.multiple_of(LEAD + here, BASE), BASE)] = eye
        work[...] = state[rows, pl.ds(here, BASE)]
        eliminate_base(work, spread, solved, lines, raw)
        l0, l1 = split(jnp.where(row >= lane, work[...], 0.0))
        window = pl.ds(here, WINDOW)

        def load(values):
            first, second = split(values)
            stack[0:128, :] = first
            stack[128:256, :] = second

        load(both([state[rows, window], side[rows, :]], 1))
        done = dot(both([l0, l0], 1), stack[...]) + dot(l1, stack[0:128, :])
        state[rows, window] = done[:, :WINDOW]
        side[rows, :] = done[:, WINDOW:]
        load(done)

        @pl.loop(0, blocks - 1 - k)
        def _(i):
            there = pl.multiple_of((i + 1) * BASE, BASE)
            parts = split(jnp.transpose(state[rows, pl.ds(pl.multiple_of(here + there, BASE), BASE)]))
            for n, part in enumerate(parts):
                tall[pl.ds(pl.multiple_of(i * BASE, BASE), BASE), n * 128 : n * 128 + 128] = part

        for pair in range(blocks // 2):
            @pl.when(pair < (blocks - k) // 2)
            def _():
                skip = pair * 256 + BASE
                below = pl.ds(pl.multiple_of(here + skip, BASE), 256)
                t0, t1 = [tall[pair * 256 : pair * 256 + 256, n * 128 : n * 128 + 128] for n in range(2)]
                update = dot(both([t0, t0], 1), stack[:, skip:]) + dot(t1, stack[0:128, skip:])
                width = WINDOW - skip
                into = pl.ds(pl.multiple_of(here + skip, BASE), width)
                state[below, into] = state[below, into] - update[:, :width]
                side[below, :] = side[below, :] - update[:, width:]

    which = info[11]

    @pl.when((which == 0) | (which == 2) | (which == 3))
    def _():
        from_rows = pl.ds(pl.multiple_of(which % 2 * TILE, TILE), TILE)
        for chunk in range(TILE // BASE):
            from_cols = pl.ds(pl.multiple_of(which // 2 * TILE + chunk * BASE, BASE), BASE)
            values = jnp.transpose(state[from_rows, from_cols])
            line = chunk * BASE + lax.broadcasted_iota(jnp.int32, (BASE, TILE), 0)
            across = lax.broadcasted_iota(jnp.int32, (BASE, TILE), 1)
            keep = (line >= across) | (which == 2)
            f_ref[chunk * BASE : chunk * BASE + BASE, :] = jnp.where(keep, values, 0.0)

    @pl.when(column < 2)
    def _():
        line = lax.broadcasted_iota(jnp.int32, (LEAD, BASE), 0)
        across = lax.broadcasted_iota(jnp.int32, (LEAD, BASE), 1)
        side[:LEAD, :] = jnp.where(line == across + (column * TILE + offset), -1.0, 0.0)

    for out in range(4):
        total = jnp.zeros((256, BASE), F32)
        for part in range(out, 4):
            rows = slice(part * 256, part * 256 + 256)
            factor = jnp.transpose(state[rows, LEAD + out * 256 : LEAD + out * 256 + 256])
            high, low = split(factor)
            z_high, z_low = split(side[rows, :])
            wide = dot(high, both([z_high, z_low], 1))
            total = total + (wide[:, :BASE] + (wide[:, BASE:] + dot(low, z_high)))
        y_ref[out * 256 : out * 256 + 256, :] = total


def panel_kernel(info, u_ref, v_ref, wr_ref, wc_ref, ah_ref, al_ref):
    slot, chunk = pl.program_id(0), pl.program_id(1)
    start = pl.multiple_of(chunk * CHUNK, CHUNK)
    kinds = [info[3 + slot * 2], info[4 + slot * 2]]
    needed = lambda kind: (kind != ZERO) & (kind != FACTOR)

    @pl.when(needed(kinds[0]) | needed(kinds[1]))
    def _():
        for half in range(2):
            values = assemble(u_ref, v_ref, wr_ref, wc_ref, 0, half, start, CHUNK)
            cols = slice(half * TILE, half * TILE + TILE)
            ah_ref[:, cols], al_ref[:, cols] = split(values)


def own_kernel(info, u_ref, v_ref, wr_ref, wc_ref, own_ref):
    slot, chunk = pl.program_id(0), pl.program_id(1)
    start = pl.multiple_of(chunk * CHUNK, CHUNK)
    for j in range(2):
        kind = info[3 + slot * 2 + j]

        @pl.when((kind == UPDATE) | (kind == DIAGONAL))
        def _():
            values = assemble(u_ref, v_ref, wr_ref, wc_ref, 0, j, start, CHUNK)
            row = start + lax.broadcasted_iota(jnp.int32, (CHUNK, TILE), 0)
            col = lax.broadcasted_iota(jnp.int32, (CHUNK, TILE), 1)
            shift = wr_ref[0, pl.ds(start, CHUNK), 4:5]
            values = values + jnp.where((row == col) & (kind == DIAGONAL), shift, 0.0)
            own_ref[:, j * TILE : j * TILE + TILE] = values


CHUNK = 256
ZERO, UPDATE, DIAGONAL, PANEL, FACTOR = range(5)


def final_kernel(info, f_ref, *rest):
    parts, (ah, al, own, out_ref, yh, yl) = rest[:8], rest[8:]
    slot, chunk = pl.program_id(0), pl.program_id(1)
    start = pl.multiple_of(chunk * CHUNK, CHUNK)
    rows = pl.ds(pl.multiple_of(slot * TILE + start, CHUNK), CHUNK)
    kinds = [info[3 + slot * 2], info[4 + slot * 2]]

    @pl.when((slot == 0) & (chunk == 0))
    def _():
        for p, part in enumerate(parts):
            source = info[12 + p]
            lanes = pl.ds(pl.multiple_of(source % 4 * 128, 128), 128)
            yh[source // 4, :, lanes], yl[source // 4, :, lanes] = split(part[...])

    def store(j, values):
        for q in range(TILE // 128):
            out_ref[pl.ds(j * 4 + q, CHUNK, stride=8), :] = values[:, q * 128 : (q + 1) * 128]

    for j in range(2):
        kind = kinds[j]

        @pl.when(kind == ZERO)
        def _():
            store(j, jnp.zeros((CHUNK, TILE), F32))

        @pl.when(kind == PANEL)
        def _():
            store(j, -dot3(ah[rows, :], al[rows, :], yh[j], yl[j]))

        @pl.when((kind == UPDATE) | (kind == DIAGONAL))
        def _():
            values = own[rows, j * TILE : j * TILE + TILE]
            store(j, values - dot3(ah[rows, :], al[rows, :], yh[j], yl[j]))

        if j == 0:
            @pl.when(kind == FACTOR)
            def _():
                store(j, f_ref[pl.ds(start, CHUNK), :])


def whole(count):
    return [pl.BlockSpec(memory_space=pltpu.VMEM)] * count


def shards(points, weights, shift, cluster_rank):
    rows, cols = lax.axis_size("row"), lax.axis_size("col")
    row, col = lax.axis_index("row"), lax.axis_index("col")
    width = shift.shape[0]
    shard = jnp.concatenate([points.reshape(12, width), weights, shift[None]], 0)[:, None]
    gathered = gather_shards(shard)

    slots = jnp.arange(4, dtype=jnp.int32)
    tile_rows = row + rows * slots
    tile_cols = col + cols * slots[:2]
    wanted = jnp.concatenate([slots[:2], tile_rows, tile_cols])
    clusters = jnp.arange(cluster_rank.shape[0], dtype=jnp.int32)
    found = jnp.sum(jnp.where(cluster_rank[None, :] == wanted[:, None], clusters[None, :], 0), axis=1)
    from_row, from_x = found // 4, found % 4
    dy = (row // 2 - from_row // 2) % 4
    dc = (row % 2 - from_row % 2) % 2
    first = (dc * 4 + dy) * cols + from_x * 4
    where = (first[:, None] + slots[None, :]).reshape(-1).astype(jnp.int32)

    u, v, wr, wc = pl.pallas_call(
        prep_kernel,
        grid_spec=pltpu.PrefetchScalarGridSpec(
            num_scalar_prefetch=1,
            grid=(8,),
            in_specs=whole(1),
            out_specs=[
                pl.BlockSpec((None, QUAD, TILE, FEAT), lambda t, at: (t, 0, 0, 0)),
                pl.BlockSpec((None, QUAD, FEAT, TILE), lambda t, at: (t, 0, 0, 0)),
                pl.BlockSpec((None, TILE, 128), lambda t, at: (t, 0, 0)),
                pl.BlockSpec((None, 8, TILE), lambda t, at: (t, 0, 0)),
            ],
            scratch_shapes=[pltpu.VMEM((128, TILE), F32)],
        ),
        out_shape=[
            jax.ShapeDtypeStruct((8, QUAD, TILE, FEAT), BF16),
            jax.ShapeDtypeStruct((8, QUAD, FEAT, TILE), BF16),
            jax.ShapeDtypeStruct((8, TILE, 128), F32),
            jax.ShapeDtypeStruct((8, 8, TILE), F32),
        ],
        name="prep",
        compiler_params=pltpu.CompilerParams(vmem_limit_bytes=16 << 20),
    )(where, gathered)

    block_rows, block_cols = tile_rows[:, None], tile_cols[None, :]
    kinds = jnp.where(
        block_rows < block_cols,
        ZERO,
        jnp.where(
            block_cols >= 2,
            jnp.where(block_rows == block_cols, DIAGONAL, UPDATE),
            jnp.where(block_rows < 2, FACTOR, PANEL),
        ),
    )
    mine = row // 4
    order = jnp.arange(8, dtype=jnp.int32)
    sources = (row // 2 - order % 4) % 4 * 2 + (row % 2 - order // 4) % 2
    head = jnp.stack([mine, col + cols * mine, row % 4 * BASE])
    info = jnp.concatenate([head, kinds.reshape(-1), jnp.where((row < 2) & (col < 2), row * 2 + col, 1)[None], sources]).astype(jnp.int32)

    def geometry(left, right, held):
        return [
            pl.BlockSpec((held, QUAD, TILE, FEAT), lambda *at: (left(*at), 0, 0, 0)),
            pl.BlockSpec((2, QUAD, FEAT, TILE), lambda *at: (right, 0, 0, 0)),
            pl.BlockSpec((held, TILE, 128), lambda *at: (left(*at), 0, 0)),
            pl.BlockSpec((2, 8, TILE), lambda *at: (right, 0, 0)),
        ]

    factor, weights_part = pl.pallas_call(
        chain_kernel,
        grid_spec=pltpu.PrefetchScalarGridSpec(
            num_scalar_prefetch=1,
            grid=(1,),
            in_specs=geometry(lambda *at: 0, 0, 2)
            + [
                pl.BlockSpec((1, QUAD, FEAT, TILE), lambda i, info: (6 + info[0], 0, 0, 0)),
                pl.BlockSpec((1, 8, TILE), lambda i, info: (6 + info[0], 0, 0)),
            ],
            out_specs=[
                pl.BlockSpec((TILE, TILE), lambda i, info: (0, 0)),
                pl.BlockSpec((LEAD, BASE), lambda i, info: (0, 0)),
            ],
            scratch_shapes=[
                pltpu.VMEM((LEAD + BASE, 2 * LEAD), F32),
                pltpu.VMEM((LEAD + BASE, BASE), F32),
                pltpu.VMEM((BASE, BASE), F32),
                pltpu.VMEM((STEP, STEP, BASE), F32),
                pltpu.VMEM((STEP, STEP, BASE), F32),
                pltpu.VMEM((STEP, BASE), F32),
                pltpu.VMEM((STEP, 8, BASE), F32),
                pltpu.VMEM((2 * BASE, WINDOW + BASE), BF16),
                pltpu.VMEM((LEAD, 2 * BASE), BF16),
            ],
        ),
        out_shape=[jax.ShapeDtypeStruct((TILE, TILE), F32), jax.ShapeDtypeStruct((LEAD, BASE), F32)],
        name="chain",
        compiler_params=pltpu.CompilerParams(vmem_limit_bytes=36 << 20),
    )(info, u, v, wr, wc, v, wc)

    tall = jax.ShapeDtypeStruct((4 * TILE, LEAD), BF16)
    chunks = TILE // CHUNK

    blocked = pl.BlockSpec((CHUNK, LEAD), lambda i, h, info: (i * chunks + h, 0))

    def assembled(kernel, right, shapes, tiles, name):
        return pl.pallas_call(
            kernel,
            grid_spec=pltpu.PrefetchScalarGridSpec(
                num_scalar_prefetch=1,
                grid=(4, chunks),
                in_specs=geometry(lambda i, h, info: 2 + i, right, 1),
                out_specs=[blocked] * len(shapes),
            ),
            out_shape=shapes,
            cost_estimate=pl.CostEstimate(
                flops=tiles * 7_500_000_000, bytes_accessed=tiles * 2_000_000, transcendentals=tiles * 4_000_000
            ),
            name=name,
            compiler_params=pltpu.CompilerParams(vmem_limit_bytes=20 << 20),
        )(info, u, v, wr, wc)

    near = [send(weights_part, lambda y, c, x, z, k=k: (y + k, c, x, z), rows, cols) for k in range(1, 4)]
    panels = assembled(panel_kernel, 0, [tall] * 2, 8, "panel")
    *near, ah, al = lax.optimization_barrier((*near, *panels))
    parts = [weights_part] + near
    parts = parts + [send(part, lambda y, c, x, z: (y, c + 1, x, z), rows, cols) for part in parts]
    own = assembled(own_kernel, 3, [jax.ShapeDtypeStruct((4 * TILE, LEAD), F32)], 6, "own")
    *parts, own = lax.optimization_barrier((*parts, *own))

    lines = CHUNK * 8
    out = pl.pallas_call(
        final_kernel,
        grid_spec=pltpu.PrefetchScalarGridSpec(
            num_scalar_prefetch=1,
            grid=(4, chunks),
            in_specs=whole(12),
            out_specs=pl.BlockSpec((lines, 128), lambda i, h, info: (i * chunks + h, 0)),
            scratch_shapes=[pltpu.VMEM((2, LEAD, TILE), BF16)] * 2,
        ),
        out_shape=jax.ShapeDtypeStruct((4 * TILE * 8, 128), F32),
        name="final",
        compiler_params=pltpu.CompilerParams(vmem_limit_bytes=24 << 20),
    )(info, factor, *parts, ah, al, own)
    return out.reshape(4, 1, TILE, 2, 1, TILE)


def solution(mesh):
    return jax.shard_map(
        shards,
        mesh=mesh,
        in_specs=(P(None, None, ("row", "col")), P(None, ("row", "col")), P(("row", "col")), P()),
        out_specs=P(None, "row", None, None, "col", None),
        check_vma=False,
    )
```

```python
import functools

import jax
import jax.numpy as jnp
from jax import lax
from jax.experimental import pallas as pl
from jax.experimental.pallas import tpu as pltpu
from jax.sharding import PartitionSpec as P

SOFTENING_SQUARED = 0.0004
F32 = jnp.float32
BF16 = jnp.bfloat16
QUAD = 4
TILE = 512
FEAT = 48
LEAD = 1024
BASE = 128
STEP = 32
HALVES = STEP // 8
WINDOW = LEAD + BASE
HIGHEST = lax.Precision.HIGHEST


def split(value):
    high = value.astype(BF16)
    return high, (value - high.astype(F32)).astype(BF16)


def dot3(a_high, a_low, b_high, b_low):
    dot = functools.partial(jnp.dot, preferred_element_type=F32)
    return dot(a_high, b_high) + (dot(a_high, b_low) + dot(a_low, b_high))


def send(value, move, rows, cols):
    ys, xs = rows // 2, 4
    zs = cols // xs
    pairs = []
    for source in range(rows * cols):
        row, col = divmod(source, cols)
        y, core, x, z = move(row // 2, row % 2, col // zs, col % zs)
        pairs.append((source, ((y % ys) * 2 + core % 2) * cols + (x % xs) * zs + z % zs))
    return lax.ppermute(value, ("row", "col"), pairs)


def gather_shards(shard):
    rows, cols = lax.axis_size("row"), lax.axis_size("col")
    copies = jnp.broadcast_to(shard[None], (cols, *shard.shape))
    held = lax.all_to_all(copies, "col", 0, 0, tiled=True)
    moved = [held] + [send(held, lambda y, c, x, z, k=k: (y + k, c, x, z), rows, cols) for k in range(1, 4)]
    held = jnp.concatenate(moved, 0)
    return jnp.concatenate([held, send(held, lambda y, c, x, z: (y, c + 1, x, z), rows, cols)], 0)


def prep_kernel(where_ref, g_ref, u_ref, v_ref, wr_ref, wc_ref, pad):
    tile = pl.program_id(0)
    geometry = jnp.concatenate([g_ref[where_ref[4 * tile + z], :, 0, :] for z in range(4)], axis=1)
    centred = geometry[0:12] - 0.5
    coarse = jnp.floor(centred * 256.0 + 0.5) * (1.0 / 256.0)
    fine = centred - coarse
    fine_high = fine.astype(BF16).astype(F32)
    fine_low = fine - fine_high
    per = lambda value: [value[4 * c : 4 * c + 4] for c in range(3)]
    coarse, fine, fine_high, fine_low = per(coarse), per(fine), per(fine_high), per(fine_low)
    norm = sum(c * c for c in coarse)
    norm_high = jnp.floor(norm * 256.0) * (1.0 / 256.0)
    norm_low = norm - norm_high
    mixed = sum(2.0 * c * f + f * f for c, f in zip(coarse, fine))

    def pieces(value):
        first = value.astype(BF16).astype(F32)
        second = (value - first).astype(BF16).astype(F32)
        return [first, second, value - first - second]

    one = jnp.ones_like(norm)
    twice = lambda values: [-2.0 * value for value in values]
    left = twice(coarse) + [norm_high, norm_low, one, one]
    left += twice(coarse) + twice(coarse) + twice(fine_high) + twice(fine_low)
    left += twice(fine_high) + twice(fine_high) + twice(fine_low)
    left += pieces(mixed) + [one] * 3
    right = coarse + [one, one, norm_high, norm_low]
    right += fine_high + fine_low + coarse + coarse
    right += fine_high + fine_low + fine_high
    right += [one] * 3 + pieces(mixed + SOFTENING_SQUARED)
    pad[...] = jnp.zeros_like(pad)
    @pl.when(tile < 6)
    def _():
        for quad in range(QUAD):
            for k, value in enumerate(left):
                pad[k : k + 1, :] = value[quad : quad + 1, :]
            u_ref[quad] = jnp.transpose(pad[...])[:, :FEAT].astype(BF16)

    @pl.when((tile < 2) | (tile >= 6))
    def _():
        for quad in range(QUAD):
            for k, value in enumerate(right):
                pad[k : k + 1, :] = value[quad : quad + 1, :]
            v_ref[quad] = pad[0:FEAT, :].astype(BF16)

    pad[0:5, :] = geometry[12:17]
    wr_ref[...] = jnp.transpose(pad[...])
    wc_ref[0:5, :] = geometry[12:17]


def assemble(u_ref, v_ref, wr_ref, wc_ref, left, right, start, count, cols=slice(0, TILE)):
    rows = pl.ds(start, count)
    total = None
    for first in range(QUAD):
        part = None
        for second in range(QUAD):
            squared = jnp.dot(u_ref[left, first, rows, :], v_ref[right, second, :, cols], preferred_element_type=F32)
            term = lax.rsqrt(squared) * wc_ref[right, second : second + 1, cols]
            part = term if part is None else part + term
        part = part * wr_ref[left, rows, first : first + 1]
        total = part if total is None else total + part
    return total


def split3(value):
    first = value.astype(BF16)
    rest = value - first.astype(F32)
    second = rest.astype(BF16)
    return first, second, (rest - second.astype(F32)).astype(BF16)


def dot_rows(left, right):
    return lax.dot_general(left, right, (((0,), (0,)), ((), ())), preferred_element_type=F32)


def eliminate_base(work, spread, solved, lines, raw):
    lane = lax.broadcasted_iota(jnp.int32, (8, BASE), 1)
    sub = lax.broadcasted_iota(jnp.int32, (8, BASE), 0)
    repeat = lambda ref, i: ref[pl.ds(i, 8, stride=0), :]
    for step in range(BASE // STEP):
        low = step * STEP
        high = low + STEP
        a, c = [], [[] for _ in range(HALVES)]
        for half in range(HALVES):
            left = work[low + 8 * half : low + 8 * half + 8, :]
            for j in range(STEP):
                column = jnp.broadcast_to(left[:, low + j : low + j + 1], (8, BASE))
                c[half].append(column)
            inside = (lane >= low) & (lane < high)
            a.append(jnp.where(inside, jnp.where(lane == sub + (low + 8 * half), 1.0, 0.0), left))
            lines[8 * half : 8 * half + 8, :] = a[half]
        d = []
        for half in range(HALVES):
            diagonal = c[half][8 * half]
            for j in range(8 * half + 1, 8 * half + 8):
                diagonal = jnp.where(sub == j % 8, c[half][j], diagonal)
            d.append(diagonal)
            spread[0, 8 * half : 8 * half + 8, :] = diagonal
        pivot = repeat(spread.at[0], 0)
        raw[0] = c[0][0]
        for j in range(STEP):
            scale = lax.rsqrt(pivot)
            if j + 1 < STEP:
                below = repeat(raw.at[j], (j + 1) % 8)
                pivot = repeat(spread.at[j], j + 1) - (below * below) * (scale * scale)
            first = j // 8
            line = repeat(lines, j) * scale
            for half in range(first, HALVES):
                c[half][j] = c[half][j] * scale
                solved[j, 8 * half : 8 * half + 8, :] = c[half][j]
                if j + 2 < STEP:
                    d[half] = d[half] - c[half][j] * c[half][j]
                    spread[j + 1, 8 * half : 8 * half + 8, :] = d[half]
            for k in range(j + 1, STEP):
                factor = repeat(solved.at[j], k)
                for half in range(k // 8, HALVES):
                    c[half][k] = c[half][k] - c[half][j] * factor
                if k == j + 1 and k + 1 < STEP:
                    raw[k] = c[(k + 1) // 8][k]
            for half in range(first, HALVES):
                update = a[half] - c[half][j] * line
                if half == first:
                    update = jnp.where(sub > j % 8, update, jnp.where(sub == j % 8, line, a[half]))
                a[half] = update
                lines[8 * half : 8 * half + 8, :] = update
        for half in range(HALVES):
            work[low + 8 * half : low + 8 * half + 8, :] = a[half]
        if high < BASE:
            w0, w1, w2 = split3(jnp.concatenate(a, 0))
            product = dot_rows(
                jnp.concatenate([w0, w0, w1, w0, w1, w2], 0), jnp.concatenate([w0, w1, w0, w2, w1, w0], 0)
            )
            rest = lax.broadcasted_iota(jnp.int32, (BASE - high, BASE), 1)
            kept = jnp.where((rest >= low) & (rest < high), 0.0, work[high:, :])
            work[high:, :] = kept - product[high:, :]


def chain_kernel(
    info, u_ref, v_ref, wr_ref, wc_ref, vj_ref, wj_ref,
    f_ref, y_ref,
    state, side, work, spread, solved, lines, raw, stack, tall,
):
    state[:, LEAD:] = jnp.zeros((LEAD + BASE, LEAD), F32)
    state[LEAD:, :LEAD] = jnp.zeros((BASE, LEAD), F32)
    side[LEAD:, :] = jnp.zeros((BASE, BASE), F32)
    lane = lax.broadcasted_iota(jnp.int32, (BASE, BASE), 1)
    row = lax.broadcasted_iota(jnp.int32, (BASE, BASE), 0)
    eye = (row == lane).astype(F32)
    geometry = (u_ref, v_ref, wr_ref, wc_ref)
    column = info[1]
    offset = pl.multiple_of(info[2], BASE)

    @pl.loop(0, TILE // 256)
    def _(chunk):
        start = pl.multiple_of(chunk * 256, 256)
        rows = pl.ds(start, 256)
        for tile in range(2):
            here = pl.ds(pl.multiple_of(tile * TILE + start, 256), 256)
            low = tile * TILE
            values = assemble(*geometry, tile, tile, start, 256, slice(256, TILE))
            line = start + lax.broadcasted_iota(jnp.int32, (256, 256), 0)
            across = 256 + lax.broadcasted_iota(jnp.int32, (256, 256), 1)
            values = values + jnp.where(line == across, wr_ref[tile, rows, 4:5], 0.0)
            state[here, low + 256 : low + TILE] = values
            side[here, :] = assemble(u_ref, vj_ref, wr_ref, wj_ref, tile, 0, start, 256, pl.ds(offset, BASE))
        state[rows, TILE : 2 * TILE] = assemble(*geometry, 0, 1, start, 256)

    for tile in range(2):
        values = assemble(*geometry, tile, tile, 0, 256, slice(0, 256))
        line = lax.broadcasted_iota(jnp.int32, (256, 256), 0)
        across = lax.broadcasted_iota(jnp.int32, (256, 256), 1)
        values = values + jnp.where(line == across, wr_ref[tile, 0:256, 4:5], 0.0)
        state[tile * TILE : tile * TILE + 256, tile * TILE : tile * TILE + 256] = values

    blocks = LEAD // BASE
    both = jnp.concatenate
    dot = functools.partial(jnp.dot, preferred_element_type=F32)

    @pl.loop(0, blocks)
    def _(k):
        here = pl.multiple_of(k * BASE, BASE)
        rows = pl.ds(here, BASE)
        state[rows, pl.ds(pl.multiple_of(LEAD + here, BASE), BASE)] = eye
        work[...] = state[rows, pl.ds(here, BASE)]
        eliminate_base(work, spread, solved, lines, raw)
        l0, l1 = split(jnp.where(row >= lane, work[...], 0.0))
        window = pl.ds(here, WINDOW)

        def load(values):
            first, second = split(values)
            stack[0:128, :] = first
            stack[128:256, :] = second

        load(both([state[rows, window], side[rows, :]], 1))
        done = dot(both([l0, l0], 1), stack[...]) + dot(l1, stack[0:128, :])
        state[rows, window] = done[:, :WINDOW]
        side[rows, :] = done[:, WINDOW:]
        load(done)

        @pl.loop(0, blocks - 1 - k)
        def _(i):
            there = pl.multiple_of((i + 1) * BASE, BASE)
            parts = split(jnp.transpose(state[rows, pl.ds(pl.multiple_of(here + there, BASE), BASE)]))
            for n, part in enumerate(parts):
                tall[pl.ds(pl.multiple_of(i * BASE, BASE), BASE), n * 128 : n * 128 + 128] = part

        for pair in range(blocks // 2):
            @pl.when(pair < (blocks - k) // 2)
            def _():
                skip = pair * 256 + BASE
                below = pl.ds(pl.multiple_of(here + skip, BASE), 256)
                t0, t1 = [tall[pair * 256 : pair * 256 + 256, n * 128 : n * 128 + 128] for n in range(2)]
                update = dot(both([t0, t0], 1), stack[:, skip:]) + dot(t1, stack[0:128, skip:])
                width = WINDOW - skip
                into = pl.ds(pl.multiple_of(here + skip, BASE), width)
                state[below, into] = state[below, into] - update[:, :width]
                side[below, :] = side[below, :] - update[:, width:]

    which = info[11]

    @pl.when((which == 0) | (which == 2) | (which == 3))
    def _():
        from_rows = pl.ds(pl.multiple_of(which % 2 * TILE, TILE), TILE)
        for chunk in range(TILE // BASE):
            from_cols = pl.ds(pl.multiple_of(which // 2 * TILE + chunk * BASE, BASE), BASE)
            values = jnp.transpose(state[from_rows, from_cols])
            line = chunk * BASE + lax.broadcasted_iota(jnp.int32, (BASE, TILE), 0)
            across = lax.broadcasted_iota(jnp.int32, (BASE, TILE), 1)
            keep = (line >= across) | (which == 2)
            f_ref[chunk * BASE : chunk * BASE + BASE, :] = jnp.where(keep, values, 0.0)

    @pl.when(column < 2)
    def _():
        line = lax.broadcasted_iota(jnp.int32, (LEAD, BASE), 0)
        across = lax.broadcasted_iota(jnp.int32, (LEAD, BASE), 1)
        side[:LEAD, :] = jnp.where(line == across + (column * TILE + offset), -1.0, 0.0)

    for out in range(4):
        total = jnp.zeros((256, BASE), F32)
        for part in range(out, 4):
            rows = slice(part * 256, part * 256 + 256)
            factor = jnp.transpose(state[rows, LEAD + out * 256 : LEAD + out * 256 + 256])
            high, low = split(factor)
            z_high, z_low = split(side[rows, :])
            wide = dot(high, both([z_high, z_low], 1))
            total = total + (wide[:, :BASE] + (wide[:, BASE:] + dot(low, z_high)))
        y_ref[out * 256 : out * 256 + 256, :] = total


def panel_kernel(info, u_ref, v_ref, wr_ref, wc_ref, ah_ref, al_ref):
    slot, chunk = pl.program_id(0), pl.program_id(1)
    start = pl.multiple_of(chunk * CHUNK, CHUNK)
    kinds = [info[3 + slot * 2], info[4 + slot * 2]]
    needed = lambda kind: (kind != ZERO) & (kind != FACTOR)

    @pl.when(needed(kinds[0]) | needed(kinds[1]))
    def _():
        for half in range(2):
            values = assemble(u_ref, v_ref, wr_ref, wc_ref, 0, half, start, CHUNK)
            cols = slice(half * TILE, half * TILE + TILE)
            ah_ref[:, cols], al_ref[:, cols] = split(values)


def own_kernel(info, u_ref, v_ref, wr_ref, wc_ref, own_ref):
    slot, chunk = pl.program_id(0), pl.program_id(1)
    start = pl.multiple_of(chunk * CHUNK, CHUNK)
    for j in range(2):
        kind = info[3 + slot * 2 + j]

        @pl.when((kind == UPDATE) | (kind == DIAGONAL))
        def _():
            values = assemble(u_ref, v_ref, wr_ref, wc_ref, 0, j, start, CHUNK)
            row = start + lax.broadcasted_iota(jnp.int32, (CHUNK, TILE), 0)
            col = lax.broadcasted_iota(jnp.int32, (CHUNK, TILE), 1)
            shift = wr_ref[0, pl.ds(start, CHUNK), 4:5]
            values = values + jnp.where((row == col) & (kind == DIAGONAL), shift, 0.0)
            own_ref[:, j * TILE : j * TILE + TILE] = values


CHUNK = 256
ROWS = 512
ZERO, UPDATE, DIAGONAL, PANEL, FACTOR = range(5)


def final_kernel(info, f_ref, *rest):
    parts, (ah, al, own, out_ref, yh, yl) = rest[:8], rest[8:]
    slot, chunk = pl.program_id(0), pl.program_id(1)
    start = pl.multiple_of(chunk * ROWS, ROWS)
    rows = pl.ds(pl.multiple_of(slot * TILE + start, ROWS), ROWS)
    kinds = [info[3 + slot * 2], info[4 + slot * 2]]

    @pl.when((slot == 0) & (chunk == 0))
    def _():
        for p, part in enumerate(parts):
            source = info[12 + p]
            lanes = pl.ds(pl.multiple_of(source % 4 * 128, 128), 128)
            yh[source // 4, :, lanes], yl[source // 4, :, lanes] = split(part[...])

    def store(j, values):
        for q in range(TILE // 128):
            out_ref[pl.ds(j * 4 + q, ROWS, stride=8), :] = values[:, q * 128 : (q + 1) * 128]

    for j in range(2):
        kind = kinds[j]

        @pl.when(kind == ZERO)
        def _():
            store(j, jnp.zeros((ROWS, TILE), F32))

        @pl.when(kind == PANEL)
        def _():
            store(j, -dot3(ah[rows, :], al[rows, :], yh[j], yl[j]))

        @pl.when((kind == UPDATE) | (kind == DIAGONAL))
        def _():
            values = own[rows, j * TILE : j * TILE + TILE]
            store(j, values - dot3(ah[rows, :], al[rows, :], yh[j], yl[j]))

        if j == 0:
            @pl.when(kind == FACTOR)
            def _():
                store(j, f_ref[pl.ds(start, ROWS), :])


def whole(count):
    return [pl.BlockSpec(memory_space=pltpu.VMEM)] * count


def shards(points, weights, shift, cluster_rank):
    rows, cols = lax.axis_size("row"), lax.axis_size("col")
    row, col = lax.axis_index("row"), lax.axis_index("col")
    width = shift.shape[0]
    shard = jnp.concatenate([points.reshape(12, width), weights, shift[None]], 0)[:, None]
    gathered = gather_shards(shard)

    slots = jnp.arange(4, dtype=jnp.int32)
    tile_rows = row + rows * slots
    tile_cols = col + cols * slots[:2]
    wanted = jnp.concatenate([slots[:2], tile_rows, tile_cols])
    clusters = jnp.arange(cluster_rank.shape[0], dtype=jnp.int32)
    found = jnp.sum(jnp.where(cluster_rank[None, :] == wanted[:, None], clusters[None, :], 0), axis=1)
    from_row, from_x = found // 4, found % 4
    dy = (row // 2 - from_row // 2) % 4
    dc = (row % 2 - from_row % 2) % 2
    first = (dc * 4 + dy) * cols + from_x * 4
    where = (first[:, None] + slots[None, :]).reshape(-1).astype(jnp.int32)

    u, v, wr, wc = pl.pallas_call(
        prep_kernel,
        grid_spec=pltpu.PrefetchScalarGridSpec(
            num_scalar_prefetch=1,
            grid=(8,),
            in_specs=whole(1),
            out_specs=[
                pl.BlockSpec((None, QUAD, TILE, FEAT), lambda t, at: (t, 0, 0, 0)),
                pl.BlockSpec((None, QUAD, FEAT, TILE), lambda t, at: (t, 0, 0, 0)),
                pl.BlockSpec((None, TILE, 128), lambda t, at: (t, 0, 0)),
                pl.BlockSpec((None, 8, TILE), lambda t, at: (t, 0, 0)),
            ],
            scratch_shapes=[pltpu.VMEM((128, TILE), F32)],
        ),
        out_shape=[
            jax.ShapeDtypeStruct((8, QUAD, TILE, FEAT), BF16),
            jax.ShapeDtypeStruct((8, QUAD, FEAT, TILE), BF16),
            jax.ShapeDtypeStruct((8, TILE, 128), F32),
            jax.ShapeDtypeStruct((8, 8, TILE), F32),
        ],
        name="prep",
        compiler_params=pltpu.CompilerParams(vmem_limit_bytes=16 << 20),
    )(where, gathered)

    block_rows, block_cols = tile_rows[:, None], tile_cols[None, :]
    kinds = jnp.where(
        block_rows < block_cols,
        ZERO,
        jnp.where(
            block_cols >= 2,
            jnp.where(block_rows == block_cols, DIAGONAL, UPDATE),
            jnp.where(block_rows < 2, FACTOR, PANEL),
        ),
    )
    mine = row // 4
    order = jnp.arange(8, dtype=jnp.int32)
    sources = (row // 2 - order % 4) % 4 * 2 + (row % 2 - order // 4) % 2
    head = jnp.stack([mine, col + cols * mine, row % 4 * BASE])
    info = jnp.concatenate([head, kinds.reshape(-1), jnp.where((row < 2) & (col < 2), row * 2 + col, 1)[None], sources]).astype(jnp.int32)

    def geometry(left, right, held):
        return [
            pl.BlockSpec((held, QUAD, TILE, FEAT), lambda *at: (left(*at), 0, 0, 0)),
            pl.BlockSpec((2, QUAD, FEAT, TILE), lambda *at: (right, 0, 0, 0)),
            pl.BlockSpec((held, TILE, 128), lambda *at: (left(*at), 0, 0)),
            pl.BlockSpec((2, 8, TILE), lambda *at: (right, 0, 0)),
        ]

    factor, weights_part = pl.pallas_call(
        chain_kernel,
        grid_spec=pltpu.PrefetchScalarGridSpec(
            num_scalar_prefetch=1,
            grid=(1,),
            in_specs=geometry(lambda *at: 0, 0, 2)
            + [
                pl.BlockSpec((1, QUAD, FEAT, TILE), lambda i, info: (6 + info[0], 0, 0, 0)),
                pl.BlockSpec((1, 8, TILE), lambda i, info: (6 + info[0], 0, 0)),
            ],
            out_specs=[
                pl.BlockSpec((TILE, TILE), lambda i, info: (0, 0)),
                pl.BlockSpec((LEAD, BASE), lambda i, info: (0, 0)),
            ],
            scratch_shapes=[
                pltpu.VMEM((LEAD + BASE, 2 * LEAD), F32),
                pltpu.VMEM((LEAD + BASE, BASE), F32),
                pltpu.VMEM((BASE, BASE), F32),
                pltpu.VMEM((STEP, STEP, BASE), F32),
                pltpu.VMEM((STEP, STEP, BASE), F32),
                pltpu.VMEM((STEP, BASE), F32),
                pltpu.VMEM((STEP, 8, BASE), F32),
                pltpu.VMEM((2 * BASE, WINDOW + BASE), BF16),
                pltpu.VMEM((LEAD, 2 * BASE), BF16),
            ],
        ),
        out_shape=[jax.ShapeDtypeStruct((TILE, TILE), F32), jax.ShapeDtypeStruct((LEAD, BASE), F32)],
        name="chain",
        compiler_params=pltpu.CompilerParams(vmem_limit_bytes=36 << 20),
    )(info, u, v, wr, wc, v, wc)

    tall = jax.ShapeDtypeStruct((4 * TILE, LEAD), BF16)
    chunks = TILE // CHUNK

    blocked = pl.BlockSpec((CHUNK, LEAD), lambda i, h, info: (i * chunks + h, 0))

    def assembled(kernel, right, shapes, tiles, name):
        return pl.pallas_call(
            kernel,
            grid_spec=pltpu.PrefetchScalarGridSpec(
                num_scalar_prefetch=1,
                grid=(4, chunks),
                in_specs=geometry(lambda i, h, info: 2 + i, right, 1),
                out_specs=[blocked] * len(shapes),
            ),
            out_shape=shapes,
            cost_estimate=pl.CostEstimate(
                flops=tiles * 7_500_000_000, bytes_accessed=tiles * 2_000_000, transcendentals=tiles * 4_000_000
            ),
            name=name,
            compiler_params=pltpu.CompilerParams(vmem_limit_bytes=20 << 20),
        )(info, u, v, wr, wc)

    near = [send(weights_part, lambda y, c, x, z, k=k: (y + k, c, x, z), rows, cols) for k in range(1, 4)]
    panels = assembled(panel_kernel, 0, [tall] * 2, 8, "panel")
    *near, ah, al = lax.optimization_barrier((*near, *panels))
    parts = [weights_part] + near
    parts = parts + [send(part, lambda y, c, x, z: (y, c + 1, x, z), rows, cols) for part in parts]
    own = assembled(own_kernel, 3, [jax.ShapeDtypeStruct((4 * TILE, LEAD), F32)], 6, "own")
    *parts, own = lax.optimization_barrier((*parts, *own))

    lines = ROWS * 8
    out = pl.pallas_call(
        final_kernel,
        grid_spec=pltpu.PrefetchScalarGridSpec(
            num_scalar_prefetch=1,
            grid=(4, TILE // ROWS),
            in_specs=whole(12),
            out_specs=pl.BlockSpec((lines, 128), lambda i, h, info: (i * (TILE // ROWS) + h, 0)),
            scratch_shapes=[pltpu.VMEM((2, LEAD, TILE), BF16)] * 2,
        ),
        out_shape=jax.ShapeDtypeStruct((4 * TILE * 8, 128), F32),
        name="final",
        compiler_params=pltpu.CompilerParams(vmem_limit_bytes=24 << 20),
    )(info, factor, *parts, ah, al, own)
    return out.reshape(4, 1, TILE, 2, 1, TILE)


def solution(mesh):
    return jax.shard_map(
        shards,
        mesh=mesh,
        in_specs=(P(None, None, ("row", "col")), P(None, ("row", "col")), P(("row", "col")), P()),
        out_specs=P(None, "row", None, None, "col", None),
        check_vma=False,
    )
```
